32 devices in a mesh: passage: 8 (over y, x, core), sub: 4 (over z).
Axes of the slice: x: 2, y: 2, z: 4, core: 2. Of those that a mesh axis runs over, the one named last changes fastest.
Arguments:
- block_vectors: float32 [32, 8192], P(None, ('passage', 'sub')), may hold values from -75 to 75
- stiffness: float32 [8192], P(('passage', 'sub')), may hold values from 2 to 8
- mass_diag: float32 [8192], P(('passage', 'sub')), may hold values from 0.5 to 2
- kblocks: float32 [64, 4, 128, 128], P(('passage', 'sub')), may hold values from -0.25 to 0.25
- block_cols: int32 [64, 4], P(('passage', 'sub')), may hold values from 0 to 5
- slot_node: int32 [32768], P(('passage', 'sub')), may hold values from 0 to 255
- slot_owner: int32 [32768, 1], P(('passage', 'sub')), may hold values from 0 to 3; in each aligned block of 1024 rows (0 to 1023, 1024 to 2047, ...) at most 512 rows name the same one
- slot_cell: int32 [32768], P(('passage', 'sub')), may hold values from 0 to 8191
- slot_weight: float32 [32768], P(('passage', 'sub')), may hold values from 0.5 to 4
- live_slots: int32 [32], P(('passage', 'sub')), may hold values from 768 to 1024, as said below
Outputs:
- residual: float32 [32, 8192], P(None, ('passage', 'sub'))
- gram_stiff: float32 [64, 64], replicated
- gram_plain: float32 [64, 64], replicated
The draws below stay inside these ranges and needn't reach their ends.
Inputs may be any that keep to these rules, and one draw needn't show every extreme that they name: `slot_owner`: per device at most 512 slots name the same owner, and some device reaches 512 for some owner. `live_slots`: some device has all 1024 slots live.
All inputs are finite; a program needn't handle non-finite values.
Results may differ from the reference program's by a relative error of at most 0.00019.
Values sent between devices are 32-bit elements; how exact they have to be, the bound alone decides.
No kernel may reach another device: no remote copies, remote signals or barrier semaphores. Data moves between devices by JAX's collectives and lax.ppermute only.
A program may use at most 64 MiB of HBM per device.

```python
import math
import jax
import jax.numpy as jnp
import numpy as np
from jax import lax

M = 32
BS = 128
NB = 4
RB = 2
NI = 1024
CX = 8
CY = 8
CZ = 128
NSD = 256
NSG = 8192
NI_ALL = 32768
CAP = 512
N_PASSAGE = 8
N_SUB = 4


def draw_block_vectors(key, part):
    key_base, key_scale = jax.random.split(key, 2)
    mode_scale = 0.5 * jnp.exp(jax.random.uniform(key_scale, (M, 1), jnp.float32, 0.0, math.log(10.0)))
    rising = jnp.exp(math.log(3.0) * jnp.arange(NSG, dtype=jnp.float32) / NSG)[None, :]
    base = jnp.clip(jax.random.normal(key_base, (M, NSG), jnp.float32), -5.0, 5.0)
    return (base * mode_scale * rising).astype(jnp.float32)


def draw_live_slots(key, part):
    devices_all = NSG // NSD
    key_counts, key_choice = jax.random.split(key)
    drawn_counts = jax.random.randint(key_counts, (devices_all,), 3 * NI // 4, NI + 1)
    chosen_one = jax.random.randint(key_choice, (), 0, devices_all)
    return jnp.where(jnp.arange(devices_all) == chosen_one, NI, drawn_counts).astype(jnp.int32)


def place_ends(values, own_key, low, top_value):
    extent = values.shape
    place = [jax.random.randint(jax.random.fold_in(own_key, axis), (), 0, extent[axis]) for axis in range(len(extent))]
    values = values.at[tuple(place)].set(low)
    longest = extent.index(max(extent))
    place[longest] = (place[longest] + 1) % extent[longest]
    return values.at[tuple(place)].set(top_value)


def block_scale(own_key, dims, cuts, smallest, high):
    def one(dim, shards_of):
        heights = jax.random.uniform(jax.random.fold_in(jax.random.fold_in(own_key, 6), dim), (shards_of,), jnp.float32, smallest / len(cuts), high / len(cuts))
        return jnp.repeat(jnp.exp(heights), dims[dim] // shards_of).reshape((-1,) + (1,) * (len(dims) - dim - 1))

    gain = one(*cuts[0])
    for cut in cuts[1:]:
        gain = gain * one(*cut)
    return gain


def assign_block(key, own, number, rows, count, top, limit, slope):
    sequence = jax.random.permutation(key, count)
    crowded, usual = portions_of(count, rows * top, limit, slope, True), portions_of(count, rows * top, limit, slope, False)
    places = jnp.arange(count)

    def named(lengths, rotation):
        used = int((lengths > 0).sum())
        fixed = max(1, used // 4)
        moved = fixed + (places - fixed + rotation * (used - fixed)) % max(1, count - fixed)
        return jnp.zeros((count,), jnp.int32).at[sequence[jnp.where(places < fixed, places, moved)]].set(jnp.asarray(lengths, jnp.int32))

    lengths = jnp.where(number % 4 == 0, named(crowded, number // 4), named(usual, number - number // 4 - 1))
    mixed = jax.random.permutation(jax.random.fold_in(own, 3), count)
    donor, taker = mixed[0:count // 2 * 2:2], mixed[1:count // 2 * 2:2]
    room = jnp.minimum(lengths[donor] - 1, limit - lengths[taker]) // 2
    room = jnp.where((donor == sequence[0]) | (taker == sequence[0]) | (lengths[taker] == 0), 0, jnp.maximum(room, 0))
    moved = jax.random.randint(jax.random.fold_in(own, 4), (count // 2,), 0, 1 << 20) % (room + 1)
    lengths = lengths.at[donor].add(-moved).at[taker].add(moved)
    items = jnp.searchsorted(jnp.cumsum(lengths), jnp.arange(rows * top), side="right").astype(jnp.int32)
    listing = items.reshape(top, rows).T
    listing = listing[jax.random.permutation(jax.random.fold_in(own, 1), rows)]
    rotation = jax.random.randint(jax.random.fold_in(own, 2), (rows, 1), 0, top)
    return jnp.take_along_axis(listing, (jnp.arange(top)[None, :] + rotation) % top, axis=1)


def portions_of(amount, total, limit, skew, full):
    weights = [(1 << 20) // math.isqrt(standing ** skew) + 1 for standing in range(1, amount + 1)]
    largest = limit if full else min(limit, max(-(-total // amount), total * weights[0] // sum(weights)))
    least = 1 if total - largest >= amount - 1 else 0
    holding, rest = [largest] + [least] * (amount - 1), total - largest - least * (amount - 1)
    while rest > 0:
        candidates = [i for i in range(1, amount) if holding[i] < largest] or [i for i in range(1, amount) if holding[i] < limit]
        mass, left = sum([weights[i] for i in candidates]), rest
        for i in candidates:
            more = min(limit - holding[i], max(1, left * weights[i] // mass), rest)
            holding[i] = holding[i] + more
            rest = rest - more
    return np.array(holding)


def centred(key, shape, deviation, most, cuts=(), kind=jnp.bfloat16):
    array = jax.random.normal(key, shape, jnp.float32) * deviation
    if len(cuts) > 0:
        array = block_scale(key, shape, cuts, -0.22, 0.18) * array
    return jnp.clip(array, min=-most, max=most).astype(kind)


def setup_inputs(seed: int = 0) -> dict:
    keys = jax.random.split(jax.random.key(seed), 11)
    block_vectors = draw_block_vectors(jax.random.fold_in(keys[10], 71), 0)
    stiffness = jnp.clip(jnp.exp(math.log(8.0) - 1.3862944 * jax.random.uniform(keys[1], (NSG,), jnp.float32) ** block_scale(keys[1], (NSG,), ((0, 32),), -0.2, 0.2)), 2.0, 8.0)
    mass_diag = jnp.clip(jnp.exp(math.log(2.0) - 1.3862944 * jax.random.uniform(keys[2], (NSG,), jnp.float32) ** block_scale(keys[2], (NSG,), ((0, 32),), -0.2, 0.2)), 0.5, 2.0)
    kblocks = centred(keys[3], (RB * N_PASSAGE * N_SUB, NB, BS, BS), (NB * BS) ** -0.5, 0.25, ((0, 32),), jnp.float32)
    block_cols = place_ends(jax.random.randint(keys[4], (RB * N_PASSAGE * N_SUB, NB), 0, 3 * RB), jax.random.fold_in(keys[4], 1), 0, (3 * RB) - 1).astype(jnp.int32)
    slot_node = place_ends(jax.random.randint(keys[5], (NI_ALL,), 0, NSD), jax.random.fold_in(keys[5], 1), 0, NSD - 1).astype(jnp.int32)
    slot_owner_keys = jax.random.split(jax.random.fold_in(keys[6], 1), NI_ALL // NI)
    slot_owner_turns = jax.random.permutation(jax.random.fold_in(keys[6], 3), NI_ALL // NI)
    slot_owner = jax.vmap(lambda own, number: assign_block(jax.random.fold_in(keys[6], 2), own, number, NI, N_SUB, 1, CAP, 2))(slot_owner_keys, slot_owner_turns).reshape((NI_ALL, 1))
    slot_cell = place_ends(jax.random.randint(keys[7], (NI_ALL,), 0, CX * CY * CZ), jax.random.fold_in(keys[7], 1), 0, (CX * CY * CZ) - 1).astype(jnp.int32)
    slot_weight = jnp.clip(jnp.exp(math.log(4.0) - 2.0794415 * jax.random.uniform(keys[8], (NI_ALL,), jnp.float32) ** block_scale(keys[8], (NI_ALL,), ((0, 32),), -0.2, 0.2)), 0.5, 4.0)
    live_slots = draw_live_slots(jax.random.fold_in(keys[10], 71), 0)
    return {"block_vectors": block_vectors, "stiffness": stiffness, "mass_diag": mass_diag, "kblocks": kblocks, "block_cols": block_cols, "slot_node": slot_node, "slot_owner": slot_owner, "slot_cell": slot_cell, "slot_weight": slot_weight, "live_slots": live_slots}


center_weight = 15.0
lower_bound = 1.0 / 15.0
upper_bound = 17.0 / 15.0
middle = (upper_bound + lower_bound) / 2.0
radius = (upper_bound - lower_bound) / 2.0
sigma_ratio = middle / radius
first_rho = 1.0 / sigma_ratio
second_rho = 1.0 / (2.0 * sigma_ratio - first_rho)
third_rho = 1.0 / (2.0 * sigma_ratio - second_rho)


def laplace_inner(padded):
    rows_one = padded.shape[1] - 2
    rows_two = padded.shape[2] - 2
    depth = padded.shape[3]
    zpadded = jnp.pad(padded, ((0, 0), (0, 0), (0, 0), (1, 1)))
    neighbours = jnp.zeros((padded.shape[0], rows_one, rows_two, depth), jnp.float32)
    for offset_one in range(3):
        for offset_two in range(3):
            for offset_three in range(3):
                distance = abs(offset_one - 1) + abs(offset_two - 1) + abs(offset_three - 1)
                if distance == 0:
                    continue
                weight = 0.5 ** (distance - 1)
                neighbours = neighbours + weight * zpadded[:, offset_one:offset_one + rows_one, offset_two:offset_two + rows_two, offset_three:offset_three + depth]
    return center_weight * padded[:, 1:-1, 1:-1, :] - neighbours


def extend_field(field):
    looped = jnp.concatenate([field[-1:], field, field[:1]], axis=0)
    return jnp.pad(looped, ((0, 0), (1, 1), (0, 0)))[None]


def chebyshev(source):
    first = source / (center_weight * middle)
    resid = source - laplace_inner(extend_field(first))[0]
    second_step = second_rho * first_rho * first + (2.0 * second_rho / radius) * (resid / center_weight)
    second = first + second_step
    resid = source - laplace_inner(extend_field(second))[0]
    third_step = third_rho * second_rho * second_step + (2.0 * third_rho / radius) * (resid / center_weight)
    return second + third_step


def apply_stiffness(field, block_cols, kblocks, stiffness):
    width = field.shape[0]
    total_blocks = block_cols.shape[0]
    blocks = field.reshape(width, total_blocks, BS)
    row_ids = jnp.arange(total_blocks, dtype=jnp.int32)[:, None]
    device = row_ids // RB
    sub_pos = device % N_SUB
    offset = block_cols // RB - 1
    valid = (sub_pos + offset >= 0) & (sub_pos + offset < N_SUB)
    source = jnp.where(valid, device * RB + block_cols - RB, 0).astype(jnp.int32)
    window = blocks[:, source] * valid[None, :, :, None].astype(jnp.float32)
    mixed = jnp.einsum("mrnb,rnbk->mrk", window, kblocks, precision=lax.Precision.HIGHEST)
    return stiffness[None, :] * field + mixed.reshape(width, -1)


def inner(left, right):
    return lax.dot_general(left, right, (((1,), (1,)), ((), ())), precision=lax.Precision.HIGHEST, preferred_element_type=jnp.float32)


def reference(block_vectors, stiffness, mass_diag, kblocks, block_cols, slot_node, slot_owner, slot_cell, slot_weight, live_slots):
    total = block_vectors.shape[1]
    slot_ids = jnp.arange(slot_node.shape[0], dtype=jnp.int32)
    device = slot_ids // NI
    passage = device // N_SUB
    live = (slot_ids % NI < live_slots[device]).astype(jnp.float32)
    scaled = slot_weight * live
    column = (device * (RB * BS) + slot_node).astype(jnp.int32)
    cell_one = slot_cell // (CY * CZ)
    cell_two = (slot_cell // CZ) % CY
    cell_three = slot_cell % CZ
    flat = (((passage * CX + cell_one) * (CY * N_SUB) + slot_owner[:, 0] * CY + cell_two) * CZ + cell_three).astype(jnp.int32)
    cells_all = CX * N_PASSAGE * CY * N_SUB * CZ

    def added_force(mode_row):
        source = jnp.zeros((cells_all,), jnp.float32).at[flat].add(mode_row[column] * scaled)
        press = chebyshev(source.reshape(CX * N_PASSAGE, CY * N_SUB, CZ)).reshape(-1)
        return jnp.zeros((total,), jnp.float32).at[column].add(press[flat] * scaled)

    stiff_image = apply_stiffness(block_vectors, block_cols, kblocks, stiffness)
    mass_image = mass_diag[None, :] * block_vectors + lax.map(added_force, block_vectors)
    theta = jnp.sum(block_vectors * stiff_image, axis=1) / jnp.sum(block_vectors * mass_image, axis=1)
    residual = stiff_image - theta[:, None] * mass_image
    stiff_resid = apply_stiffness(residual, block_cols, kblocks, stiffness)
    search = jnp.concatenate([block_vectors, residual], axis=0)
    image = jnp.concatenate([stiff_image, stiff_resid], axis=0)
    gram_stiff = inner(search, image) / total
    gram_plain = inner(search, search) / total
    return residual, gram_stiff, gram_plain
```

```python
import functools
import jax
import jax.numpy as jnp
from jax import lax
from jax.experimental import pallas as pl
from jax.experimental.pallas import tpu as pltpu
from jax.sharding import PartitionSpec as P

CX = 8
CY = 8
CZ = 128
HALO = 2

center_weight = 15.0
lower_bound = 1.0 / 15.0
upper_bound = 17.0 / 15.0
middle = (upper_bound + lower_bound) / 2.0
radius = (upper_bound - lower_bound) / 2.0
sigma_ratio = middle / radius
first_rho = 1.0 / sigma_ratio
second_rho = 1.0 / (2.0 * sigma_ratio - first_rho)
third_rho = 1.0 / (2.0 * sigma_ratio - second_rho)

FIRST = 1.0 / (center_weight * middle)
GAIN2 = 2.0 * second_rho / (radius * center_weight)
SEC_U = FIRST * (1.0 + second_rho * first_rho) + GAIN2 * (1.0 - 17.0 * FIRST)
SEC_T = GAIN2 * 2.0 * FIRST
STEP3 = third_rho * second_rho
GAIN3 = 2.0 * third_rho / (radius * center_weight)
PRE_SRC = GAIN3 - STEP3 * FIRST
PRE_SEC = 1.0 + STEP3 - 17.0 * GAIN3
PRE_T = 2.0 * GAIN3

BF = jnp.bfloat16
F32 = jnp.float32
NB1 = (CY + 2 * HALO) // 2
CELLS = CX * CY * CZ


def log2(n):
    return n.bit_length() - 1


def split(x):
    hi = x.astype(BF)
    return hi, (x - hi.astype(F32)).astype(BF)


def decode(row):
    flat = row.astype(jnp.int32)
    a = lax.shift_right_logical(flat, log2(CY * CZ)) & (CX - 1)
    owner = lax.shift_right_logical(flat, log2(CELLS))
    b = lax.shift_right_logical(flat, log2(CZ)) & (CY - 1)
    return a, owner, b, flat & (CZ - 1)


def lanes_from(x, index):
    index = jnp.broadcast_to(index, x.shape)
    return jnp.take_along_axis(x, index, axis=1, mode="promise_in_bounds")


def onehot(values, height):
    shape = (height, values.shape[1])
    rows = lax.broadcasted_iota(jnp.int32, shape, 0)
    return jnp.where(rows == values, 1.0, 0.0).astype(BF)


def add_source(blk, sub, a_first, a_count, out, lhs, rhs, modes, slots, fresh):
    local = blk.shape[1]
    top = modes + 1
    count = slots // local
    for j in range(count):
        a, owner, b, c = decode(blk[top + j : top + j + 1, :])
        node = blk[top + count + j : top + count + j + 1, :].astype(jnp.int32)
        weight = blk[top + 2 * count + j : top + 2 * count + j + 1, :]
        bext = owner * CY + b - (sub * CY - HALO)
        aloc = a - a_first
        valid = (bext >= 0) & (bext < CY + 2 * HALO) & (aloc >= 0) & (aloc < a_count)
        pair = jnp.where(valid, aloc * NB1 + lax.shift_right_arithmetic(bext, 1), -1)
        place = (bext & 1) * CZ + c
        pieces = []
        for h in range(local // 128):
            idx = node[:, h * 128 : (h + 1) * 128]
            got = jnp.zeros((modes, 128), F32)
            for g in range(local // 128):
                part = lanes_from(blk[0:modes, g * 128 : (g + 1) * 128], idx & 127)
                got = jnp.where(lax.shift_right_logical(idx, 7) == g, part, got)
            pieces.append(got)
        vals = jnp.concatenate(pieces, axis=1) * weight
        hi, lo = split(vals)
        wide = jnp.broadcast_to(pair.astype(F32), (modes, local)).astype(BF)
        zero = jnp.zeros((modes, local), BF)
        at = 2 * j * local
        for r in range(a_count * NB1):
            mask = wide == jnp.asarray(r, BF)
            lhs[r * modes : (r + 1) * modes, at : at + local] = jnp.where(mask, hi, zero)
            lhs[r * modes : (r + 1) * modes, at + local : at + 2 * local] = jnp.where(mask, lo, zero)
        hot = onehot(place, 2 * CZ)
        rhs[:, at : at + local] = hot
        rhs[:, at + local : at + 2 * local] = hot
    total = a_count * NB1 * modes
    step = min(total, 384)

    def rows(i, carry):
        at = pl.ds(pl.multiple_of(i * step, step), step)
        got = lax.dot_general(
            lhs[at, :], rhs[...], (((1,), (1,)), ((), ())), preferred_element_type=F32
        )
        if fresh:
            out[at, :] = got
        else:
            out[at, :] = out[at, :] + got
        return carry

    lax.fori_loop(0, total // step, rows, 0)


def own_source_kernel(slots, modes, count, sub_ref, *refs):
    blks, out, lhs, rhs = refs[:count], refs[count], refs[count + 1], refs[count + 2]
    for k in range(count):
        add_source(blks[k], sub_ref[0], 0, CX, out, lhs, rhs, modes, slots, k == 0)


def t_b(plane_e, plane_o, modes, low, high):
    e, o = plane_e, plane_o
    return e, o


def shift_sum(x):
    lane = lax.broadcasted_iota(jnp.int32, x.shape, 1)
    left = jnp.where(lane == 0, 0.0, pltpu.roll(x, 1, 1))
    right = jnp.where(lane == CZ - 1, 0.0, pltpu.roll(x, CZ - 1, 1))
    return x + 0.5 * (left + right)


def fluid_kernel(slots, modes, count, groups, sub_ref, *refs):
    own = refs[:count]
    low, high, src_own, out, edge, second, press, lhs, rhs, force = refs[count:]
    sub = sub_ref[0]
    local = own[0].shape[1]
    top = modes + 1
    per = slots // local
    plane = NB1 * modes
    for k in range(count):
        add_source(low.at[k], sub, CX - HALO, HALO, edge.at[0], lhs, rhs, modes, slots, k == 0)
        add_source(high.at[k], sub, 0, HALO, edge.at[1], lhs, rhs, modes, slots, k == 0)

    def src(a, b):
        rows = slice((b // 2) * modes, (b // 2 + 1) * modes)
        lanes = slice((b % 2) * CZ, (b % 2 + 1) * CZ)
        if a < HALO:
            return edge[0, a * plane + rows.start : a * plane + rows.stop, lanes]
        if a >= CX + HALO:
            at = (a - CX - HALO) * plane
            return edge[1, at + rows.start : at + rows.stop, lanes]
        at = (a - HALO) * plane
        return src_own[at + rows.start : at + rows.stop, lanes]

    for a in range(1, CX + 2 * HALO - 1):
        cols = [
            src(a, b) + 0.5 * (src(a - 1, b) + src(a + 1, b)) for b in range(CY + 2 * HALO)
        ]
        for b in range(1, CY + 2 * HALO - 1):
            t = shift_sum(cols[b] + 0.5 * (cols[b - 1] + cols[b + 1]))
            sec = SEC_U * src(a, b) + SEC_T * t
            if b < HALO:
                sec = sec * jnp.where(sub == 0, 0.0, 1.0)
            if b >= CY + HALO:
                sec = sec * jnp.where(sub == groups - 1, 0.0, 1.0)
            second[a - 1, b - 1] = sec
    for a in range(CX):
        cols = [
            second[a + 1, b] + 0.5 * (second[a, b] + second[a + 2, b]) for b in range(CY + 2)
        ]
        for b in range(CY):
            t = shift_sum(cols[b + 1] + 0.5 * (cols[b] + cols[b + 2]))
            press[a * CY + b] = (
                PRE_SRC * src(a + HALO, b + HALO) + PRE_SEC * second[a + 1, b + 1] + PRE_T * t
            )
    for k in range(count):
        total = jnp.zeros((2 * modes, local), F32)
        for j in range(per):
            a, owner, b, c = decode(own[k][top + j : top + j + 1, :])
            node = own[k][top + per + j : top + per + j + 1, :].astype(jnp.int32)
            weight = own[k][top + 2 * per + j : top + 2 * per + j + 1, :]
            row = jnp.where(owner == sub, a * CY + b, -1)
            halves = local // 128
            idx = [
                jnp.broadcast_to(c[:, h * 128 : (h + 1) * 128], (modes, 128)) for h in range(halves)
            ]
            row_w = [
                jnp.broadcast_to(row[:, h * 128 : (h + 1) * 128], (modes, 128))
                for h in range(halves)
            ]

            def pick(i, accs):
                accs = list(accs)
                for u in range(4):
                    r = i * 4 + u
                    cell = press[r]
                    for h in range(halves):
                        got = jnp.take_along_axis(cell, idx[h], axis=1, mode="promise_in_bounds")
                        accs[h] = jnp.where(row_w[h] == r, got, accs[h])
                return tuple(accs)

            accs = lax.fori_loop(
                0, CX * CY // 4, pick, tuple(jnp.zeros((modes, 128), F32) for _ in range(halves))
            )
            picked = jnp.concatenate(accs, axis=1) * weight
            hi, lo = split(picked)
            hot = onehot(node, local)
            total = total + lax.dot_general(
                jnp.concatenate([hi, lo], axis=0),
                hot,
                (((1,), (1,)), ((), ())),
                preferred_element_type=F32,
            )
        force[k] = total[:modes] + total[modes:]
    for k in range(count):
        for w in range(3):
            out[k, w] = force[(1 - k - w) % count]


def apply_blocks(window, cols_ref, kb_ref, sub, groups, diag, field):
    rb, nb, bs, _ = kb_ref.shape
    pieces = []
    for q in range(rb):
        acc = None
        for n in range(nb):
            j = cols_ref[q, n]
            where = sub + j // rb - 1
            inside = jnp.where((where >= 0) & (where < groups), 1.0, 0.0)
            part = lax.dot_general(
                window[j] * inside,
                kb_ref[q, n],
                (((1,), (0,)), ((), ())),
                precision=lax.Precision.HIGHEST,
                preferred_element_type=F32,
            )
            acc = part if acc is None else acc + part
        pieces.append(acc)
    return diag * field + jnp.concatenate(pieces, axis=1)


def fill_window(win, blocks, bs):
    at = 0
    for blk in blocks:
        for i in range(blk.shape[1] // bs):
            win[at] = blk[:, i * bs : (i + 1) * bs]
            at += 1


def stiff_kernel(modes, groups, sub_ref, cols_ref, prev, own, nxt, diag, kb, out, win):
    bs = kb.shape[2]
    fill_window(win, [prev[0:modes, :], own[0:modes, :], nxt[0:modes, :]], bs)
    out[...] = apply_blocks(win, cols_ref, kb, sub_ref[0], groups, diag[...], own[0:modes, :])


def gram_kernel(modes, groups, count, sub_ref, cols_ref, *refs):
    packs, parts = refs[:3], refs[3 : 3 + count]
    stiff, kstiff, diag, kb, gram, mass, win = refs[3 + count :]
    bs = kb.shape[2]
    fields = []
    for w in range(3):
        blk = packs[w]
        m = blk[modes : modes + 1, :] * blk[0:modes, :]
        for part in parts:
            m = m + part[w]
        fields.append(m)
    fill_window(win, fields, bs)
    own = fields[1]
    mass[...] = own
    km = apply_blocks(win, cols_ref, kb, sub_ref[0], groups, diag[...], own)
    v = packs[1][0:modes, :]
    s = stiff[...]
    left = jnp.concatenate([v, s, own], axis=0)
    right = jnp.concatenate([s, kstiff[...], km, own], axis=0)

    def inner(x, y):
        return lax.dot_general(
            x,
            y,
            (((1,), (1,)), ((), ())),
            precision=lax.Precision.HIGHEST,
            preferred_element_type=F32,
        )

    gram[...] = inner(left, right)
    gram[2 * modes : 3 * modes, 0:modes] = inner(v, v)


def final_kernel(modes, total, gram, stiff, mass, residual, g_stiff, g_plain):
    m = modes
    blocks = [
        [gram[i * m : (i + 1) * m, j * m : (j + 1) * m] for j in range(4)] for i in range(3)
    ]
    (vs, vks, vkm, vm), (ss, sks, skm, sm), (vv, mks, mkm, mm) = blocks
    rows = lax.broadcasted_iota(jnp.int32, (m, m), 0)
    lanes = lax.broadcasted_iota(jnp.int32, (m, m), 1)
    eye = rows == lanes

    def column(x):
        return jnp.sum(jnp.where(eye, x, 0.0), axis=1, keepdims=True)

    def line(x):
        return jnp.sum(jnp.where(eye, x, 0.0), axis=0, keepdims=True)

    tc = column(vs) / column(vm)
    tl = line(vs) / line(vm)
    residual[...] = stiff[...] - tc * mass[...]
    ms = sm.T
    scale = 1.0 / total
    vr = vs - vm * tl
    g_plain[0:m, 0:m] = vv * scale
    g_plain[0:m, m : 2 * m] = vr * scale
    g_plain[m : 2 * m, 0:m] = vr.T * scale
    g_plain[m : 2 * m, m : 2 * m] = (ss - sm * tl - tc * (ms - mm * tl)) * scale
    g_stiff[0:m, 0:m] = vs * scale
    g_stiff[0:m, m : 2 * m] = (vks - vkm * tl) * scale
    g_stiff[m : 2 * m, 0:m] = (ss - tc * ms) * scale
    g_stiff[m : 2 * m, m : 2 * m] = (sks - skm * tl - tc * (mks - mkm * tl)) * scale


def shifted(x, axis, k):
    n = lax.axis_size(axis)
    return lax.ppermute(x, axis, [(i, (i + k) % n) for i in range(n)])


def swapped(x, axis, k):
    n = lax.axis_size(axis)
    return lax.ppermute(x, axis, [(i, i ^ k) for i in range(n)])


def summed(x, axis, bit):
    n = lax.axis_size(axis)
    while (1 << bit) < n:
        if (4 << bit) <= n:
            one, two, three = [swapped(x, axis, k << bit) for k in (1, 2, 3)]
            x = (x + one) + (two + three)
            bit += 2
        else:
            x = x + swapped(x, axis, 1 << bit)
            bit += 1
    return x


def smem():
    return pl.BlockSpec(memory_space=pltpu.SMEM)


def vmem():
    return pl.BlockSpec(memory_space=pltpu.VMEM)


def call(kernel, name, out_shape, scalars, arrays, scratch, flops):
    return pl.pallas_call(
        kernel,
        name=name,
        out_shape=out_shape,
        in_specs=[smem()] * len(scalars) + [vmem()] * len(arrays),
        out_specs=jax.tree.map(lambda _: vmem(), out_shape),
        scratch_shapes=scratch,
        cost_estimate=pl.CostEstimate(flops=flops, transcendentals=0, bytes_accessed=1 << 20),
    )(*scalars, *arrays)


def body(
    block_vectors,
    stiffness,
    mass_diag,
    kblocks,
    block_cols,
    slot_node,
    slot_owner,
    slot_cell,
    slot_weight,
    live_slots,
):
    modes, local = block_vectors.shape
    groups = lax.axis_size("sub")
    slots = slot_node.shape[0]
    per = slots // local
    bs = kblocks.shape[2]
    total = local * lax.axis_size("passage") * groups
    sub = lax.axis_index("sub").astype(jnp.int32).reshape(1)
    live = jnp.arange(slots, dtype=jnp.int32) < live_slots[0]
    weight = jnp.where(live, slot_weight, 0.0)
    flat = (slot_owner[:, 0] * CELLS + slot_cell).astype(F32)
    pieces = [
        block_vectors,
        mass_diag[None, :],
        flat.reshape(per, local),
        slot_node.astype(F32).reshape(per, local),
        weight.reshape(per, local),
    ]
    height = modes + 1 + 3 * per
    padded = -(-height // 8) * 8
    pieces.append(jnp.zeros((padded - height, local), F32))
    pack = jnp.concatenate(pieces, axis=0)
    packs = [pack] + [shifted(pack, "sub", k) for k in range(1, groups)]
    both = jnp.stack(packs)
    low = shifted(both, "passage", 1)
    high = shifted(both, "passage", -1)
    diag = stiffness[None, :]
    window = [packs[1], packs[0], packs[groups - 1]]
    nwin = 3 * local // bs
    stiff = call(
        functools.partial(stiff_kernel, modes, groups),
        "stiff",
        jax.ShapeDtypeStruct((modes, local), F32),
        [sub, block_cols],
        [*window, diag, kblocks],
        [pltpu.VMEM((nwin, modes, bs), F32)],
        1 << 29,
    )
    stiff_prev = shifted(stiff, "sub", 1)
    stiff_next = shifted(stiff, "sub", -1)
    kstiff = call(
        functools.partial(stiff_kernel, modes, groups),
        "stiff_image",
        jax.ShapeDtypeStruct((modes, local), F32),
        [sub, block_cols],
        [stiff_prev, stiff, stiff_next, diag, kblocks],
        [pltpu.VMEM((nwin, modes, bs), F32)],
        1 << 29,
    )
    own_rows = CX * NB1 * modes
    source = call(
        functools.partial(own_source_kernel, slots, modes, groups),
        "own_source",
        jax.ShapeDtypeStruct((own_rows, 2 * CZ), F32),
        [sub],
        packs,
        [pltpu.VMEM((own_rows, 2 * slots), BF), pltpu.VMEM((2 * CZ, 2 * slots), BF)],
        1 << 33,
    )
    edge_rows = HALO * NB1 * modes
    force = call(
        functools.partial(fluid_kernel, slots, modes, groups, groups),
        "fluid",
        jax.ShapeDtypeStruct((groups, 3, modes, local), F32),
        [sub],
        [*packs, low, high, source],
        [
            pltpu.VMEM((2, edge_rows, 2 * CZ), F32),
            pltpu.VMEM((CX + 2, CY + 2, modes, CZ), F32),
            pltpu.VMEM((CX * CY, modes, CZ), F32),
            pltpu.VMEM((edge_rows, 2 * slots), BF),
            pltpu.VMEM((2 * CZ, 2 * slots), BF),
            pltpu.VMEM((groups, modes, local), F32),
        ],
        1 << 33,
    )
    parts = [force[0]] + [shifted(force[k], "sub", k) for k in range(1, groups)]
    gram, mass = call(
        functools.partial(gram_kernel, modes, groups, groups),
        "gram",
        (
            jax.ShapeDtypeStruct((3 * modes, 4 * modes), F32),
            jax.ShapeDtypeStruct((modes, local), F32),
        ),
        [sub, block_cols],
        [*window, *parts, stiff, kstiff, diag, kblocks],
        [pltpu.VMEM((nwin, modes, bs), F32)],
        1 << 29,
    )
    gram = gram + swapped(gram, "passage", 1)
    gram = summed(gram, "passage", 1)
    gram = summed(gram, "sub", 0)
    return call(
        functools.partial(final_kernel, modes, float(total)),
        "final",
        (
            jax.ShapeDtypeStruct((modes, local), F32),
            jax.ShapeDtypeStruct((2 * modes, 2 * modes), F32),
            jax.ShapeDtypeStruct((2 * modes, 2 * modes), F32),
        ),
        [],
        [gram, stiff, mass],
        [],
        1 << 20,
    )


def solution(mesh):
    return jax.shard_map(
        body,
        mesh=mesh,
        in_specs=(
            P(None, ("passage", "sub")),
            P(("passage", "sub")),
            P(("passage", "sub")),
            P(("passage", "sub"), None, None, None),
            P(("passage", "sub"), None),
            P(("passage", "sub")),
            P(("passage", "sub"), None),
            P(("passage", "sub")),
            P(("passage", "sub")),
            P(("passage", "sub")),
        ),
        out_specs=(P(None, ("passage", "sub")), P(), P()),
        check_vma=False,
    )
```

```python
import functools
import jax
import jax.numpy as jnp
from jax import lax
from jax.experimental import pallas as pl
from jax.experimental.pallas import tpu as pltpu
from jax.sharding import PartitionSpec as P

CX = 8
CY = 8
CZ = 128
HALO = 2

center_weight = 15.0
lower_bound = 1.0 / 15.0
upper_bound = 17.0 / 15.0
middle = (upper_bound + lower_bound) / 2.0
radius = (upper_bound - lower_bound) / 2.0
sigma_ratio = middle / radius
first_rho = 1.0 / sigma_ratio
second_rho = 1.0 / (2.0 * sigma_ratio - first_rho)
third_rho = 1.0 / (2.0 * sigma_ratio - second_rho)

FIRST = 1.0 / (center_weight * middle)
GAIN2 = 2.0 * second_rho / (radius * center_weight)
SEC_U = FIRST * (1.0 + second_rho * first_rho) + GAIN2 * (1.0 - 17.0 * FIRST)
SEC_T = GAIN2 * 2.0 * FIRST
STEP3 = third_rho * second_rho
GAIN3 = 2.0 * third_rho / (radius * center_weight)
PRE_SRC = GAIN3 - STEP3 * FIRST
PRE_SEC = 1.0 + STEP3 - 17.0 * GAIN3
PRE_T = 2.0 * GAIN3

BF = jnp.bfloat16
F32 = jnp.float32
CELLS = CX * CY * CZ


def log2(n):
    return n.bit_length() - 1


def split(x):
    hi = x.astype(BF)
    return hi, (x - hi.astype(F32)).astype(BF)


def lanes_from(x, index):
    return jnp.take_along_axis(
        x, jnp.broadcast_to(index, x.shape), axis=1, mode="promise_in_bounds"
    )


def onehot(values, height):
    shape = (height, values.shape[1])
    rows = lax.broadcasted_iota(jnp.int32, shape, 0)
    return jnp.where(rows == values, 1.0, 0.0).astype(BF)


def dot_t(x, y):
    return lax.dot_general(x, y, (((1,), (1,)), ((), ())), preferred_element_type=F32)


def dot(x, y):
    return lax.dot_general(x, y, (((1,), (0,)), ((), ())), preferred_element_type=F32)


def pack_kernel(modes, groups, live_ref, v_ref, owner_ref, cell_ref, node_ref, weight_ref, out):
    deep, wide = owner_ref.shape
    capacity = 2 * deep * wide // groups
    keys = groups * CX
    owner, cell, weight = owner_ref[...], cell_ref[...], weight_ref[...]
    shape = (deep, wide)
    place = lax.broadcasted_iota(jnp.int32, shape, 0) * wide + lax.broadcasted_iota(
        jnp.int32, shape, 1
    )
    live = place < live_ref[0]
    a = lax.shift_right_logical(cell, log2(CY * CZ))
    key = jnp.where(live, owner * CX + ((a + HALO) & (CX - 1)), -1)
    hots = jnp.concatenate([jnp.where(key == k, 1.0, 0.0) for k in range(keys)], axis=0).astype(BF)
    rows = lax.broadcasted_iota(jnp.int32, (wide, wide), 0)
    lanes = lax.broadcasted_iota(jnp.int32, (wide, wide), 1)
    within = dot(hots, jnp.where(rows <= lanes, 1.0, 0.0).astype(BF))
    size = keys * deep
    rows = lax.broadcasted_iota(jnp.int32, (size, size), 0)
    lanes = lax.broadcasted_iota(jnp.int32, (size, size), 1)
    shift = log2(CX * deep)
    same = lax.shift_right_logical(rows, shift) == lax.shift_right_logical(lanes, shift)
    earlier = jnp.where(same & (lanes < rows), 1.0, 0.0).astype(BF)
    ahead = dot(dot(earlier, hots).astype(BF), jnp.ones((wide, wide), BF))
    order = within + ahead - 1.0
    pos = jnp.zeros(shape, F32)
    for k in range(keys):
        pos = jnp.where(key == k, order[k * deep : (k + 1) * deep], pos)
    target = owner * capacity + pos.astype(jnp.int32)
    line = lax.shift_right_logical(target, log2(wide))
    half = deep
    line = jnp.where(live, lax.shift_right_logical(line, 1) + (line & 1) * half, -1)
    lane = target & (wide - 1)
    w1 = weight.astype(BF).astype(F32)
    w2 = (weight - w1).astype(BF).astype(F32)
    values = [
        lax.shift_right_logical(cell, 8).astype(F32),
        (cell & 255).astype(F32),
        node_ref[...].astype(F32),
        w1,
        w2,
        weight - w1 - w2,
    ]
    lefts, rights = [], []
    for r in range(deep):
        into = lax.broadcasted_iota(jnp.int32, (2 * half, wide), 0) == line[r : r + 1]
        lefts.append(
            jnp.concatenate([jnp.where(into, v[r : r + 1], 0.0) for v in values], axis=0).astype(BF)
        )
        rights.append(onehot(lane[r : r + 1], wide))
    listed = dot_t(jnp.concatenate(lefts, axis=1), jnp.concatenate(rights, axis=1))
    part = [listed[i * 2 * half : (i + 1) * 2 * half] for i in range(6)]
    lists = [256.0 * part[0] + part[1], part[2], part[3] + part[4] + part[5]]
    out[0:modes, :] = v_ref[...]
    for i, x in enumerate(lists):
        at = modes + i * half
        out[at : at + half, 0:wide] = x[:half]
        out[at : at + half, wide : 2 * wide] = x[half:]


class Lists:
    def __init__(self, blk, modes, capacity):
        self.blk, self.modes = blk, modes
        self.local = blk.shape[1]
        self.lines = (blk.shape[0] - modes) // 3
        self.width = min(self.local, capacity)
        self.capacity = capacity
        self.chunks = capacity // self.width

    def row(self, kind, owner, chunk):
        at = owner * self.capacity + chunk * self.width
        line = lax.shift_right_logical(at, log2(self.local))
        x = self.blk[pl.ds(self.modes + kind * self.lines + line, 1), :]
        if self.width < self.local:
            group = lax.shift_right_logical(at, log2(self.width)) & (self.local // self.width - 1)
            got = x[:, : self.width]
            for g in range(1, self.local // self.width):
                got = jnp.where(group == g, x[:, g * self.width : (g + 1) * self.width], got)
            x = got
        return x

    def load(self, owner, chunk):
        cell = self.row(0, owner, chunk).astype(jnp.int32)
        node = self.row(1, owner, chunk).astype(jnp.int32)
        weight = self.row(2, owner, chunk)
        a = lax.shift_right_logical(cell, log2(CY * CZ))
        b = lax.shift_right_logical(cell, log2(CZ)) & (CY - 1)
        return a, b, cell & (CZ - 1), node, weight


def fill(lists, owner, chunk, a_first, a_count, b_first, b_count, inside, lhs, rhs, at, side):
    modes, width = lists.modes, lists.width
    a, b, c, node, weight = lists.load(owner, chunk)
    if inside is not None:
        weight = weight * inside
    aloc, bloc = a - a_first, b - b_first
    valid = (aloc >= 0) & (aloc < a_count) & (bloc >= 0) & (bloc < 2 * b_count)
    pair = jnp.where(valid, aloc * b_count + lax.shift_right_arithmetic(bloc, 1), -1)
    place = (b & 1) * CZ + c
    pieces = []
    for h in range(width // 128):
        idx = node[:, h * 128 : (h + 1) * 128]
        got = None
        for g in range(lists.local // 128):
            part = lanes_from(lists.blk[0:modes, g * 128 : (g + 1) * 128], idx & 127)
            got = part if g == 0 else jnp.where(lax.shift_right_logical(idx, 7) == g, part, got)
        pieces.append(got)
    hi, lo = split(jnp.concatenate(pieces, axis=1) * weight)
    wide = jnp.broadcast_to(pair.astype(F32), (modes, width)).astype(BF)
    zero = jnp.zeros((modes, width), BF)
    for r in range(a_count * b_count):
        mask = wide == jnp.asarray(r, BF)
        lhs[r * modes : (r + 1) * modes, at : at + width] = jnp.where(mask, hi, zero)
        lhs[r * modes : (r + 1) * modes, at + width : at + 2 * width] = jnp.where(mask, lo, zero)
    hot = onehot(place, 2 * CZ)
    rhs[:, at : at + width] = hot
    rhs[:, at + width : at + 2 * width] = hot


def scatter(blks, modes, capacity, owner, inside, a_first, a_count, b_first, b_count, out, lhs, rhs):
    every = [Lists(blk, modes, capacity) for blk in blks]
    width = every[0].width
    rows = a_count * b_count * modes
    spec = (a_first, a_count, b_first, b_count, inside)
    left = lhs.at[0:rows, :]
    for k, lists in enumerate(every):
        fill(lists, owner, 0, *spec, left, rhs, 2 * k * width, None)
    deep = 2 * width * len(every)
    out[...] = dot_t(lhs[0:rows, 0:deep], rhs[:, 0:deep])
    for lists in every:
        for chunk in range(1, lists.chunks):
            a, b, c, node, weight = lists.load(owner, chunk)
            needed = jnp.where((a >= a_first) & (a < a_first + a_count), weight, 0.0)

            @pl.when(jnp.max(needed) > 0.0)
            def _():
                fill(lists, owner, chunk, *spec, left, rhs, 0, None)
                out[...] += dot_t(lhs[0:rows, 0 : 2 * width], rhs[:, 0 : 2 * width])


def around(sub, groups):
    below = jnp.maximum(sub - 1, 0), jnp.where(sub > 0, 1.0, 0.0)
    above = jnp.minimum(sub + 1, groups - 1), jnp.where(sub < groups - 1, 1.0, 0.0)
    return below, above


def own_source_kernel(modes, groups, capacity, sub_ref, *refs):
    blks = refs[:groups]
    own, below, above, lhs, rhs = refs[groups:]
    sub = sub_ref[0]
    (lo_owner, lo_in), (hi_owner, hi_in) = around(sub, groups)
    scatter(blks, modes, capacity, sub, None, 0, CX, 0, CY // 2, own, lhs, rhs)
    scatter(blks, modes, capacity, lo_owner, lo_in, 0, CX, CY - HALO, HALO // 2, below, lhs, rhs)
    scatter(blks, modes, capacity, hi_owner, hi_in, 0, CX, 0, HALO // 2, above, lhs, rhs)


def shift_sum(x):
    lane = lax.broadcasted_iota(jnp.int32, x.shape, 1)
    left = jnp.where(lane == 0, 0.0, pltpu.roll(x, 1, 1))
    right = jnp.where(lane == CZ - 1, 0.0, pltpu.roll(x, CZ - 1, 1))
    return x + 0.5 * (left + right)


def fluid_kernel(modes, groups, capacity, sub_ref, *refs):
    blks = refs[:groups]
    low, high, mid, below, above, mdiag = refs[groups : groups + 6]
    outs = refs[groups + 6 : 2 * groups + 6]
    edge, corner, second, press, lhs, rhs, force = refs[2 * groups + 6 :]
    sub = sub_ref[0]
    local = blks[0].shape[1]
    half = HALO // 2
    (lo_owner, lo_in), (hi_owner, hi_in) = around(sub, groups)
    for side, both in enumerate((low, high)):
        there = [both.at[k] for k in range(groups)]
        a_first = CX - HALO if side == 0 else 0
        args = (there, modes, capacity)
        scatter(*args, sub, None, a_first, HALO, 0, CY // 2, edge.at[side], lhs, rhs)
        scatter(
            *args, lo_owner, lo_in, a_first, HALO, CY - HALO, half, corner.at[2 * side], lhs, rhs
        )
        scatter(*args, hi_owner, hi_in, a_first, HALO, 0, half, corner.at[2 * side + 1], lhs, rhs)

    def src(a, b):
        lanes = slice((b % 2) * CZ, (b % 2 + 1) * CZ)
        outer = -1
        if a < HALO:
            outer, a = 0, a
        elif a >= CX + HALO:
            outer, a = 1, a - CX - HALO
        else:
            a = a - HALO
        if b < HALO:
            ref, at = (below if outer < 0 else corner.at[2 * outer]), a * half + b // 2
        elif b >= CY + HALO:
            ref = above if outer < 0 else corner.at[2 * outer + 1]
            at = a * half + (b - CY - HALO) // 2
        else:
            ref, at = (mid if outer < 0 else edge.at[outer]), a * (CY // 2) + (b - HALO) // 2
        return ref[at * modes : (at + 1) * modes, lanes]

    for a in range(1, CX + 2 * HALO - 1):
        cols = [
            src(a, b) + 0.5 * (src(a - 1, b) + src(a + 1, b)) for b in range(CY + 2 * HALO)
        ]
        for b in range(1, CY + 2 * HALO - 1):
            t = shift_sum(cols[b] + 0.5 * (cols[b - 1] + cols[b + 1]))
            sec = SEC_U * src(a, b) + SEC_T * t
            if b < HALO:
                sec = sec * lo_in
            if b >= CY + HALO:
                sec = sec * hi_in
            second[a - 1, b - 1] = sec
    for a in range(CX):
        cols = [
            second[a + 1, b] + 0.5 * (second[a, b] + second[a + 2, b]) for b in range(CY + 2)
        ]
        for b in range(CY):
            t = shift_sum(cols[b + 1] + 0.5 * (cols[b] + cols[b + 2]))
            p = PRE_SRC * src(a + HALO, b + HALO) + PRE_SEC * second[a + 1, b + 1] + PRE_T * t
            hi, lo = split(p)
            at = (a * (CY // 2) + b // 2) * modes
            lanes = (b % 2) * CZ
            press[at : at + modes, lanes : lanes + CZ] = hi
            press[at : at + modes, 2 * CZ + lanes : 3 * CZ + lanes] = lo

    def collect(lists, chunk):
        a, b, c, node, weight = lists.load(sub, chunk)
        hot = onehot((b & 1) * CZ + c, 2 * CZ)
        got = dot(press[...], jnp.concatenate([hot, hot], axis=0))
        pair = a * (CY // 2) + lax.shift_right_logical(b, 1)
        wide = jnp.broadcast_to(pair, (modes, lists.width))
        picked = jnp.zeros((modes, lists.width), F32)
        for r in range(CX * CY // 2):
            picked = jnp.where(wide == r, got[r * modes : (r + 1) * modes], picked)
        hi, lo = split(picked * weight)
        both = dot_t(jnp.concatenate([hi, lo], axis=0), onehot(node, local))
        return both[:modes] + both[modes:]

    every = [Lists(blk, modes, capacity) for blk in blks]
    for k, lists in enumerate(every):
        add = collect(lists, 0)
        force[k] = add + mdiag[...] * blks[0][0:modes, :] if k == 0 else add
        for chunk in range(1, lists.chunks):

            @pl.when(jnp.max(lists.row(2, sub, chunk)) > 0.0)
            def _():
                force[k] += collect(lists, chunk)

    for k in range(groups):
        for w in range(3):
            outs[k][w] = force[(1 - k - w) % groups]


def apply_blocks(window, cols_ref, kb_ref, sub, groups, diag, field):
    rb, nb, bs, _ = kb_ref.shape
    pieces = []
    for q in range(rb):
        acc = None
        for n in range(nb):
            j = cols_ref[q, n]
            where = sub + j // rb - 1
            inside = jnp.where((where >= 0) & (where < groups), 1.0, 0.0)
            part = lax.dot_general(
                window[j] * inside,
                kb_ref[q, n],
                (((1,), (0,)), ((), ())),
                precision=lax.Precision.HIGHEST,
                preferred_element_type=F32,
            )
            acc = part if acc is None else acc + part
        pieces.append(acc)
    return diag * field + jnp.concatenate(pieces, axis=1)


def fill_window(win, blocks, bs):
    at = 0
    for blk in blocks:
        for i in range(blk.shape[1] // bs):
            win[at] = blk[:, i * bs : (i + 1) * bs]
            at += 1


def stiff_kernel(modes, groups, sub_ref, cols_ref, prev, own, nxt, diag, kb, out, win):
    bs = kb.shape[2]
    fill_window(win, [prev[0:modes, :], own[0:modes, :], nxt[0:modes, :]], bs)
    out[...] = apply_blocks(win, cols_ref, kb, sub_ref[0], groups, diag[...], own[0:modes, :])


def gram_kernel(modes, groups, sub_ref, cols_ref, v_ref, *refs):
    parts = refs[:groups]
    stiff, kstiff, diag, kb, gram, mass, win = refs[groups:]
    bs = kb.shape[2]
    fields = []
    for w in range(3):
        m = parts[0][w]
        for part in parts[1:]:
            m = m + part[w]
        fields.append(m)
    fill_window(win, fields, bs)
    own = fields[1]
    mass[...] = own
    km = apply_blocks(win, cols_ref, kb, sub_ref[0], groups, diag[...], own)
    v = v_ref[...]
    s = stiff[...]
    left = jnp.concatenate([v, s, own], axis=0)
    right = jnp.concatenate([s, kstiff[...], km, own], axis=0)

    def inner(x, y):
        return lax.dot_general(
            x,
            y,
            (((1,), (1,)), ((), ())),
            precision=lax.Precision.HIGHEST,
            preferred_element_type=F32,
        )

    gram[...] = inner(left, right)
    gram[2 * modes : 3 * modes, 0:modes] = inner(v, v)


def final_kernel(modes, total, gram, stiff, mass, residual, g_stiff, g_plain):
    m = modes
    blocks = [
        [gram[i * m : (i + 1) * m, j * m : (j + 1) * m] for j in range(4)] for i in range(3)
    ]
    (vs, vks, vkm, vm), (ss, sks, skm, sm), (vv, mks, mkm, mm) = blocks
    rows = lax.broadcasted_iota(jnp.int32, (m, m), 0)
    lanes = lax.broadcasted_iota(jnp.int32, (m, m), 1)
    eye = rows == lanes

    def column(x):
        return jnp.sum(jnp.where(eye, x, 0.0), axis=1, keepdims=True)

    def line(x):
        return jnp.sum(jnp.where(eye, x, 0.0), axis=0, keepdims=True)

    tc = column(vs) / column(vm)
    tl = line(vs) / line(vm)
    residual[...] = stiff[...] - tc * mass[...]
    ms = sm.T
    scale = 1.0 / total
    vr = vs - vm * tl
    g_plain[0:m, 0:m] = vv * scale
    g_plain[0:m, m : 2 * m] = vr * scale
    g_plain[m : 2 * m, 0:m] = vr.T * scale
    g_plain[m : 2 * m, m : 2 * m] = (ss - sm * tl - tc * (ms - mm * tl)) * scale
    g_stiff[0:m, 0:m] = vs * scale
    g_stiff[0:m, m : 2 * m] = (vks - vkm * tl) * scale
    g_stiff[m : 2 * m, 0:m] = (ss - tc * ms) * scale
    g_stiff[m : 2 * m, m : 2 * m] = (sks - skm * tl - tc * (mks - mkm * tl)) * scale


def shifted(x, axis, k):
    n = lax.axis_size(axis)
    return lax.ppermute(x, axis, [(i, (i + k) % n) for i in range(n)])


def swapped(x, axis, k):
    n = lax.axis_size(axis)
    return lax.ppermute(x, axis, [(i, i ^ k) for i in range(n)])


def summed(x, axis, bit):
    n = lax.axis_size(axis)
    while (1 << bit) < n:
        if (4 << bit) <= n:
            one, two, three = [swapped(x, axis, k << bit) for k in (1, 2, 3)]
            x = (x + one) + (two + three)
            bit += 2
        else:
            x = x + swapped(x, axis, 1 << bit)
            bit += 1
    return x


def smem():
    return pl.BlockSpec(memory_space=pltpu.SMEM)


def vmem():
    return pl.BlockSpec(memory_space=pltpu.VMEM)


def call(kernel, name, out_shape, scalars, arrays, scratch, flops):
    return pl.pallas_call(
        kernel,
        name=name,
        out_shape=out_shape,
        in_specs=[smem()] * len(scalars) + [vmem()] * len(arrays),
        out_specs=jax.tree.map(lambda _: vmem(), out_shape),
        scratch_shapes=scratch,
        cost_estimate=pl.CostEstimate(flops=flops, transcendentals=0, bytes_accessed=1 << 20),
    )(*scalars, *arrays)


def body(
    block_vectors,
    stiffness,
    mass_diag,
    kblocks,
    block_cols,
    slot_node,
    slot_owner,
    slot_cell,
    slot_weight,
    live_slots,
):
    modes, local = block_vectors.shape
    groups = lax.axis_size("sub")
    slots = slot_node.shape[0]
    bs = kblocks.shape[2]
    total = local * lax.axis_size("passage") * groups
    sub = lax.axis_index("sub").astype(jnp.int32).reshape(1)
    deep, wide = slots // 128, 128
    capacity = 2 * slots // groups
    pack = call(
        functools.partial(pack_kernel, modes, groups),
        "pack",
        jax.ShapeDtypeStruct((modes + 3 * deep, local), F32),
        [live_slots],
        [block_vectors]
        + [x.reshape(deep, wide) for x in (slot_owner, slot_cell, slot_node, slot_weight)],
        [],
        1 << 28,
    )
    packs = [pack] + [shifted(pack, "sub", k) for k in range(1, groups)]
    both = jnp.stack(packs)
    low = shifted(both, "passage", 1)
    high = shifted(both, "passage", -1)
    diag = stiffness[None, :]
    window = [packs[1], packs[0], packs[groups - 1]]
    nwin = 3 * local // bs
    stiff = call(
        functools.partial(stiff_kernel, modes, groups),
        "stiff",
        jax.ShapeDtypeStruct((modes, local), F32),
        [sub, block_cols],
        [*window, diag, kblocks],
        [pltpu.VMEM((nwin, modes, bs), F32)],
        1 << 29,
    )
    stiff_prev = shifted(stiff, "sub", 1)
    stiff_next = shifted(stiff, "sub", -1)
    kstiff = call(
        functools.partial(stiff_kernel, modes, groups),
        "stiff_image",
        jax.ShapeDtypeStruct((modes, local), F32),
        [sub, block_cols],
        [stiff_prev, stiff, stiff_next, diag, kblocks],
        [pltpu.VMEM((nwin, modes, bs), F32)],
        1 << 29,
    )
    pairs = CY // 2
    half = HALO // 2
    width = min(local, capacity)
    rhs = pltpu.VMEM((2 * CZ, 2 * width * groups), BF)

    def field(*shape):
        return jax.ShapeDtypeStruct(shape, F32)

    source = call(
        functools.partial(own_source_kernel, modes, groups, capacity),
        "own_source",
        (
            field(CX * pairs * modes, 2 * CZ),
            field(CX * half * modes, 2 * CZ),
            field(CX * half * modes, 2 * CZ),
        ),
        [sub],
        packs,
        [pltpu.VMEM((CX * pairs * modes, 2 * width * groups), BF), rhs],
        1 << 32,
    )
    force = call(
        functools.partial(fluid_kernel, modes, groups, capacity),
        "fluid",
        tuple(field(3, modes, local) for _ in range(groups)),
        [sub],
        [*packs, low, high, *source, mass_diag[None, :]],
        [
            pltpu.VMEM((2, HALO * pairs * modes, 2 * CZ), F32),
            pltpu.VMEM((4, HALO * half * modes, 2 * CZ), F32),
            pltpu.VMEM((CX + 2, CY + 2, modes, CZ), F32),
            pltpu.VMEM((CX * pairs * modes, 4 * CZ), BF),
            pltpu.VMEM((HALO * pairs * modes, 2 * width * groups), BF),
            rhs,
            pltpu.VMEM((groups, modes, local), F32),
        ],
        1 << 32,
    )
    parts = [force[0]] + [shifted(force[k], "sub", k) for k in range(1, groups)]
    gram, mass = call(
        functools.partial(gram_kernel, modes, groups),
        "gram",
        (field(3 * modes, 4 * modes), field(modes, local)),
        [sub, block_cols],
        [block_vectors, *parts, stiff, kstiff, diag, kblocks],
        [pltpu.VMEM((nwin, modes, bs), F32)],
        1 << 29,
    )
    gram = gram + swapped(gram, "passage", 1)
    gram = summed(gram, "passage", 1)
    gram = summed(gram, "sub", 0)
    return call(
        functools.partial(final_kernel, modes, float(total)),
        "final",
        (
            jax.ShapeDtypeStruct((modes, local), F32),
            jax.ShapeDtypeStruct((2 * modes, 2 * modes), F32),
            jax.ShapeDtypeStruct((2 * modes, 2 * modes), F32),
        ),
        [],
        [gram, stiff, mass],
        [],
        1 << 20,
    )


def solution(mesh):
    return jax.shard_map(
        body,
        mesh=mesh,
        in_specs=(
            P(None, ("passage", "sub")),
            P(("passage", "sub")),
            P(("passage", "sub")),
            P(("passage", "sub"), None, None, None),
            P(("passage", "sub"), None),
            P(("passage", "sub")),
            P(("passage", "sub"), None),
            P(("passage", "sub")),
            P(("passage", "sub")),
            P(("passage", "sub")),
        ),
        out_specs=(P(None, ("passage", "sub")), P(), P()),
        check_vma=False,
    )
```

```python
import functools
import jax
import jax.numpy as jnp
from jax import lax
from jax.experimental import pallas as pl
from jax.experimental.pallas import tpu as pltpu
from jax.sharding import PartitionSpec as P

CX = 8
CY = 8
CZ = 128
HALO = 2

center_weight = 15.0
lower_bound = 1.0 / 15.0
upper_bound = 17.0 / 15.0
middle = (upper_bound + lower_bound) / 2.0
radius = (upper_bound - lower_bound) / 2.0
sigma_ratio = middle / radius
first_rho = 1.0 / sigma_ratio
second_rho = 1.0 / (2.0 * sigma_ratio - first_rho)
third_rho = 1.0 / (2.0 * sigma_ratio - second_rho)

FIRST = 1.0 / (center_weight * middle)
GAIN2 = 2.0 * second_rho / (radius * center_weight)
SEC_U = FIRST * (1.0 + second_rho * first_rho) + GAIN2 * (1.0 - 17.0 * FIRST)
SEC_T = GAIN2 * 2.0 * FIRST
STEP3 = third_rho * second_rho
GAIN3 = 2.0 * third_rho / (radius * center_weight)
PRE_SRC = GAIN3 - STEP3 * FIRST
PRE_SEC = 1.0 + STEP3 - 17.0 * GAIN3
PRE_T = 2.0 * GAIN3

BF = jnp.bfloat16
F32 = jnp.float32
CELLS = CX * CY * CZ


def log2(n):
    return n.bit_length() - 1


def split(x):
    hi = x.astype(BF)
    return hi, (x - hi.astype(F32)).astype(BF)


def lanes_from(x, index):
    return jnp.take_along_axis(
        x, jnp.broadcast_to(index, x.shape), axis=1, mode="promise_in_bounds"
    )


def onehot(values, height):
    shape = (height, values.shape[1])
    rows = lax.broadcasted_iota(jnp.int32, shape, 0)
    return jnp.where(rows == values, 1.0, 0.0).astype(BF)


def dot_t(x, y):
    return lax.dot_general(x, y, (((1,), (1,)), ((), ())), preferred_element_type=F32)


def dot(x, y):
    return lax.dot_general(x, y, (((1,), (0,)), ((), ())), preferred_element_type=F32)


def pack_kernel(modes, groups, live_ref, *refs):
    sources, (out, mdiag, diag, cols) = refs[:8], refs[8:12]
    owner_ref, cell_ref, node_ref, weight_ref, sems = refs[12:]
    targets = [owner_ref, cell_ref, node_ref, weight_ref]
    targets += [out.at[0:modes, :], mdiag, diag, cols]
    copies = [
        pltpu.make_async_copy(x, y, sems.at[i]) for i, (x, y) in enumerate(zip(sources, targets))
    ]
    for copy in copies:
        copy.start()
    for copy in copies[:4]:
        copy.wait()
    deep, wide = owner_ref.shape
    capacity = 2 * deep * wide // groups
    keys = groups * CX
    owner, cell, weight = owner_ref[...], cell_ref[...], weight_ref[...]
    shape = (deep, wide)
    place = lax.broadcasted_iota(jnp.int32, shape, 0) * wide + lax.broadcasted_iota(
        jnp.int32, shape, 1
    )
    live = place < live_ref[0]
    a = lax.shift_right_logical(cell, log2(CY * CZ))
    key = jnp.where(live, owner * CX + ((a + HALO) & (CX - 1)), -1)
    hots = jnp.concatenate([jnp.where(key == k, 1.0, 0.0) for k in range(keys)], axis=0).astype(BF)
    rows = lax.broadcasted_iota(jnp.int32, (wide, wide), 0)
    lanes = lax.broadcasted_iota(jnp.int32, (wide, wide), 1)
    within = dot(hots, jnp.where(rows <= lanes, 1.0, 0.0).astype(BF))
    size = keys * deep
    rows = lax.broadcasted_iota(jnp.int32, (size, size), 0)
    lanes = lax.broadcasted_iota(jnp.int32, (size, size), 1)
    shift = log2(CX * deep)
    same = lax.shift_right_logical(rows, shift) == lax.shift_right_logical(lanes, shift)
    earlier = jnp.where(same & (lanes < rows), 1.0, 0.0).astype(BF)
    ahead = dot(dot(earlier, hots).astype(BF), jnp.ones((wide, wide), BF))
    order = within + ahead - 1.0
    pos = jnp.zeros(shape, F32)
    for k in range(keys):
        pos = jnp.where(key == k, order[k * deep : (k + 1) * deep], pos)
    target = owner * capacity + pos.astype(jnp.int32)
    line = lax.shift_right_logical(target, log2(wide))
    half = deep
    line = jnp.where(live, lax.shift_right_logical(line, 1) + (line & 1) * half, -1)
    lane = target & (wide - 1)
    w1 = weight.astype(BF).astype(F32)
    w2 = (weight - w1).astype(BF).astype(F32)
    values = [
        lax.shift_right_logical(cell, 8).astype(F32),
        (cell & 255).astype(F32),
        node_ref[...].astype(F32),
        w1,
        w2,
        weight - w1 - w2,
    ]
    lefts, rights = [], []
    for r in range(deep):
        into = lax.broadcasted_iota(jnp.int32, (2 * half, wide), 0) == line[r : r + 1]
        lefts.append(
            jnp.concatenate([jnp.where(into, v[r : r + 1], 0.0) for v in values], axis=0).astype(BF)
        )
        rights.append(onehot(lane[r : r + 1], wide))
    listed = dot_t(jnp.concatenate(lefts, axis=1), jnp.concatenate(rights, axis=1))
    part = [listed[i * 2 * half : (i + 1) * 2 * half] for i in range(6)]
    lists = [256.0 * part[0] + part[1], part[2], part[3] + part[4] + part[5]]
    for i, x in enumerate(lists):
        at = modes + i * half
        out[at : at + half, 0:wide] = x[:half]
        out[at : at + half, wide : 2 * wide] = x[half:]
    for copy in copies[4:]:
        copy.wait()


class Lists:
    def __init__(self, blk, modes, capacity, width=None):
        self.blk, self.modes = blk, modes
        self.local = blk.shape[1]
        self.lines = (blk.shape[0] - modes) // 3
        self.width = min(width or self.local, capacity)
        self.capacity = capacity
        self.chunks = capacity // self.width

    def row(self, kind, owner, chunk):
        at = owner * self.capacity + chunk * self.width
        line = lax.shift_right_logical(at, log2(self.local))
        x = self.blk[pl.ds(self.modes + kind * self.lines + line, 1), :]
        if self.width < self.local:
            group = lax.shift_right_logical(at, log2(self.width)) & (self.local // self.width - 1)
            got = x[:, : self.width]
            for g in range(1, self.local // self.width):
                got = jnp.where(group == g, x[:, g * self.width : (g + 1) * self.width], got)
            x = got
        return x

    def load(self, owner, chunk):
        cell = self.row(0, owner, chunk).astype(jnp.int32)
        node = self.row(1, owner, chunk).astype(jnp.int32)
        weight = self.row(2, owner, chunk)
        a = lax.shift_right_logical(cell, log2(CY * CZ))
        b = lax.shift_right_logical(cell, log2(CZ)) & (CY - 1)
        return a, b, cell & (CZ - 1), node, weight


def fill(lists, owner, chunk, a_first, a_count, b_first, b_count, inside, lhs, rhs, at, side):
    modes, width = lists.modes, lists.width
    a, b, c, node, weight = lists.load(owner, chunk)
    if inside is not None:
        weight = weight * inside
    aloc, bloc = a - a_first, b - b_first
    valid = (aloc >= 0) & (aloc < a_count) & (bloc >= 0) & (bloc < 2 * b_count)
    pair = jnp.where(valid, aloc * b_count + lax.shift_right_arithmetic(bloc, 1), -1)
    place = (b & 1) * CZ + c
    pieces = []
    for h in range(width // 128):
        idx = node[:, h * 128 : (h + 1) * 128]
        got = None
        for g in range(lists.local // 128):
            part = lanes_from(lists.blk[0:modes, g * 128 : (g + 1) * 128], idx & 127)
            got = part if g == 0 else jnp.where(lax.shift_right_logical(idx, 7) == g, part, got)
        pieces.append(got)
    hi, lo = split(jnp.concatenate(pieces, axis=1) * weight)
    wide = jnp.broadcast_to(pair.astype(F32), (modes, width)).astype(BF)
    zero = jnp.zeros((modes, width), BF)
    for r in range(a_count * b_count):
        mask = wide == jnp.asarray(r, BF)
        lhs[r * modes : (r + 1) * modes, at : at + width] = jnp.where(mask, hi, zero)
        lhs[r * modes : (r + 1) * modes, at + width : at + 2 * width] = jnp.where(mask, lo, zero)
    hot = onehot(place, 2 * CZ)
    rhs[:, at : at + width] = hot
    rhs[:, at + width : at + 2 * width] = hot


def scatter(
    blks, modes, capacity, owner, inside, a_first, a_count, b_first, b_count, out, lhs, rhs, width=None
):
    every = [Lists(blk, modes, capacity, width) for blk in blks]
    width = every[0].width
    rows = a_count * b_count * modes
    spec = (a_first, a_count, b_first, b_count, inside)
    left = lhs.at[0:rows, :]
    counts = []
    for k, lists in enumerate(every):
        last = jnp.zeros((1, width), jnp.int32)
        for chunk in range(1, lists.chunks):
            a, b, c, node, weight = lists.load(owner, chunk)
            needed = (weight > 0.0) & (a >= a_first) & (a < a_first + a_count)
            last = jnp.where(needed, chunk + 1, last)
        counts.append(jnp.max(last))
        fill(lists, owner, 0, *spec, left, rhs, 2 * k * width, None)
    deep = 2 * width * len(every)
    out[...] = dot_t(lhs[0:rows, 0:deep], rhs[:, 0:deep])
    if every[0].chunks == 1:
        return
    for lists, count in zip(every, counts):

        def more(chunk, carry):
            fill(lists, owner, chunk, *spec, left, rhs, 0, None)
            out[...] += dot_t(lhs[0:rows, 0 : 2 * width], rhs[:, 0 : 2 * width])
            return carry

        lax.fori_loop(1, count, more, 0)


def around(sub, groups):
    below = jnp.maximum(sub - 1, 0), jnp.where(sub > 0, 1.0, 0.0)
    above = jnp.minimum(sub + 1, groups - 1), jnp.where(sub < groups - 1, 1.0, 0.0)
    return below, above


def own_source_kernel(modes, groups, capacity, sub_ref, *refs):
    blks = refs[:groups]
    own, below, above, lhs, rhs = refs[groups + 1 :]
    sub = sub_ref[0]
    (lo_owner, lo_in), (hi_owner, hi_in) = around(sub, groups)
    scatter(blks, modes, capacity, sub, None, 0, CX, 0, CY // 2, own, lhs, rhs)
    scatter(blks, modes, capacity, lo_owner, lo_in, 0, CX, CY - HALO, HALO // 2, below, lhs, rhs)
    scatter(blks, modes, capacity, hi_owner, hi_in, 0, CX, 0, HALO // 2, above, lhs, rhs)


def shift_sum(x):
    lane = lax.broadcasted_iota(jnp.int32, x.shape, 1)
    left = jnp.where(lane == 0, 0.0, pltpu.roll(x, 1, 1))
    right = jnp.where(lane == CZ - 1, 0.0, pltpu.roll(x, CZ - 1, 1))
    return x + 0.5 * (left + right)


def fluid_kernel(modes, groups, capacity, sub_ref, *refs):
    blks = refs[:groups]
    low, high, mid, below, above, mdiag, stiff = refs[groups : groups + 7]
    outs = refs[groups + 7 : 2 * groups + 7]
    edge, corner, second, press, lhs, rhs, force = refs[2 * groups + 7 :]
    sub = sub_ref[0]
    local = blks[0].shape[1]
    half = HALO // 2
    (lo_owner, lo_in), (hi_owner, hi_in) = around(sub, groups)
    for side, both in enumerate((low, high)):
        there = [both.at[k] for k in range(groups)]
        a_first = CX - HALO if side == 0 else 0
        wide = 128 if side == 0 else 256
        args = (there, modes, capacity)
        scatter(*args, sub, None, a_first, HALO, 0, CY // 2, edge.at[side], lhs, rhs, wide)
        spec = (a_first, HALO, CY - HALO, half)
        scatter(*args, lo_owner, lo_in, *spec, corner.at[2 * side], lhs, rhs, wide)
        scatter(*args, hi_owner, hi_in, a_first, HALO, 0, half, corner.at[2 * side + 1], lhs, rhs, wide)

    def src(a, b):
        lanes = slice((b % 2) * CZ, (b % 2 + 1) * CZ)
        outer = -1
        if a < HALO:
            outer, a = 0, a
        elif a >= CX + HALO:
            outer, a = 1, a - CX - HALO
        else:
            a = a - HALO
        if b < HALO:
            ref, at = (below if outer < 0 else corner.at[2 * outer]), a * half + b // 2
        elif b >= CY + HALO:
            ref = above if outer < 0 else corner.at[2 * outer + 1]
            at = a * half + (b - CY - HALO) // 2
        else:
            ref, at = (mid if outer < 0 else edge.at[outer]), a * (CY // 2) + (b - HALO) // 2
        return ref[at * modes : (at + 1) * modes, lanes]

    for a in range(1, CX + 2 * HALO - 1):
        cols = [
            src(a, b) + 0.5 * (src(a - 1, b) + src(a + 1, b)) for b in range(CY + 2 * HALO)
        ]
        for b in range(1, CY + 2 * HALO - 1):
            t = shift_sum(cols[b] + 0.5 * (cols[b - 1] + cols[b + 1]))
            sec = SEC_U * src(a, b) + SEC_T * t
            if b < HALO:
                sec = sec * lo_in
            if b >= CY + HALO:
                sec = sec * hi_in
            second[a - 1, b - 1] = sec
    for a in range(CX):
        cols = [
            second[a + 1, b] + 0.5 * (second[a, b] + second[a + 2, b]) for b in range(CY + 2)
        ]
        for b in range(CY):
            t = shift_sum(cols[b + 1] + 0.5 * (cols[b] + cols[b + 2]))
            p = PRE_SRC * src(a + HALO, b + HALO) + PRE_SEC * second[a + 1, b + 1] + PRE_T * t
            hi, lo = split(p)
            at = (a * (CY // 2) + b // 2) * modes
            lanes = (b % 2) * CZ
            press[at : at + modes, lanes : lanes + CZ] = hi
            press[at : at + modes, 2 * CZ + lanes : 3 * CZ + lanes] = lo

    def collect(lists, chunk):
        a, b, c, node, weight = lists.load(sub, chunk)
        hot = onehot((b & 1) * CZ + c, 2 * CZ)
        got = dot(press[...], jnp.concatenate([hot, hot], axis=0))
        pair = a * (CY // 2) + lax.shift_right_logical(b, 1)
        wide = jnp.broadcast_to(pair, (modes, lists.width))
        picked = jnp.zeros((modes, lists.width), F32)
        for r in range(CX * CY // 2):
            picked = jnp.where(wide == r, got[r * modes : (r + 1) * modes], picked)
        hi, lo = split(picked * weight)
        both = dot_t(jnp.concatenate([hi, lo], axis=0), onehot(node, local))
        return both[:modes] + both[modes:]

    every = [Lists(blk, modes, capacity) for blk in blks]
    for k, lists in enumerate(every):
        add = collect(lists, 0)
        force[k] = add + mdiag[...] * blks[0][0:modes, :] if k == 0 else add
        for chunk in range(1, lists.chunks):

            @pl.when(jnp.max(lists.row(2, sub, chunk)) > 0.0)
            def _():
                force[k] += collect(lists, chunk)

    for k in range(groups):
        for w in range(3):
            outs[k][w] = force[(1 - k - w) % groups]
        if k in (1, groups - 1):
            outs[k][3] = stiff[...]


def apply_blocks(window, cols_ref, kb_ref, sub, groups, diag, field):
    rb, nb, bs, _ = kb_ref.shape
    pieces = []
    for q in range(rb):
        acc = None
        for n in range(nb):
            j = cols_ref[q, n]
            where = sub + j // rb - 1
            inside = jnp.where((where >= 0) & (where < groups), 1.0, 0.0)
            part = lax.dot_general(
                window[j] * inside,
                kb_ref[q, n],
                (((1,), (0,)), ((), ())),
                precision=lax.Precision.HIGHEST,
                preferred_element_type=F32,
            )
            acc = part if acc is None else acc + part
        pieces.append(acc)
    return diag * field + jnp.concatenate(pieces, axis=1)


def fill_window(win, blocks, bs):
    at = 0
    for blk in blocks:
        for i in range(blk.shape[1] // bs):
            win[at] = blk[:, i * bs : (i + 1) * bs]
            at += 1


def stiff_kernel(modes, groups, sub_ref, cols_ref, prev, own, nxt, diag, kb, out, win):
    bs = kb.shape[2]
    fill_window(win, [prev[0:modes, :], own[0:modes, :], nxt[0:modes, :]], bs)
    out[...] = apply_blocks(win, cols_ref, kb, sub_ref[0], groups, diag[...], own[0:modes, :])


def gram_kernel(modes, groups, sub_ref, cols_ref, pack, *refs):
    parts = refs[:groups]
    stiff, diag, kb, keep, send, mass, win, gram = refs[groups:]
    bs = kb.shape[2]
    fields = []
    for w in range(3):
        m = parts[0][w]
        for part in parts[1:]:
            m = m + part[w]
        fields.append(m)
    own = fields[1]
    mass[...] = own
    s = stiff[...]
    ends = [parts[1][3], s, parts[groups - 1][3]]
    both = [jnp.concatenate([x, y], axis=0) for x, y in zip(ends, fields)]
    fill_window(win, both, bs)
    image = apply_blocks(win, cols_ref, kb, sub_ref[0], groups, diag[...], both[1])
    v = pack[0:modes, :]
    left = jnp.concatenate([v, s, own], axis=0)
    right = jnp.concatenate([s, image, own], axis=0)

    def inner(x, y):
        return lax.dot_general(
            x,
            y,
            (((1,), (1,)), ((), ())),
            precision=lax.Precision.HIGHEST,
            preferred_element_type=F32,
        )

    whole = inner(left, right)
    half = 3 * modes // 2
    gram[0] = whole[:half]
    gram[1] = whole[half:]
    gram[1, 2 * modes - half : 3 * modes - half, 0:modes] = inner(v, v)
    core = sub_ref[1]
    keep[...] = gram[core]
    send[...] = gram[1 - core]


def final_kernel(modes, total, sub_ref, mine, other, stiff, mass, residual, g_stiff, g_plain, gram):
    m = modes
    core = sub_ref[1]
    half = 3 * m // 2
    gram[pl.ds(pl.multiple_of(core * half, half), half), :] = mine[...]
    gram[pl.ds(pl.multiple_of((1 - core) * half, half), half), :] = other[...]
    blocks = [
        [gram[i * m : (i + 1) * m, j * m : (j + 1) * m] for j in range(4)] for i in range(3)
    ]
    (vs, vks, vkm, vm), (ss, sks, skm, sm), (vv, mks, mkm, mm) = blocks
    rows = lax.broadcasted_iota(jnp.int32, (m, m), 0)
    lanes = lax.broadcasted_iota(jnp.int32, (m, m), 1)
    eye = rows == lanes

    def column(x):
        return jnp.sum(jnp.where(eye, x, 0.0), axis=1, keepdims=True)

    def line(x):
        return jnp.sum(jnp.where(eye, x, 0.0), axis=0, keepdims=True)

    tc = column(vs) / column(vm)
    tl = line(vs) / line(vm)
    residual[...] = stiff[...] - tc * mass[...]
    ms = sm.T
    scale = 1.0 / total
    vr = vs - vm * tl
    g_plain[0:m, 0:m] = vv * scale
    g_plain[0:m, m : 2 * m] = vr * scale
    g_plain[m : 2 * m, 0:m] = vr.T * scale
    g_plain[m : 2 * m, m : 2 * m] = (ss - sm * tl - tc * (ms - mm * tl)) * scale
    g_stiff[0:m, 0:m] = vs * scale
    g_stiff[0:m, m : 2 * m] = (vks - vkm * tl) * scale
    g_stiff[m : 2 * m, 0:m] = (ss - tc * ms) * scale
    g_stiff[m : 2 * m, m : 2 * m] = (sks - skm * tl - tc * (mks - mkm * tl)) * scale


def shifted(x, axis, k):
    n = lax.axis_size(axis)
    return lax.ppermute(x, axis, [(i, (i + k) % n) for i in range(n)])


def swapped(x, axis, k):
    n = lax.axis_size(axis)
    return lax.ppermute(x, axis, [(i, i ^ k) for i in range(n)])


def summed(x, axis, bit):
    n = lax.axis_size(axis)
    while (1 << bit) < n:
        if (4 << bit) <= n:
            one, two, three = [swapped(x, axis, k << bit) for k in (1, 2, 3)]
            x = (x + one) + (two + three)
            bit += 2
        else:
            x = x + swapped(x, axis, 1 << bit)
            bit += 1
    return x


def smem():
    return pl.BlockSpec(memory_space=pltpu.SMEM)


def vmem():
    return pl.BlockSpec(memory_space=pltpu.VMEM)


def call(kernel, name, out_shape, scalars, arrays, scratch, flops, mib=4):
    return pl.pallas_call(
        kernel,
        name=name,
        out_shape=out_shape,
        in_specs=[smem()] * len(scalars) + [vmem()] * len(arrays),
        out_specs=jax.tree.map(lambda _: vmem(), out_shape),
        scratch_shapes=scratch,
        compiler_params=pltpu.CompilerParams(vmem_limit_bytes=mib << 20),
        cost_estimate=pl.CostEstimate(flops=flops, transcendentals=0, bytes_accessed=1 << 20),
    )(*scalars, *arrays)


def body(
    block_vectors,
    stiffness,
    mass_diag,
    kblocks,
    block_cols,
    slot_node,
    slot_owner,
    slot_cell,
    slot_weight,
    live_slots,
):
    modes, local = block_vectors.shape
    groups = lax.axis_size("sub")
    slots = slot_node.shape[0]
    bs = kblocks.shape[2]
    total = local * lax.axis_size("passage") * groups
    sub = jnp.stack([lax.axis_index("sub"), lax.axis_index("passage") & 1]).astype(jnp.int32)
    deep, wide = slots // 128, 128
    capacity = 2 * slots // groups
    slotted = [x.reshape(deep, wide) for x in (slot_owner, slot_cell, slot_node, slot_weight)]
    pack, mdiag, diag, cols = pl.pallas_call(
        functools.partial(pack_kernel, modes, groups),
        name="pack",
        out_shape=(
            jax.ShapeDtypeStruct((modes + 3 * deep, local), F32),
            jax.ShapeDtypeStruct((1, local), F32),
            jax.ShapeDtypeStruct((1, local), F32),
            jax.ShapeDtypeStruct(block_cols.shape, jnp.int32),
        ),
        in_specs=[smem()] + [pl.BlockSpec(memory_space=pltpu.MemorySpace.HBM)] * 8,
        out_specs=(vmem(), vmem(), vmem(), vmem()),
        scratch_shapes=[pltpu.VMEM((deep, wide), x.dtype) for x in slotted]
        + [pltpu.SemaphoreType.DMA((8,))],
        compiler_params=pltpu.CompilerParams(vmem_limit_bytes=4 << 20),
        cost_estimate=pl.CostEstimate(flops=1 << 28, transcendentals=0, bytes_accessed=1 << 20),
    )(
        live_slots,
        *[
            pltpu.with_memory_space_constraint(x, pltpu.MemorySpace.HBM)
            for x in (
                *slotted,
                block_vectors,
                mass_diag[None, :],
                stiffness[None, :],
                block_cols,
            )
        ]
    )
    packs = [pack] + [shifted(pack, "sub", k) for k in range(1, groups)]
    both = jnp.stack(packs)
    low = shifted(both, "passage", 1)
    high = shifted(both, "passage", -1)
    window = [packs[1], packs[0], packs[groups - 1]]
    nwin = 3 * local // bs
    stiff = call(
        functools.partial(stiff_kernel, modes, groups),
        "stiff",
        jax.ShapeDtypeStruct((modes, local), F32),
        [sub, cols],
        [*window, diag, kblocks],
        [pltpu.VMEM((nwin, modes, bs), F32)],
        1 << 29,
    )
    pairs = CY // 2
    half = HALO // 2
    width = min(local, capacity)
    rhs = pltpu.VMEM((2 * CZ, 2 * width * groups), BF)

    def field(*shape):
        return jax.ShapeDtypeStruct(shape, F32)

    source = call(
        functools.partial(own_source_kernel, modes, groups, capacity),
        "own_source",
        (
            field(CX * pairs * modes, 2 * CZ),
            field(CX * half * modes, 2 * CZ),
            field(CX * half * modes, 2 * CZ),
        ),
        [sub],
        [*packs, stiff],
        [pltpu.VMEM((CX * pairs * modes, 2 * width * groups), BF), rhs],
        1 << 32,
        16,
    )
    force = call(
        functools.partial(fluid_kernel, modes, groups, capacity),
        "fluid",
        tuple(field(4 if k in (1, groups - 1) else 3, modes, local) for k in range(groups)),
        [sub],
        [*packs, low, high, *source, mdiag, stiff],
        [
            pltpu.VMEM((2, HALO * pairs * modes, 2 * CZ), F32),
            pltpu.VMEM((4, HALO * half * modes, 2 * CZ), F32),
            pltpu.VMEM((CX + 2, CY + 2, modes, CZ), F32),
            pltpu.VMEM((CX * pairs * modes, 4 * CZ), BF),
            pltpu.VMEM((HALO * pairs * modes, 2 * width * groups), BF),
            rhs,
            pltpu.VMEM((groups, modes, local), F32),
        ],
        1 << 32,
        16,
    )
    parts = [force[0]] + [shifted(force[k], "sub", k) for k in range(1, groups)]
    keep, send, mass = call(
        functools.partial(gram_kernel, modes, groups),
        "gram",
        (field(3 * modes // 2, 4 * modes), field(3 * modes // 2, 4 * modes), field(modes, local)),
        [sub, cols],
        [pack, *parts, stiff, diag, kblocks],
        [
            pltpu.VMEM((nwin, 2 * modes, bs), F32),
            pltpu.VMEM((2, 3 * modes // 2, 4 * modes), F32),
        ],
        1 << 29,
    )
    mine = keep + swapped(send, "passage", 1)
    mine = summed(mine, "passage", 1)
    mine = summed(mine, "sub", 0)
    other = swapped(mine, "passage", 1)
    return call(
        functools.partial(final_kernel, modes, float(total)),
        "final",
        (field(modes, local), field(2 * modes, 2 * modes), field(2 * modes, 2 * modes)),
        [sub],
        [mine, other, stiff, mass],
        [pltpu.VMEM((3 * modes, 4 * modes), F32)],
        1 << 20,
    )


def solution(mesh):
    return jax.shard_map(
        body,
        mesh=mesh,
        in_specs=(
            P(None, ("passage", "sub")),
            P(("passage", "sub")),
            P(("passage", "sub")),
            P(("passage", "sub"), None, None, None),
            P(("passage", "sub"), None),
            P(("passage", "sub")),
            P(("passage", "sub"), None),
            P(("passage", "sub")),
            P(("passage", "sub")),
            P(("passage", "sub")),
        ),
        out_specs=(P(None, ("passage", "sub")), P(), P()),
        check_vma=False,
    )
```

```python
import functools
import jax
import jax.numpy as jnp
from jax import lax
from jax.experimental import pallas as pl
from jax.experimental.pallas import tpu as pltpu
from jax.sharding import PartitionSpec as P

CX = 8
CY = 8
CZ = 128
HALO = 2

center_weight = 15.0
lower_bound = 1.0 / 15.0
upper_bound = 17.0 / 15.0
middle = (upper_bound + lower_bound) / 2.0
radius = (upper_bound - lower_bound) / 2.0
sigma_ratio = middle / radius
first_rho = 1.0 / sigma_ratio
second_rho = 1.0 / (2.0 * sigma_ratio - first_rho)
third_rho = 1.0 / (2.0 * sigma_ratio - second_rho)

FIRST = 1.0 / (center_weight * middle)
GAIN2 = 2.0 * second_rho / (radius * center_weight)
SEC_U = FIRST * (1.0 + second_rho * first_rho) + GAIN2 * (1.0 - 17.0 * FIRST)
SEC_T = GAIN2 * 2.0 * FIRST
STEP3 = third_rho * second_rho
GAIN3 = 2.0 * third_rho / (radius * center_weight)
PRE_SRC = GAIN3 - STEP3 * FIRST
PRE_SEC = 1.0 + STEP3 - 17.0 * GAIN3
PRE_T = 2.0 * GAIN3

BF = jnp.bfloat16
F32 = jnp.float32
CELLS = CX * CY * CZ


def log2(n):
    return n.bit_length() - 1


def split(x):
    hi = x.astype(BF)
    return hi, (x - hi.astype(F32)).astype(BF)


def lanes_from(x, index):
    return jnp.take_along_axis(
        x, jnp.broadcast_to(index, x.shape), axis=1, mode="promise_in_bounds"
    )


def onehot(values, height):
    shape = (height, values.shape[1])
    rows = lax.broadcasted_iota(jnp.int32, shape, 0)
    return jnp.where(rows == values, 1.0, 0.0).astype(BF)


def dot_t(x, y):
    return lax.dot_general(x, y, (((1,), (1,)), ((), ())), preferred_element_type=F32)


def dot(x, y):
    return lax.dot_general(x, y, (((1,), (0,)), ((), ())), preferred_element_type=F32)


def pack_kernel(modes, groups, live_ref, *refs):
    sources, (out, mdiag, diag, cols) = refs[:8], refs[8:12]
    owner_ref, cell_ref, node_ref, weight_ref, sems = refs[12:]
    targets = [owner_ref, cell_ref, node_ref, weight_ref]
    targets += [out.at[0:modes, :], mdiag, diag, cols]
    copies = [
        pltpu.make_async_copy(x, y, sems.at[i]) for i, (x, y) in enumerate(zip(sources, targets))
    ]
    for copy in copies:
        copy.start()
    for copy in copies[:4]:
        copy.wait()
    deep, wide = owner_ref.shape
    capacity = 2 * deep * wide // groups
    keys = groups * CX
    owner, cell, weight = owner_ref[...], cell_ref[...], weight_ref[...]
    shape = (deep, wide)
    place = lax.broadcasted_iota(jnp.int32, shape, 0) * wide + lax.broadcasted_iota(
        jnp.int32, shape, 1
    )
    live = place < live_ref[0]
    a = lax.shift_right_logical(cell, log2(CY * CZ))
    key = jnp.where(live, owner * CX + ((a + HALO) & (CX - 1)), -1)
    hots = jnp.concatenate([jnp.where(key == k, 1.0, 0.0) for k in range(keys)], axis=0).astype(BF)
    rows = lax.broadcasted_iota(jnp.int32, (wide, wide), 0)
    lanes = lax.broadcasted_iota(jnp.int32, (wide, wide), 1)
    within = dot(hots, jnp.where(rows <= lanes, 1.0, 0.0).astype(BF))
    size = keys * deep
    rows = lax.broadcasted_iota(jnp.int32, (size, size), 0)
    lanes = lax.broadcasted_iota(jnp.int32, (size, size), 1)
    shift = log2(CX * deep)
    same = lax.shift_right_logical(rows, shift) == lax.shift_right_logical(lanes, shift)
    earlier = jnp.where(same & (lanes < rows), 1.0, 0.0).astype(BF)
    ahead = dot(dot(earlier, hots).astype(BF), jnp.ones((wide, wide), BF))
    order = within + ahead - 1.0
    pos = jnp.zeros(shape, F32)
    for k in range(keys):
        pos = jnp.where(key == k, order[k * deep : (k + 1) * deep], pos)
    target = owner * capacity + pos.astype(jnp.int32)
    line = lax.shift_right_logical(target, log2(wide))
    half = deep
    line = jnp.where(live, lax.shift_right_logical(line, 1) + (line & 1) * half, -1)
    lane = target & (wide - 1)
    w1 = weight.astype(BF).astype(F32)
    w2 = (weight - w1).astype(BF).astype(F32)
    values = [
        lax.shift_right_logical(cell, 8).astype(F32),
        (cell & 255).astype(F32),
        node_ref[...].astype(F32),
        w1,
        w2,
        weight - w1 - w2,
    ]
    lefts, rights = [], []
    for r in range(deep):
        into = lax.broadcasted_iota(jnp.int32, (2 * half, wide), 0) == line[r : r + 1]
        lefts.append(
            jnp.concatenate([jnp.where(into, v[r : r + 1], 0.0) for v in values], axis=0).astype(BF)
        )
        rights.append(onehot(lane[r : r + 1], wide))
    listed = dot_t(jnp.concatenate(lefts, axis=1), jnp.concatenate(rights, axis=1))
    part = [listed[i * 2 * half : (i + 1) * 2 * half] for i in range(6)]
    lists = [256.0 * part[0] + part[1], part[2], part[3] + part[4] + part[5]]
    for i, x in enumerate(lists):
        at = modes + i * half
        out[at : at + half, 0:wide] = x[:half]
        out[at : at + half, wide : 2 * wide] = x[half:]
    for copy in copies[4:]:
        copy.wait()


class Lists:
    def __init__(self, blk, modes, capacity, width=None):
        self.blk, self.modes = blk, modes
        self.local = blk.shape[1]
        self.lines = (blk.shape[0] - modes) // 3
        self.width = min(width or self.local, capacity)
        self.capacity = capacity
        self.chunks = capacity // self.width

    def row(self, kind, owner, chunk):
        at = owner * self.capacity + chunk * self.width
        line = lax.shift_right_logical(at, log2(self.local))
        x = self.blk[pl.ds(self.modes + kind * self.lines + line, 1), :]
        if self.width < self.local:
            group = lax.shift_right_logical(at, log2(self.width)) & (self.local // self.width - 1)
            got = x[:, : self.width]
            for g in range(1, self.local // self.width):
                got = jnp.where(group == g, x[:, g * self.width : (g + 1) * self.width], got)
            x = got
        return x

    def load(self, owner, chunk):
        cell = self.row(0, owner, chunk).astype(jnp.int32)
        node = self.row(1, owner, chunk).astype(jnp.int32)
        weight = self.row(2, owner, chunk)
        a = lax.shift_right_logical(cell, log2(CY * CZ))
        b = lax.shift_right_logical(cell, log2(CZ)) & (CY - 1)
        return a, b, cell & (CZ - 1), node, weight


def fill(lists, owner, chunk, a_first, a_count, b_first, b_count, inside, lhs, rhs, at, side):
    modes, width = lists.modes, lists.width
    a, b, c, node, weight = lists.load(owner, chunk)
    if inside is not None:
        weight = weight * inside
    aloc, bloc = a - a_first, b - b_first
    valid = (aloc >= 0) & (aloc < a_count) & (bloc >= 0) & (bloc < 2 * b_count)
    pair = jnp.where(valid, aloc * b_count + lax.shift_right_arithmetic(bloc, 1), -1)
    place = (b & 1) * CZ + c
    pieces = []
    for h in range(width // 128):
        idx = node[:, h * 128 : (h + 1) * 128]
        got = None
        for g in range(lists.local // 128):
            part = lanes_from(lists.blk[0:modes, g * 128 : (g + 1) * 128], idx & 127)
            got = part if g == 0 else jnp.where(lax.shift_right_logical(idx, 7) == g, part, got)
        pieces.append(got)
    hi, lo = split(jnp.concatenate(pieces, axis=1) * weight)
    wide = jnp.broadcast_to(pair.astype(F32), (modes, width)).astype(BF)
    zero = jnp.zeros((modes, width), BF)
    for r in range(a_count * b_count):
        mask = wide == jnp.asarray(r, BF)
        lhs[r * modes : (r + 1) * modes, at : at + width] = jnp.where(mask, hi, zero)
        lhs[r * modes : (r + 1) * modes, at + width : at + 2 * width] = jnp.where(mask, lo, zero)
    hot = onehot(place, 2 * CZ)
    rhs[:, at : at + width] = hot
    rhs[:, at + width : at + 2 * width] = hot


def scatter(
    blks, modes, capacity, owner, inside, a_first, a_count, b_first, b_count, out, lhs, rhs, width=None
):
    every = [Lists(blk, modes, capacity, width) for blk in blks]
    width = every[0].width
    spec = (a_first, a_count, b_first, b_count, inside)
    counts = []
    for k, lists in enumerate(every):
        last = jnp.zeros((1, width), jnp.int32)
        for chunk in range(1, lists.chunks):
            a, b, c, node, weight = lists.load(owner, chunk)
            needed = (weight > 0.0) & (a >= a_first) & (a < a_first + a_count)
            last = jnp.where(needed, chunk + 1, last)
        counts.append(last)
        fill(lists, owner, 0, *spec, lhs, rhs, 2 * k * width, None)
    out[...] = dot_t(lhs[...], rhs[...])
    if every[0].chunks == 1:
        return []

    def more(lists):
        def one(chunk, carry):
            fill(lists, owner, chunk, *spec, lhs, rhs, 0, None)
            out[...] += dot_t(lhs[:, 0 : 2 * width], rhs[:, 0 : 2 * width])
            return carry

        return one

    return [(count, more(lists)) for count, lists in zip(counts, every)]


def later_chunks(jobs):
    if not jobs:
        return
    top = None
    for count, _ in jobs:
        most = jnp.max(count, axis=1, keepdims=True)
        top = most if top is None else jnp.maximum(top, most)

    @pl.when(jnp.max(top) > 0)
    def _():
        for last, (count, one) in zip([jnp.max(count) for count, _ in jobs], jobs):
            lax.fori_loop(1, last, one, 0)


def around(sub, groups):
    below = jnp.maximum(sub - 1, 0), jnp.where(sub > 0, 1.0, 0.0)
    above = jnp.minimum(sub + 1, groups - 1), jnp.where(sub < groups - 1, 1.0, 0.0)
    return below, above


def shift_sum(x):
    lane = lax.broadcasted_iota(jnp.int32, x.shape, 1)
    left = jnp.where(lane == 0, 0.0, pltpu.roll(x, 1, 1))
    right = jnp.where(lane == CZ - 1, 0.0, pltpu.roll(x, CZ - 1, 1))
    return x + 0.5 * (left + right)


def plane_sum(src, a, b_range):
    cols = [src(a, b) + 0.5 * (src(a - 1, b) + src(a + 1, b)) for b in b_range]
    return [
        shift_sum(cols[i] + 0.5 * (cols[i - 1] + cols[i + 1])) for i in range(1, len(cols) - 1)
    ]


def second_plane(src, a, lo_in, hi_in):
    out = []
    for i, t in enumerate(plane_sum(src, a, range(CY + 2 * HALO))):
        sec = SEC_U * src(a, i + 1) + SEC_T * t
        if i + 1 < HALO:
            sec = sec * lo_in
        if i + 1 >= CY + HALO:
            sec = sec * hi_in
        out.append(sec)
    return out


def source_reader(modes, mid, below, above, edge=None, corner=None):
    half = HALO // 2

    def src(a, b):
        lanes = slice((b % 2) * CZ, (b % 2 + 1) * CZ)
        outer = -1
        if a < HALO:
            outer = 0
        elif a >= CX + HALO:
            outer, a = 1, a - CX - HALO
        else:
            a = a - HALO
        if b < HALO:
            ref, at = (below if outer < 0 else corner[2 * outer]), a * half + b // 2
        elif b >= CY + HALO:
            ref = above if outer < 0 else corner[2 * outer + 1]
            at = a * half + (b - CY - HALO) // 2
        else:
            ref, at = (mid if outer < 0 else edge[outer]), a * (CY // 2) + (b - HALO) // 2
        return ref[at * modes : (at + 1) * modes, lanes]

    return src


def own_source_kernel(modes, groups, capacity, sub_ref, *refs):
    blks = refs[:groups]
    own, below, above, inner, *scratch = refs[groups + 1 :]
    sub = sub_ref[0]
    (lo_owner, lo_in), (hi_owner, hi_in) = around(sub, groups)
    args = (blks, modes, capacity)
    half = HALO // 2
    jobs = scatter(*args, sub, None, 0, CX, 0, CY // 2, own, *scratch[0:2])
    jobs += scatter(*args, lo_owner, lo_in, 0, CX, CY - HALO, half, below, *scratch[2:4])
    jobs += scatter(*args, hi_owner, hi_in, 0, CX, 0, half, above, *scratch[4:6])
    later_chunks(jobs)
    src = source_reader(modes, own, below, above)
    for a in range(HALO + 1, CX + HALO - 1):
        for b, sec in enumerate(second_plane(src, a, lo_in, hi_in)):
            inner[a - HALO - 1, b] = sec


def fluid_kernel(modes, groups, capacity, sub_ref, *refs):
    blks = refs[:groups]
    low, high, mid, below, above, inner, mdiag, stiff = refs[groups : groups + 8]
    outs = refs[groups + 8 : 2 * groups + 8]
    rest = refs[2 * groups + 8 :]
    edge, corner, outer, press, force = rest[0:2], rest[2:6], rest[6], rest[7], rest[8]
    scratch = rest[9:]
    sub = sub_ref[0]
    local = blks[0].shape[1]
    half = HALO // 2
    (lo_owner, lo_in), (hi_owner, hi_in) = around(sub, groups)
    jobs = []
    for side, both in enumerate((low, high)):
        there = [both.at[k] for k in range(groups)]
        a_first = CX - HALO if side == 0 else 0
        wide = 128 if side == 0 else 256
        args = (there, modes, capacity)
        mem = scratch[6 * side : 6 * side + 6]
        spec = (a_first, HALO)
        jobs += scatter(*args, sub, None, *spec, 0, CY // 2, edge[side], *mem[0:2], wide)
        jobs += scatter(
            *args, lo_owner, lo_in, *spec, CY - HALO, half, corner[2 * side], *mem[2:4], wide
        )
        jobs += scatter(
            *args, hi_owner, hi_in, *spec, 0, half, corner[2 * side + 1], *mem[4:6], wide
        )
    later_chunks(jobs)
    src = source_reader(modes, mid, below, above, edge, corner)
    for i, a in enumerate((1, 2, CX + HALO - 1, CX + HALO)):
        for b, sec in enumerate(second_plane(src, a, lo_in, hi_in)):
            outer[i, b] = sec

    def second(a, b):
        if a < HALO:
            return outer[a, b]
        if a >= CX:
            return outer[a - CX + HALO, b]
        return inner[a - HALO, b]

    for a in range(CX):
        for b, t in enumerate(plane_sum(second, a + 1, range(CY + 2))):
            p = PRE_SRC * src(a + HALO, b + HALO) + PRE_SEC * second(a + 1, b + 1) + PRE_T * t
            hi, lo = split(p)
            at = (a * (CY // 2) + b // 2) * modes
            lanes = (b % 2) * CZ
            press[at : at + modes, lanes : lanes + CZ] = hi
            press[at : at + modes, 2 * CZ + lanes : 3 * CZ + lanes] = lo

    def collect(lists, chunk):
        a, b, c, node, weight = lists.load(sub, chunk)
        hot = onehot((b & 1) * CZ + c, 2 * CZ)
        got = dot(press[...], jnp.concatenate([hot, hot], axis=0))
        pair = a * (CY // 2) + lax.shift_right_logical(b, 1)
        wide = jnp.broadcast_to(pair, (modes, lists.width))
        picked = jnp.zeros((modes, lists.width), F32)
        for r in range(CX * CY // 2):
            picked = jnp.where(wide == r, got[r * modes : (r + 1) * modes], picked)
        hi, lo = split(picked * weight)
        both = dot_t(jnp.concatenate([hi, lo], axis=0), onehot(node, local))
        return both[:modes] + both[modes:]

    every = [Lists(blk, modes, capacity) for blk in blks]
    for k, lists in enumerate(every):
        add = collect(lists, 0)
        force[k] = add + mdiag[...] * blks[0][0:modes, :] if k == 0 else add
        for chunk in range(1, lists.chunks):

            @pl.when(jnp.max(lists.row(2, sub, chunk)) > 0.0)
            def _():
                force[k] += collect(lists, chunk)

    for k in range(groups):
        for w in range(3):
            outs[k][w] = force[(1 - k - w) % groups]
        if k in (1, groups - 1):
            outs[k][3] = stiff[...]


def apply_blocks(window, cols_ref, kb_ref, sub, groups, diag, field):
    rb, nb, bs, _ = kb_ref.shape
    pieces = []
    for q in range(rb):
        parts = []
        for n in range(nb):
            j = cols_ref[q, n]
            where = sub + j // rb - 1
            inside = jnp.where((where >= 0) & (where < groups), 1.0, 0.0)
            parts.append(window[j] * inside)
        pieces.append(
            lax.dot_general(
                jnp.concatenate(parts, axis=1),
                kb_ref[q].reshape(nb * bs, bs),
                (((1,), (0,)), ((), ())),
                precision=lax.Precision.HIGHEST,
                preferred_element_type=F32,
            )
        )
    return diag * field + jnp.concatenate(pieces, axis=1)


def fill_window(win, blocks, bs):
    at = 0
    for blk in blocks:
        for i in range(blk.shape[1] // bs):
            win[at] = blk[:, i * bs : (i + 1) * bs]
            at += 1


def stiff_kernel(modes, groups, sub_ref, cols_ref, prev, own, nxt, diag, kb, out, win):
    bs = kb.shape[2]
    fill_window(win, [prev[0:modes, :], own[0:modes, :], nxt[0:modes, :]], bs)
    out[...] = apply_blocks(win, cols_ref, kb, sub_ref[0], groups, diag[...], own[0:modes, :])


def gram_kernel(modes, groups, sub_ref, cols_ref, pack, *refs):
    parts = refs[:groups]
    stiff, diag, kb, keep, send, mass, win, gram = refs[groups:]
    bs = kb.shape[2]
    fields = []
    for w in range(3):
        m = parts[0][w]
        for part in parts[1:]:
            m = m + part[w]
        fields.append(m)
    own = fields[1]
    mass[...] = own
    s = stiff[...]
    ends = [parts[1][3], s, parts[groups - 1][3]]
    both = [jnp.concatenate([x, y], axis=0) for x, y in zip(ends, fields)]
    fill_window(win, both, bs)
    image = apply_blocks(win, cols_ref, kb, sub_ref[0], groups, diag[...], both[1])
    v = pack[0:modes, :]
    left = jnp.concatenate([v, s, own], axis=0)
    right = jnp.concatenate([s, image, own], axis=0)

    def inner(x, y):
        return lax.dot_general(
            x,
            y,
            (((1,), (1,)), ((), ())),
            precision=lax.Precision.HIGHEST,
            preferred_element_type=F32,
        )

    whole = inner(left, right)
    half = 3 * modes // 2
    gram[0] = whole[:half]
    gram[1] = whole[half:]
    gram[1, 2 * modes - half : 3 * modes - half, 0:modes] = inner(v, v)
    core = sub_ref[1]
    keep[...] = gram[core]
    send[...] = gram[1 - core]


def final_kernel(modes, total, sub_ref, mine, other, stiff, mass, residual, g_stiff, g_plain, gram):
    m = modes
    core = sub_ref[1]
    half = 3 * m // 2
    gram[pl.ds(pl.multiple_of(core * half, half), half), :] = mine[...]
    gram[pl.ds(pl.multiple_of((1 - core) * half, half), half), :] = other[...]
    blocks = [
        [gram[i * m : (i + 1) * m, j * m : (j + 1) * m] for j in range(4)] for i in range(3)
    ]
    (vs, vks, vkm, vm), (ss, sks, skm, sm), (vv, mks, mkm, mm) = blocks
    rows = lax.broadcasted_iota(jnp.int32, (m, m), 0)
    lanes = lax.broadcasted_iota(jnp.int32, (m, m), 1)
    eye = rows == lanes

    def column(x):
        return jnp.sum(jnp.where(eye, x, 0.0), axis=1, keepdims=True)

    def line(x):
        return jnp.sum(jnp.where(eye, x, 0.0), axis=0, keepdims=True)

    tc = column(vs) / column(vm)
    tl = line(vs) / line(vm)
    residual[...] = stiff[...] - tc * mass[...]
    ms = sm.T
    scale = 1.0 / total
    vr = vs - vm * tl
    g_plain[0:m, 0:m] = vv * scale
    g_plain[0:m, m : 2 * m] = vr * scale
    g_plain[m : 2 * m, 0:m] = vr.T * scale
    g_plain[m : 2 * m, m : 2 * m] = (ss - sm * tl - tc * (ms - mm * tl)) * scale
    g_stiff[0:m, 0:m] = vs * scale
    g_stiff[0:m, m : 2 * m] = (vks - vkm * tl) * scale
    g_stiff[m : 2 * m, 0:m] = (ss - tc * ms) * scale
    g_stiff[m : 2 * m, m : 2 * m] = (sks - skm * tl - tc * (mks - mkm * tl)) * scale


def shifted(x, axis, k):
    n = lax.axis_size(axis)
    return lax.ppermute(x, axis, [(i, (i + k) % n) for i in range(n)])


def swapped(x, axis, k):
    n = lax.axis_size(axis)
    return lax.ppermute(x, axis, [(i, i ^ k) for i in range(n)])


def summed(x, axis, bit):
    n = lax.axis_size(axis)
    while (1 << bit) < n:
        if (4 << bit) <= n:
            one, two, three = [swapped(x, axis, k << bit) for k in (1, 2, 3)]
            x = (x + one) + (two + three)
            bit += 2
        else:
            x = x + swapped(x, axis, 1 << bit)
            bit += 1
    return x


def smem():
    return pl.BlockSpec(memory_space=pltpu.SMEM)


def vmem():
    return pl.BlockSpec(memory_space=pltpu.VMEM)


def call(kernel, name, out_shape, scalars, arrays, scratch, flops, mib=4):
    return pl.pallas_call(
        kernel,
        name=name,
        out_shape=out_shape,
        in_specs=[smem()] * len(scalars) + [vmem()] * len(arrays),
        out_specs=jax.tree.map(lambda _: vmem(), out_shape),
        scratch_shapes=scratch,
        compiler_params=pltpu.CompilerParams(vmem_limit_bytes=mib << 20),
        cost_estimate=pl.CostEstimate(flops=flops, transcendentals=0, bytes_accessed=1 << 20),
    )(*scalars, *arrays)


def body(
    block_vectors,
    stiffness,
    mass_diag,
    kblocks,
    block_cols,
    slot_node,
    slot_owner,
    slot_cell,
    slot_weight,
    live_slots,
):
    modes, local = block_vectors.shape
    groups = lax.axis_size("sub")
    slots = slot_node.shape[0]
    bs = kblocks.shape[2]
    total = local * lax.axis_size("passage") * groups
    sub = jnp.stack([lax.axis_index("sub"), lax.axis_index("passage") & 1]).astype(jnp.int32)
    deep, wide = slots // 128, 128
    capacity = 2 * slots // groups
    slotted = [x.reshape(deep, wide) for x in (slot_owner, slot_cell, slot_node, slot_weight)]
    pack, mdiag, diag, cols = pl.pallas_call(
        functools.partial(pack_kernel, modes, groups),
        name="pack",
        out_shape=(
            jax.ShapeDtypeStruct((modes + 3 * deep, local), F32),
            jax.ShapeDtypeStruct((1, local), F32),
            jax.ShapeDtypeStruct((1, local), F32),
            jax.ShapeDtypeStruct(block_cols.shape, jnp.int32),
        ),
        in_specs=[smem()] + [pl.BlockSpec(memory_space=pltpu.MemorySpace.HBM)] * 8,
        out_specs=(vmem(), vmem(), vmem(), vmem()),
        scratch_shapes=[pltpu.VMEM((deep, wide), x.dtype) for x in slotted]
        + [pltpu.SemaphoreType.DMA((8,))],
        compiler_params=pltpu.CompilerParams(vmem_limit_bytes=4 << 20),
        cost_estimate=pl.CostEstimate(flops=1 << 28, transcendentals=0, bytes_accessed=1 << 20),
    )(
        live_slots,
        *[
            pltpu.with_memory_space_constraint(x, pltpu.MemorySpace.HBM)
            for x in (
                *slotted,
                block_vectors,
                mass_diag[None, :],
                stiffness[None, :],
                block_cols,
            )
        ]
    )
    packs = [pack] + [shifted(pack, "sub", k) for k in range(1, groups)]
    both = jnp.stack(packs)
    low = shifted(both, "passage", 1)
    high = shifted(both, "passage", -1)
    window = [packs[1], packs[0], packs[groups - 1]]
    nwin = 3 * local // bs
    stiff = call(
        functools.partial(stiff_kernel, modes, groups),
        "stiff",
        jax.ShapeDtypeStruct((modes, local), F32),
        [sub, cols],
        [*window, diag, kblocks],
        [pltpu.VMEM((nwin, modes, bs), F32)],
        1 << 29,
    )
    pairs = CY // 2
    half = HALO // 2
    width = min(local, capacity)

    def operands(rows, chunk):
        deep = 2 * min(chunk, width) * groups
        return [pltpu.VMEM((rows, deep), BF), pltpu.VMEM((2 * CZ, deep), BF)]

    def field(*shape):
        return jax.ShapeDtypeStruct(shape, F32)

    source = call(
        functools.partial(own_source_kernel, modes, groups, capacity),
        "own_source",
        (
            field(CX * pairs * modes, 2 * CZ),
            field(CX * half * modes, 2 * CZ),
            field(CX * half * modes, 2 * CZ),
            field(CX - 2, CY + 2, modes, CZ),
        ),
        [sub],
        [*packs, stiff],
        operands(CX * pairs * modes, width) + 2 * operands(CX * half * modes, width),
        1 << 32,
        20 if groups <= 4 else 48,
    )
    force = call(
        functools.partial(fluid_kernel, modes, groups, capacity),
        "fluid",
        tuple(field(4 if k in (1, groups - 1) else 3, modes, local) for k in range(groups)),
        [sub],
        [*packs, low, high, *source, mdiag, stiff],
        [
            *[pltpu.VMEM((HALO * pairs * modes, 2 * CZ), F32)] * 2,
            *[pltpu.VMEM((HALO * half * modes, 2 * CZ), F32)] * 4,
            pltpu.VMEM((4, CY + 2, modes, CZ), F32),
            pltpu.VMEM((CX * pairs * modes, 4 * CZ), BF),
            pltpu.VMEM((groups, modes, local), F32),
            *[
                x
                for chunk in (128, 256)
                for x in operands(HALO * pairs * modes, chunk)
                + 2 * operands(HALO * half * modes, chunk)
            ],
        ],
        1 << 32,
        20 if groups <= 4 else 48,
    )
    parts = [force[0]] + [shifted(force[k], "sub", k) for k in range(1, groups)]
    keep, send, mass = call(
        functools.partial(gram_kernel, modes, groups),
        "gram",
        (field(3 * modes // 2, 4 * modes), field(3 * modes // 2, 4 * modes), field(modes, local)),
        [sub, cols],
        [pack, *parts, stiff, diag, kblocks],
        [
            pltpu.VMEM((nwin, 2 * modes, bs), F32),
            pltpu.VMEM((2, 3 * modes // 2, 4 * modes), F32),
        ],
        1 << 29,
    )
    mine = keep + swapped(send, "passage", 1)
    mine = summed(mine, "passage", 1)
    mine = summed(mine, "sub", 0)
    other = swapped(mine, "passage", 1)
    return call(
        functools.partial(final_kernel, modes, float(total)),
        "final",
        (field(modes, local), field(2 * modes, 2 * modes), field(2 * modes, 2 * modes)),
        [sub],
        [mine, other, stiff, mass],
        [pltpu.VMEM((3 * modes, 4 * modes), F32)],
        1 << 20,
    )


def solution(mesh):
    return jax.shard_map(
        body,
        mesh=mesh,
        in_specs=(
            P(None, ("passage", "sub")),
            P(("passage", "sub")),
            P(("passage", "sub")),
            P(("passage", "sub"), None, None, None),
            P(("passage", "sub"), None),
            P(("passage", "sub")),
            P(("passage", "sub"), None),
            P(("passage", "sub")),
            P(("passage", "sub")),
            P(("passage", "sub")),
        ),
        out_specs=(P(None, ("passage", "sub")), P(), P()),
        check_vma=False,
    )
```

```python
import functools
import jax
import jax.numpy as jnp
from jax import lax
from jax.experimental import pallas as pl
from jax.experimental.pallas import tpu as pltpu
from jax.sharding import PartitionSpec as P

CX = 8
CY = 8
CZ = 128
HALO = 2

center_weight = 15.0
lower_bound = 1.0 / 15.0
upper_bound = 17.0 / 15.0
middle = (upper_bound + lower_bound) / 2.0
radius = (upper_bound - lower_bound) / 2.0
sigma_ratio = middle / radius
first_rho = 1.0 / sigma_ratio
second_rho = 1.0 / (2.0 * sigma_ratio - first_rho)
third_rho = 1.0 / (2.0 * sigma_ratio - second_rho)

FIRST = 1.0 / (center_weight * middle)
GAIN2 = 2.0 * second_rho / (radius * center_weight)
SEC_U = FIRST * (1.0 + second_rho * first_rho) + GAIN2 * (1.0 - 17.0 * FIRST)
SEC_T = GAIN2 * 2.0 * FIRST
STEP3 = third_rho * second_rho
GAIN3 = 2.0 * third_rho / (radius * center_weight)
PRE_SRC = GAIN3 - STEP3 * FIRST
PRE_SEC = 1.0 + STEP3 - 17.0 * GAIN3
PRE_T = 2.0 * GAIN3

BF = jnp.bfloat16
F32 = jnp.float32
CELLS = CX * CY * CZ


def log2(n):
    return n.bit_length() - 1


def split(x):
    hi = x.astype(BF)
    return hi, (x - hi.astype(F32)).astype(BF)


def lanes_from(x, index):
    return jnp.take_along_axis(
        x, jnp.broadcast_to(index, x.shape), axis=1, mode="promise_in_bounds"
    )


def onehot(values, height):
    shape = (height, values.shape[1])
    rows = lax.broadcasted_iota(jnp.int32, shape, 0)
    return jnp.where(rows == values, 1.0, 0.0).astype(BF)


def dot_t(x, y):
    return lax.dot_general(x, y, (((1,), (1,)), ((), ())), preferred_element_type=F32)


def dot(x, y):
    return lax.dot_general(x, y, (((1,), (0,)), ((), ())), preferred_element_type=F32)


def pack_kernel(modes, groups, live_ref, *refs):
    sources, (out, mdiag, diag, cols) = refs[:8], refs[8:12]
    owner_ref, cell_ref, node_ref, weight_ref, sems = refs[12:]
    targets = [owner_ref, cell_ref, node_ref, weight_ref]
    targets += [out.at[0:modes, :], mdiag, diag, cols]
    copies = [
        pltpu.make_async_copy(x, y, sems.at[i]) for i, (x, y) in enumerate(zip(sources, targets))
    ]
    for copy in copies:
        copy.start()
    for copy in copies[:4]:
        copy.wait()
    deep, wide = owner_ref.shape
    capacity = 2 * deep * wide // groups
    keys = groups * CX
    owner, cell, weight = owner_ref[...], cell_ref[...], weight_ref[...]
    shape = (deep, wide)
    place = lax.broadcasted_iota(jnp.int32, shape, 0) * wide + lax.broadcasted_iota(
        jnp.int32, shape, 1
    )
    live = place < live_ref[0]
    a = lax.shift_right_logical(cell, log2(CY * CZ))
    key = jnp.where(live, owner * CX + ((a + HALO) & (CX - 1)), -1)
    hots = jnp.concatenate([jnp.where(key == k, 1.0, 0.0) for k in range(keys)], axis=0).astype(BF)
    rows = lax.broadcasted_iota(jnp.int32, (wide, wide), 0)
    lanes = lax.broadcasted_iota(jnp.int32, (wide, wide), 1)
    within = dot(hots, jnp.where(rows <= lanes, 1.0, 0.0).astype(BF))
    size = keys * deep
    rows = lax.broadcasted_iota(jnp.int32, (size, size), 0)
    lanes = lax.broadcasted_iota(jnp.int32, (size, size), 1)
    shift = log2(CX * deep)
    same = lax.shift_right_logical(rows, shift) == lax.shift_right_logical(lanes, shift)
    earlier = jnp.where(same & (lanes < rows), 1.0, 0.0).astype(BF)
    ahead = dot(dot(earlier, hots).astype(BF), jnp.ones((wide, wide), BF))
    order = within + ahead - 1.0
    pos = jnp.zeros(shape, F32)
    for k in range(keys):
        pos = jnp.where(key == k, order[k * deep : (k + 1) * deep], pos)
    target = owner * capacity + pos.astype(jnp.int32)
    line = lax.shift_right_logical(target, log2(wide))
    half = deep
    line = jnp.where(live, lax.shift_right_logical(line, 1) + (line & 1) * half, -1)
    lane = target & (wide - 1)
    w1 = weight.astype(BF).astype(F32)
    w2 = (weight - w1).astype(BF).astype(F32)
    values = [
        lax.shift_right_logical(cell, 8).astype(F32),
        (cell & 255).astype(F32),
        node_ref[...].astype(F32),
        w1,
        w2,
        weight - w1 - w2,
    ]
    lefts, rights = [], []
    for r in range(deep):
        into = lax.broadcasted_iota(jnp.int32, (2 * half, wide), 0) == line[r : r + 1]
        lefts.append(
            jnp.concatenate([jnp.where(into, v[r : r + 1], 0.0) for v in values], axis=0).astype(BF)
        )
        rights.append(onehot(lane[r : r + 1], wide))
    listed = dot_t(jnp.concatenate(lefts, axis=1), jnp.concatenate(rights, axis=1))
    part = [listed[i * 2 * half : (i + 1) * 2 * half] for i in range(6)]
    lists = [256.0 * part[0] + part[1], part[2], part[3] + part[4] + part[5]]
    for i, x in enumerate(lists):
        at = modes + i * half
        out[at : at + half, 0:wide] = x[:half]
        out[at : at + half, wide : 2 * wide] = x[half:]
    for copy in copies[4:]:
        copy.wait()


class Lists:
    def __init__(self, blk, modes, capacity, width=None):
        self.blk, self.modes = blk, modes
        self.local = blk.shape[1]
        self.lines = (blk.shape[0] - modes) // 3
        self.width = min(width or self.local, capacity)
        self.capacity = capacity
        self.chunks = capacity // self.width

    def row(self, kind, owner, chunk):
        at = owner * self.capacity + chunk * self.width
        line = at // self.local if isinstance(at, int) else lax.shift_right_logical(at, log2(self.local))
        x = self.blk[pl.ds(self.modes + kind * self.lines + line, 1), :]
        if self.width < self.local:
            if isinstance(at, int):
                first = at % self.local
                return x[:, first : first + self.width]
            group = lax.shift_right_logical(at, log2(self.width)) & (self.local // self.width - 1)
            got = x[:, : self.width]
            for g in range(1, self.local // self.width):
                got = jnp.where(group == g, x[:, g * self.width : (g + 1) * self.width], got)
            x = got
        return x

    def load(self, owner, chunk):
        cell = self.row(0, owner, chunk).astype(jnp.int32)
        node = self.row(1, owner, chunk).astype(jnp.int32)
        weight = self.row(2, owner, chunk)
        a = lax.shift_right_logical(cell, log2(CY * CZ))
        b = lax.shift_right_logical(cell, log2(CZ)) & (CY - 1)
        return a, b, cell & (CZ - 1), node, weight


def each(n, step):
    if n <= 4:
        for i in range(n):
            step(i)
        return

    def one(i, carry):
        step(i)
        return carry

    lax.fori_loop(0, n, one, 0)


def fill(lists, owner, chunk, a_first, a_count, lhs, rhs, at):
    modes, width = lists.modes, lists.width
    a, b, c, node, weight = lists.load(owner, chunk)
    aloc = a - a_first
    valid = (aloc >= 0) & (aloc < a_count)
    pair = jnp.where(valid, lax.shift_right_logical(b, 1) * a_count + aloc, -16)
    pieces = []
    for h in range(width // 128):
        idx = node[:, h * 128 : (h + 1) * 128]
        got = None
        for g in range(lists.local // 128):
            part = lanes_from(lists.blk[0:modes, g * 128 : (g + 1) * 128], idx & 127)
            got = part if g == 0 else jnp.where(lax.shift_right_logical(idx, 7) == g, part, got)
        pieces.append(got)
    vals = jnp.concatenate(pieces, axis=1) * weight
    times = max(1, 16 // modes)
    tall = times * modes
    hi, lo = split(jnp.concatenate([vals] * times, axis=0))
    step = lax.shift_right_logical(
        lax.broadcasted_iota(jnp.int32, (tall, width), 0), log2(modes)
    )
    wide = (pair - step).astype(F32).astype(BF)
    zero = jnp.zeros((tall, width), BF)
    first, then = pl.ds(at, width), pl.ds(at + width, width)
    for r in range(0, a_count * CY // 2, times):
        mask = wide == jnp.asarray(r, BF)
        lhs[r * modes : r * modes + tall, first] = jnp.where(mask, hi, zero)
        lhs[r * modes : r * modes + tall, then] = jnp.where(mask, lo, zero)
    hot = onehot((b & 1) * CZ + c, 2 * CZ)
    rhs[:, first] = hot
    rhs[:, then] = hot


def scatter(both, modes, capacity, owner, a_first, a_count, out, lhs, rhs, width=None):
    groups = both.shape[0]

    def lists_of(k):
        return Lists(both.at[k], modes, capacity, width)

    some = lists_of(0)
    wide = some.width

    def first(k):
        at = 2 * k * wide
        at = at if isinstance(k, int) else pl.multiple_of(at, 128)
        fill(lists_of(k), owner, 0, a_first, a_count, lhs, rhs, at)

    each(groups, first)
    out[...] = dot_t(lhs[...], rhs[...])
    jobs = []
    if some.chunks == 1:
        return jobs
    for k in range(groups):
        lists = lists_of(k)
        last = jnp.zeros((1, wide), jnp.int32)
        for chunk in range(1, lists.chunks):
            a, b, c, node, weight = lists.load(owner, chunk)
            needed = (weight > 0.0) & (a >= a_first) & (a < a_first + a_count)
            last = jnp.where(needed, chunk + 1, last)

        def one(chunk, carry, lists=lists):
            fill(lists, owner, chunk, a_first, a_count, lhs, rhs, 0)
            out[...] += dot_t(lhs[:, 0 : 2 * wide], rhs[:, 0 : 2 * wide])
            return carry

        jobs.append((last, one))
    return jobs


def later_chunks(jobs):
    if not jobs:
        return
    top = None
    for count, _ in jobs:
        most = jnp.max(count, axis=1, keepdims=True)
        top = most if top is None else jnp.maximum(top, most)

    @pl.when(jnp.max(top) > 0)
    def _():
        for last, (count, one) in zip([jnp.max(count) for count, _ in jobs], jobs):
            lax.fori_loop(1, last, one, 0)


def shift_sum(x):
    lane = lax.broadcasted_iota(jnp.int32, x.shape, 1)
    left = jnp.where(lane == 0, 0.0, pltpu.roll(x, 1, 1))
    right = jnp.where(lane == CZ - 1, 0.0, pltpu.roll(x, CZ - 1, 1))
    return x + 0.5 * (left + right)


def plane_sum(src, a, count):
    cols = [src(a, b) + 0.5 * (src(a - 1, b) + src(a + 1, b)) for b in range(count)]
    out = []
    for b in range(count):
        beside = [cols[i] for i in (b - 1, b + 1) if 0 <= i < count]
        total = beside[0] if len(beside) == 1 else beside[0] + beside[1]
        out.append(shift_sum(cols[b] + 0.5 * total))
    return out


def second_plane(src, a, count):
    return [SEC_U * src(a, b) + SEC_T * t for b, t in enumerate(plane_sum(src, a, count))]


def source_reader(modes, mid, edge=None):
    def src(a, b):
        lanes = slice((b % 2) * CZ, (b % 2 + 1) * CZ)
        owner, pair = b // CY, b % CY // 2
        if a < HALO:
            ref, at = edge[0], pair * HALO + a
        elif a >= CX + HALO:
            ref, at = edge[1], pair * HALO + a - CX - HALO
        else:
            ref, at = mid, pair * CX + a - HALO
        return ref[owner, at * modes : (at + 1) * modes, lanes]

    return src


def own_source_kernel(modes, groups, capacity, both, _, own, inner, *scratch):
    jobs = []

    def one(o):
        at = 2 * o if isinstance(o, int) else 0
        mem = scratch[at : at + 2]
        jobs.extend(scatter(both, modes, capacity, o, 0, CX, own.at[o], *mem))

    each(groups, one)
    later_chunks(jobs)
    src = source_reader(modes, own)
    for a in range(HALO + 1, CX + HALO - 1):
        for b, sec in enumerate(second_plane(src, a, groups * CY)):
            inner[a - HALO - 1, b] = sec


def fluid_kernel(modes, groups, capacity, both, low, high, mid, inner, mdiag, stiff, *refs):
    outs = refs[:groups]
    edge, outer, press, force, scratch = (
        refs[groups : groups + 2],
        *refs[groups + 2 : groups + 5],
        refs[groups + 5 :],
    )
    local = both.shape[2]
    count = groups * CY
    jobs = []
    for side, there in enumerate((low, high)):
        a_first = CX - HALO if side == 0 else 0
        wide = 128 if side == 0 else 256
        half = len(scratch) // 2
        sets = scratch[side * half : (side + 1) * half]

        def one(o, there=there, a_first=a_first, wide=wide, sets=sets, side=side):
            at = 2 * o if isinstance(o, int) else 0
            mem = sets[at : at + 2]
            target = edge[side].at[o]
            jobs.extend(scatter(there, modes, capacity, o, a_first, HALO, target, *mem, wide))

        each(groups, one)
    later_chunks(jobs)
    src = source_reader(modes, mid, edge)
    for i, a in enumerate((1, 2, CX + HALO - 1, CX + HALO)):
        for b, sec in enumerate(second_plane(src, a, count)):
            outer[i, b] = sec

    def second(a, b):
        if a < HALO:
            return outer[a, b]
        if a >= CX:
            return outer[a - CX + HALO, b]
        return inner[a - HALO, b]

    for a in range(0, CX, 2):
        two = [plane_sum(second, a + 1, count), plane_sum(second, a + 2, count)]
        for b in range(count):
            p = jnp.concatenate(
                [
                    PRE_SRC * src(a + i + HALO, b) + PRE_SEC * second(a + i + 1, b) + PRE_T * two[i][b]
                    for i in range(2)
                ],
                axis=0,
            )
            hi, lo = split(p)
            owner, at = b // CY, (b % CY // 2 * CX + a) * modes
            lanes = (b % 2) * CZ
            press[owner, at : at + 2 * modes, lanes : lanes + CZ] = hi
            press[owner, at : at + 2 * modes, 2 * CZ + lanes : 3 * CZ + lanes] = lo

    def collect(k, owner, chunk):
        lists = Lists(both.at[k], modes, capacity)
        a, b, c, node, weight = lists.load(owner, chunk)
        hot = onehot((b & 1) * CZ + c, 2 * CZ)
        got = dot(press[owner], jnp.concatenate([hot, hot], axis=0))
        pair = jnp.broadcast_to(
            lax.shift_right_logical(b, 1) * CX + a, (modes, lists.width)
        )
        picked = jnp.zeros((modes, lists.width), F32)
        for r in range(CX * CY // 2):
            picked = jnp.where(pair == r, got[r * modes : (r + 1) * modes], picked)
        hi, lo = split(picked * weight)
        sums = dot_t(jnp.concatenate([hi, lo], axis=0), onehot(node, local))
        return sums[:modes] + sums[modes:]

    if groups <= 4:
        for k in range(groups):
            total = collect(k, 0, 0)
            for o in range(1, groups):
                total = total + collect(k, o, 0)
            force[k] = total
    else:

        def per_device(k):
            force[k] = jnp.zeros((modes, local), F32)

            def per_owner(o):
                force[k] = force[k] + collect(k, o, 0)

            each(groups, per_owner)

        each(groups, per_device)
    chunks = Lists(both.at[0], modes, capacity).chunks
    if chunks > 1:
        later = [(k, o, c) for k in range(groups) for o in range(groups) for c in range(1, chunks)]
        tops = [
            jnp.max(Lists(both.at[k], modes, capacity).row(2, o, c)) for k, o, c in later
        ]
        for (k, o, c), top in zip(later, tops):

            @pl.when(top > 0.0)
            def _():
                force[k] = force[k] + collect(k, o, c)

    for k in range(groups):
        for w in range(3):
            outs[k][w * modes : (w + 1) * modes, :] = force[(1 - k - w) % groups]
        if k in (1, groups - 1):
            at = 3 * modes
            outs[k][at : at + 8, :] = jnp.broadcast_to(mdiag[...], (8, local))
            outs[k][at + 8 :, :] = stiff[...]


def apply_blocks(window, cols_ref, kb_ref, sub, groups, diag, field):
    rb, nb, bs, _ = kb_ref.shape
    pieces = []
    for q in range(rb):
        parts = []
        for n in range(nb):
            j = cols_ref[q, n]
            where = sub + j // rb - 1
            inside = jnp.where((where >= 0) & (where < groups), 1.0, 0.0)
            parts.append(window[j] * inside)
        pieces.append(
            lax.dot_general(
                jnp.concatenate(parts, axis=1),
                kb_ref[q].reshape(nb * bs, bs),
                (((1,), (0,)), ((), ())),
                precision=lax.Precision.HIGHEST,
                preferred_element_type=F32,
            )
        )
    return diag * field + jnp.concatenate(pieces, axis=1)


def fill_window(win, blocks, bs):
    at = 0
    for blk in blocks:
        for i in range(blk.shape[1] // bs):
            win[at] = blk[:, i * bs : (i + 1) * bs]
            at += 1


def stiff_kernel(modes, groups, sub_ref, cols_ref, prev, own, nxt, diag, kb, out, win):
    bs = kb.shape[2]
    fill_window(win, [prev[0:modes, :], own[0:modes, :], nxt[0:modes, :]], bs)
    out[...] = apply_blocks(win, cols_ref, kb, sub_ref[0], groups, diag[...], own[0:modes, :])


def first_mode(modes, groups, count, sub):
    return pl.multiple_of(lax.shift_right_logical(sub * (modes // groups), log2(count)) * count, count)


def gram_kernel(modes, groups, count, sub_ref, cols_ref, prev, pack, nxt, mdiag, *refs):
    parts = refs[:groups]
    stiff, diag, kb, keep, send, mass, win, gram, force = refs[groups:]
    bs = kb.shape[2]
    for k in range(groups):
        source = lax.rem(sub_ref[0] + groups - k, groups)
        at = first_mode(modes, groups, count, source)
        for w in range(3):
            force[w, pl.ds(at, count), :] = parts[k][w * count : (w + 1) * count, :]
    at = 3 * count
    before, after = parts[1], parts[groups - 1]
    fields = [
        force[0] + before[at : at + 1, :] * prev[0:modes, :],
        force[1] + mdiag[...] * pack[0:modes, :],
        force[2] + after[at : at + 1, :] * nxt[0:modes, :],
    ]
    own = fields[1]
    mass[...] = own
    s = stiff[...]
    ends = [before[at + 8 :, :], s, after[at + 8 :, :]]
    both = [jnp.concatenate([x, y], axis=0) for x, y in zip(ends, fields)]
    fill_window(win, both, bs)
    image = apply_blocks(win, cols_ref, kb, sub_ref[0], groups, diag[...], both[1])
    v = pack[0:modes, :]
    left = jnp.concatenate([v, s, own], axis=0)
    right = jnp.concatenate([s, image, own], axis=0)

    def inner(x, y):
        return lax.dot_general(
            x,
            y,
            (((1,), (1,)), ((), ())),
            precision=lax.Precision.HIGHEST,
            preferred_element_type=F32,
        )

    whole = inner(left, right)
    half = 3 * modes // 2
    gram[0] = whole[:half]
    gram[1] = whole[half:]
    gram[1, 2 * modes - half : 3 * modes - half, 0:modes] = inner(v, v)
    core = sub_ref[1]
    keep[...] = gram[core]
    send[...] = gram[1 - core]


def final_kernel(modes, total, sub_ref, mine, other, stiff, mass, residual, g_stiff, g_plain, gram):
    m = modes
    core = sub_ref[1]
    half = 3 * m // 2
    gram[pl.ds(pl.multiple_of(core * half, half), half), :] = mine[...]
    gram[pl.ds(pl.multiple_of((1 - core) * half, half), half), :] = other[...]
    blocks = [
        [gram[i * m : (i + 1) * m, j * m : (j + 1) * m] for j in range(4)] for i in range(3)
    ]
    (vs, vks, vkm, vm), (ss, sks, skm, sm), (vv, mks, mkm, mm) = blocks
    rows = lax.broadcasted_iota(jnp.int32, (m, m), 0)
    lanes = lax.broadcasted_iota(jnp.int32, (m, m), 1)
    eye = rows == lanes

    def column(x):
        return jnp.sum(jnp.where(eye, x, 0.0), axis=1, keepdims=True)

    def line(x):
        return jnp.sum(jnp.where(eye, x, 0.0), axis=0, keepdims=True)

    tc = column(vs) / column(vm)
    tl = line(vs) / line(vm)
    residual[...] = stiff[...] - tc * mass[...]
    ms = sm.T
    scale = 1.0 / total
    vr = vs - vm * tl
    g_plain[0:m, 0:m] = vv * scale
    g_plain[0:m, m : 2 * m] = vr * scale
    g_plain[m : 2 * m, 0:m] = vr.T * scale
    g_plain[m : 2 * m, m : 2 * m] = (ss - sm * tl - tc * (ms - mm * tl)) * scale
    g_stiff[0:m, 0:m] = vs * scale
    g_stiff[0:m, m : 2 * m] = (vks - vkm * tl) * scale
    g_stiff[m : 2 * m, 0:m] = (ss - tc * ms) * scale
    g_stiff[m : 2 * m, m : 2 * m] = (sks - skm * tl - tc * (mks - mkm * tl)) * scale


def shifted(x, axis, k):
    n = lax.axis_size(axis)
    return lax.ppermute(x, axis, [(i, (i + k) % n) for i in range(n)])


def swapped(x, axis, k):
    n = lax.axis_size(axis)
    return lax.ppermute(x, axis, [(i, i ^ k) for i in range(n)])


def summed(x, axis, bit):
    n = lax.axis_size(axis)
    while (1 << bit) < n:
        if (4 << bit) <= n:
            one, two, three = [swapped(x, axis, k << bit) for k in (1, 2, 3)]
            x = (x + one) + (two + three)
            bit += 2
        else:
            x = x + swapped(x, axis, 1 << bit)
            bit += 1
    return x


def smem():
    return pl.BlockSpec(memory_space=pltpu.SMEM)


def vmem():
    return pl.BlockSpec(memory_space=pltpu.VMEM)


def call(kernel, name, out_shape, scalars, arrays, scratch, flops, mib=4):
    return pl.pallas_call(
        kernel,
        name=name,
        out_shape=out_shape,
        in_specs=[smem()] * len(scalars) + [vmem()] * len(arrays),
        out_specs=jax.tree.map(lambda _: vmem(), out_shape),
        scratch_shapes=scratch,
        compiler_params=pltpu.CompilerParams(vmem_limit_bytes=mib << 20),
        cost_estimate=pl.CostEstimate(flops=flops, transcendentals=0, bytes_accessed=1 << 20),
    )(*scalars, *arrays)


def body(
    block_vectors,
    stiffness,
    mass_diag,
    kblocks,
    block_cols,
    slot_node,
    slot_owner,
    slot_cell,
    slot_weight,
    live_slots,
):
    modes, local = block_vectors.shape
    groups = lax.axis_size("sub")
    slots = slot_node.shape[0]
    bs = kblocks.shape[2]
    total = local * lax.axis_size("passage") * groups
    sub = jnp.stack([lax.axis_index("sub"), lax.axis_index("passage") & 1]).astype(jnp.int32)
    deep, wide = slots // 128, 128
    capacity = 2 * slots // groups
    slotted = [x.reshape(deep, wide) for x in (slot_owner, slot_cell, slot_node, slot_weight)]
    pack, mdiag, diag, cols = pl.pallas_call(
        functools.partial(pack_kernel, modes, groups),
        name="pack",
        out_shape=(
            jax.ShapeDtypeStruct((modes + 3 * deep, local), F32),
            jax.ShapeDtypeStruct((1, local), F32),
            jax.ShapeDtypeStruct((1, local), F32),
            jax.ShapeDtypeStruct(block_cols.shape, jnp.int32),
        ),
        in_specs=[smem()] + [pl.BlockSpec(memory_space=pltpu.MemorySpace.HBM)] * 8,
        out_specs=(vmem(), vmem(), vmem(), vmem()),
        scratch_shapes=[pltpu.VMEM((deep, wide), x.dtype) for x in slotted]
        + [pltpu.SemaphoreType.DMA((8,))],
        compiler_params=pltpu.CompilerParams(vmem_limit_bytes=4 << 20),
        cost_estimate=pl.CostEstimate(flops=1 << 28, transcendentals=0, bytes_accessed=1 << 20),
    )(
        live_slots,
        *[
            pltpu.with_memory_space_constraint(x, pltpu.MemorySpace.HBM)
            for x in (
                *slotted,
                block_vectors,
                mass_diag[None, :],
                stiffness[None, :],
                block_cols,
            )
        ]
    )
    packs = [pack] + [shifted(pack, "sub", k) for k in range(1, groups)]
    mine = max(8, modes // groups)
    start = first_mode(modes, groups, mine, lax.axis_index("sub").astype(jnp.int32))
    both = jnp.stack(
        [
            jnp.concatenate([lax.dynamic_slice_in_dim(x, start, mine), x[modes:]], axis=0)
            for x in packs
        ]
    )
    low = shifted(both, "passage", 1)
    high = shifted(both, "passage", -1)
    window = [packs[1], packs[0], packs[groups - 1]]
    nwin = 3 * local // bs
    stiff = call(
        functools.partial(stiff_kernel, modes, groups),
        "stiff",
        jax.ShapeDtypeStruct((modes, local), F32),
        [sub, cols],
        [*window, diag, kblocks],
        [pltpu.VMEM((nwin, modes, bs), F32)],
        1 << 29,
    )
    width = min(local, capacity)
    sets = groups if groups <= 4 else 1

    def field(*shape):
        return jax.ShapeDtypeStruct(shape, F32)

    def operands(rows, chunk):
        deep = 2 * min(chunk, width) * groups
        return sets * [pltpu.VMEM((rows, deep), BF), pltpu.VMEM((2 * CZ, deep), BF)]

    rows = CX * CY // 2 * mine
    edge_rows = HALO * CY // 2 * mine
    mib = 20 if groups <= 4 else 36
    source, inner = call(
        functools.partial(own_source_kernel, mine, groups, capacity),
        "own_source",
        (field(groups, rows, 2 * CZ), field(CX - 2, groups * CY, mine, CZ)),
        [],
        [both, stiff],
        operands(rows, width),
        1 << 32,
        mib,
    )
    force = call(
        functools.partial(fluid_kernel, mine, groups, capacity),
        "fluid",
        tuple(
            field(3 * mine + (8 + modes if k in (1, groups - 1) else 0), local)
            for k in range(groups)
        ),
        [],
        [both, low, high, source, inner, mdiag, stiff],
        [
            *[pltpu.VMEM((groups, edge_rows, 2 * CZ), F32)] * 2,
            pltpu.VMEM((4, groups * CY, mine, CZ), F32),
            pltpu.VMEM((groups, rows, 4 * CZ), BF),
            pltpu.VMEM((groups, mine, local), F32),
            *operands(edge_rows, 128),
            *operands(edge_rows, 256),
        ],
        1 << 32,
        mib,
    )
    parts = [force[0]] + [shifted(force[k], "sub", k) for k in range(1, groups)]
    keep, send, mass = call(
        functools.partial(gram_kernel, modes, groups, mine),
        "gram",
        (field(3 * modes // 2, 4 * modes), field(3 * modes // 2, 4 * modes), field(modes, local)),
        [sub, cols],
        [*window, mdiag, *parts, stiff, diag, kblocks],
        [
            pltpu.VMEM((nwin, 2 * modes, bs), F32),
            pltpu.VMEM((2, 3 * modes // 2, 4 * modes), F32),
            pltpu.VMEM((3, modes, local), F32),
        ],
        1 << 29,
    )
    mine = keep + swapped(send, "passage", 1)
    mine = summed(mine, "passage", 1)
    mine = summed(mine, "sub", 0)
    other = swapped(mine, "passage", 1)
    return call(
        functools.partial(final_kernel, modes, float(total)),
        "final",
        (field(modes, local), field(2 * modes, 2 * modes), field(2 * modes, 2 * modes)),
        [sub],
        [mine, other, stiff, mass],
        [pltpu.VMEM((3 * modes, 4 * modes), F32)],
        1 << 20,
    )


def solution(mesh):
    return jax.shard_map(
        body,
        mesh=mesh,
        in_specs=(
            P(None, ("passage", "sub")),
            P(("passage", "sub")),
            P(("passage", "sub")),
            P(("passage", "sub"), None, None, None),
            P(("passage", "sub"), None),
            P(("passage", "sub")),
            P(("passage", "sub"), None),
            P(("passage", "sub")),
            P(("passage", "sub")),
            P(("passage", "sub")),
        ),
        out_specs=(P(None, ("passage", "sub")), P(), P()),
        check_vma=False,
    )
```

```python
import functools
import jax
import jax.numpy as jnp
from jax import lax
from jax.experimental import pallas as pl
from jax.experimental.pallas import tpu as pltpu
from jax.sharding import PartitionSpec as P

CX = 8
CY = 8
CZ = 128
HALO = 2

center_weight = 15.0
lower_bound = 1.0 / 15.0
upper_bound = 17.0 / 15.0
middle = (upper_bound + lower_bound) / 2.0
radius = (upper_bound - lower_bound) / 2.0
sigma_ratio = middle / radius
first_rho = 1.0 / sigma_ratio
second_rho = 1.0 / (2.0 * sigma_ratio - first_rho)
third_rho = 1.0 / (2.0 * sigma_ratio - second_rho)

FIRST = 1.0 / (center_weight * middle)
GAIN2 = 2.0 * second_rho / (radius * center_weight)
SEC_U = FIRST * (1.0 + second_rho * first_rho) + GAIN2 * (1.0 - 17.0 * FIRST)
SEC_T = GAIN2 * 2.0 * FIRST
STEP3 = third_rho * second_rho
GAIN3 = 2.0 * third_rho / (radius * center_weight)
PRE_SRC = GAIN3 - STEP3 * FIRST
PRE_SEC = 1.0 + STEP3 - 17.0 * GAIN3
PRE_T = 2.0 * GAIN3

BF = jnp.bfloat16
F32 = jnp.float32
CELLS = CX * CY * CZ


def log2(n):
    return n.bit_length() - 1


def split(x):
    hi = x.astype(BF)
    return hi, (x - hi.astype(F32)).astype(BF)


def lanes_from(x, index):
    return jnp.take_along_axis(
        x, jnp.broadcast_to(index, x.shape), axis=1, mode="promise_in_bounds"
    )


def onehot(values, height):
    shape = (height, values.shape[1])
    rows = lax.broadcasted_iota(jnp.int32, shape, 0)
    return jnp.where(rows == values, 1.0, 0.0).astype(BF)


def dot_t(x, y):
    return lax.dot_general(x, y, (((1,), (1,)), ((), ())), preferred_element_type=F32)


def dot(x, y):
    return lax.dot_general(x, y, (((1,), (0,)), ((), ())), preferred_element_type=F32)


def pack_kernel(modes, groups, live_ref, *refs):
    sources, (out, mdiag, diag, cols) = refs[:8], refs[8:12]
    owner_ref, cell_ref, node_ref, weight_ref, sems = refs[12:]
    targets = [owner_ref, cell_ref, node_ref, weight_ref]
    targets += [out.at[0:modes, :], mdiag, diag, cols]
    copies = [
        pltpu.make_async_copy(x, y, sems.at[i]) for i, (x, y) in enumerate(zip(sources, targets))
    ]
    for copy in copies:
        copy.start()
    for copy in copies[:4]:
        copy.wait()
    deep, wide = owner_ref.shape
    capacity = 2 * deep * wide // groups
    keys = groups * CX
    owner, cell, weight = owner_ref[...], cell_ref[...], weight_ref[...]
    shape = (deep, wide)
    place = lax.broadcasted_iota(jnp.int32, shape, 0) * wide + lax.broadcasted_iota(
        jnp.int32, shape, 1
    )
    live = place < live_ref[0]
    a = lax.shift_right_logical(cell, log2(CY * CZ))
    key = jnp.where(live, owner * CX + ((a + HALO) & (CX - 1)), -1)
    hots = jnp.concatenate([jnp.where(key == k, 1.0, 0.0) for k in range(keys)], axis=0).astype(BF)
    rows = lax.broadcasted_iota(jnp.int32, (wide, wide), 0)
    lanes = lax.broadcasted_iota(jnp.int32, (wide, wide), 1)
    within = dot(hots, jnp.where(rows <= lanes, 1.0, 0.0).astype(BF))
    size = keys * deep
    rows = lax.broadcasted_iota(jnp.int32, (size, size), 0)
    lanes = lax.broadcasted_iota(jnp.int32, (size, size), 1)
    shift = log2(CX * deep)
    same = lax.shift_right_logical(rows, shift) == lax.shift_right_logical(lanes, shift)
    earlier = jnp.where(same & (lanes < rows), 1.0, 0.0).astype(BF)
    ahead = dot(dot(earlier, hots).astype(BF), jnp.ones((wide, wide), BF))
    order = within + ahead - 1.0
    pos = jnp.zeros(shape, F32)
    for k in range(keys):
        pos = jnp.where(key == k, order[k * deep : (k + 1) * deep], pos)
    target = owner * capacity + pos.astype(jnp.int32)
    line = lax.shift_right_logical(target, log2(wide))
    half = deep
    line = jnp.where(live, lax.shift_right_logical(line, 1) + (line & 1) * half, -1)
    lane = target & (wide - 1)
    w1 = weight.astype(BF).astype(F32)
    w2 = (weight - w1).astype(BF).astype(F32)
    values = [
        lax.shift_right_logical(cell, 8).astype(F32),
        (cell & 255).astype(F32),
        node_ref[...].astype(F32),
        w1,
        w2,
        weight - w1 - w2,
    ]
    lefts, rights = [], []
    for r in range(deep):
        into = lax.broadcasted_iota(jnp.int32, (2 * half, wide), 0) == line[r : r + 1]
        lefts.append(
            jnp.concatenate([jnp.where(into, v[r : r + 1], 0.0) for v in values], axis=0).astype(BF)
        )
        rights.append(onehot(lane[r : r + 1], wide))
    listed = dot_t(jnp.concatenate(lefts, axis=1), jnp.concatenate(rights, axis=1))
    part = [listed[i * 2 * half : (i + 1) * 2 * half] for i in range(6)]
    lists = [256.0 * part[0] + part[1], part[2], part[3] + part[4] + part[5]]
    for i, x in enumerate(lists):
        at = modes + i * half
        out[at : at + half, 0:wide] = x[:half]
        out[at : at + half, wide : 2 * wide] = x[half:]
    for copy in copies[4:]:
        copy.wait()


class Lists:
    def __init__(self, blk, modes, capacity, width=None):
        self.blk, self.modes = blk, modes
        self.local = blk.shape[1]
        self.lines = (blk.shape[0] - modes) // 3
        self.width = min(width or self.local, capacity)
        self.capacity = capacity
        self.chunks = capacity // self.width

    def row(self, kind, owner, chunk):
        at = owner * self.capacity + chunk * self.width
        line = at // self.local if isinstance(at, int) else lax.shift_right_logical(at, log2(self.local))
        x = self.blk[pl.ds(self.modes + kind * self.lines + line, 1), :]
        if self.width < self.local:
            if isinstance(at, int):
                first = at % self.local
                return x[:, first : first + self.width]
            group = lax.shift_right_logical(at, log2(self.width)) & (self.local // self.width - 1)
            got = x[:, : self.width]
            for g in range(1, self.local // self.width):
                got = jnp.where(group == g, x[:, g * self.width : (g + 1) * self.width], got)
            x = got
        return x

    def load(self, owner, chunk):
        cell = self.row(0, owner, chunk).astype(jnp.int32)
        node = self.row(1, owner, chunk).astype(jnp.int32)
        weight = self.row(2, owner, chunk)
        a = lax.shift_right_logical(cell, log2(CY * CZ))
        b = lax.shift_right_logical(cell, log2(CZ)) & (CY - 1)
        return a, b, cell & (CZ - 1), node, weight


def each(n, step):
    if n <= 4:
        for i in range(n):
            step(i)
        return

    def one(i, carry):
        step(i)
        return carry

    lax.fori_loop(0, n, one, 0)


def fill(lists, owner, chunk, a_first, a_count, lhs, rhs, at):
    modes, width = lists.modes, lists.width
    a, b, c, node, weight = lists.load(owner, chunk)
    aloc = a - a_first
    valid = (aloc >= 0) & (aloc < a_count)
    pair = jnp.where(valid, lax.shift_right_logical(b, 1) * a_count + aloc, -16)
    pieces = []
    for h in range(width // 128):
        idx = node[:, h * 128 : (h + 1) * 128]
        got = None
        for g in range(lists.local // 128):
            part = lanes_from(lists.blk[0:modes, g * 128 : (g + 1) * 128], idx & 127)
            got = part if g == 0 else jnp.where(lax.shift_right_logical(idx, 7) == g, part, got)
        pieces.append(got)
    vals = jnp.concatenate(pieces, axis=1) * weight
    times = max(1, 16 // modes)
    tall = times * modes
    hi, lo = split(jnp.concatenate([vals] * times, axis=0))
    step = lax.shift_right_logical(
        lax.broadcasted_iota(jnp.int32, (tall, width), 0), log2(modes)
    )
    wide = (pair - step).astype(F32).astype(BF)
    zero = jnp.zeros((tall, width), BF)
    lanes = pl.ds(at, width)
    half = a_count * CY // 2 * modes
    for r in range(0, a_count * CY // 2, times):
        mask = wide == jnp.asarray(r, BF)
        row = r * modes
        lhs[row : row + tall, lanes] = jnp.where(mask, hi, zero)
        lhs[half + row : half + row + tall, lanes] = jnp.where(mask, lo, zero)
    rhs[:, lanes] = onehot((b & 1) * CZ + c, 2 * CZ)


def scatter(both, modes, capacity, owner, a_first, a_count, out, lhs, rhs, width=None):
    groups = both.shape[0]

    def lists_of(k):
        return Lists(both.at[k], modes, capacity, width)

    some = lists_of(0)
    wide = some.width

    def first(k):
        at = k * wide
        at = at if isinstance(k, int) else pl.multiple_of(at, 128)
        fill(lists_of(k), owner, 0, a_first, a_count, lhs, rhs, at)

    def product(lanes):
        got = dot_t(lhs[:, 0:lanes], rhs[:, 0:lanes])
        half = got.shape[0] // 2
        return got[:half] + got[half:]

    each(groups, first)
    out[...] = product(wide * groups)
    jobs = []
    if some.chunks == 1:
        return jobs
    for k in range(groups):
        lists = lists_of(k)
        last = jnp.zeros((1, wide), jnp.int32)
        for chunk in range(1, lists.chunks):
            a, b, c, node, weight = lists.load(owner, chunk)
            needed = (weight > 0.0) & (a >= a_first) & (a < a_first + a_count)
            last = jnp.where(needed, chunk + 1, last)

        def one(chunk, carry, lists=lists):
            fill(lists, owner, chunk, a_first, a_count, lhs, rhs, 0)
            out[...] += product(wide)
            return carry

        jobs.append((last, one))
    return jobs


def later_chunks(jobs):
    if not jobs:
        return
    top = None
    for count, _ in jobs:
        most = jnp.max(count, axis=1, keepdims=True)
        top = most if top is None else jnp.maximum(top, most)

    @pl.when(jnp.max(top) > 0)
    def _():
        for last, (count, one) in zip([jnp.max(count) for count, _ in jobs], jobs):
            lax.fori_loop(1, last, one, 0)


def shift_sum(x):
    lane = lax.broadcasted_iota(jnp.int32, x.shape, 1)
    left = jnp.where(lane == 0, 0.0, pltpu.roll(x, 1, 1))
    right = jnp.where(lane == CZ - 1, 0.0, pltpu.roll(x, CZ - 1, 1))
    return x + 0.5 * (left + right)


def plane_sum(src, a, count):
    cols = [src(a, b) + 0.5 * (src(a - 1, b) + src(a + 1, b)) for b in range(count)]
    out = []
    for b in range(count):
        beside = [cols[i] for i in (b - 1, b + 1) if 0 <= i < count]
        total = beside[0] if len(beside) == 1 else beside[0] + beside[1]
        out.append(shift_sum(cols[b] + 0.5 * total))
    return out


def second_plane(src, a, count):
    return [SEC_U * src(a, b) + SEC_T * t for b, t in enumerate(plane_sum(src, a, count))]


def source_reader(modes, mid, edge=None):
    def src(a, b):
        lanes = slice((b % 2) * CZ, (b % 2 + 1) * CZ)
        owner, pair = b // CY, b % CY // 2
        if a < HALO:
            ref, at = edge[0], pair * HALO + a
        elif a >= CX + HALO:
            ref, at = edge[1], pair * HALO + a - CX - HALO
        else:
            ref, at = mid, pair * CX + a - HALO
        return ref[owner, at * modes : (at + 1) * modes, lanes]

    return src


def own_source_kernel(modes, groups, capacity, both, _, own, inner, *scratch):
    jobs = []

    def one(o):
        at = 2 * o if isinstance(o, int) else 0
        mem = scratch[at : at + 2]
        jobs.extend(scatter(both, modes, capacity, o, 0, CX, own.at[o], *mem))

    each(groups, one)
    later_chunks(jobs)
    src = source_reader(modes, own)
    for a in range(HALO + 1, CX + HALO - 1):
        for b, sec in enumerate(second_plane(src, a, groups * CY)):
            inner[a - HALO - 1, b] = sec


def fluid_kernel(modes, groups, capacity, both, low, high, mid, inner, mdiag, stiff, *refs):
    outs = refs[:groups]
    edge, outer, press, force, scratch = (
        refs[groups : groups + 2],
        *refs[groups + 2 : groups + 5],
        refs[groups + 5 :],
    )
    local = both.shape[2]
    count = groups * CY
    width = min(local, capacity)
    jobs = []
    for side, there in enumerate((low, high)):
        a_first = CX - HALO if side == 0 else 0
        wide = 128 if side == 0 else 256
        half = len(scratch) // 2
        sets = scratch[side * half : (side + 1) * half]

        def one(o, there=there, a_first=a_first, wide=wide, sets=sets, side=side):
            at = 2 * o if isinstance(o, int) else 0
            mem = sets[at : at + 2]
            target = edge[side].at[o]
            jobs.extend(scatter(there, modes, capacity, o, a_first, HALO, target, *mem, wide))

        each(groups, one)
    later_chunks(jobs)
    src = source_reader(modes, mid, edge)
    for i, a in enumerate((1, 2, CX + HALO - 1, CX + HALO)):
        for b, sec in enumerate(second_plane(src, a, count)):
            outer[i, b] = sec

    def second(a, b):
        if a < HALO:
            return outer[a, b]
        if a >= CX:
            return outer[a - CX + HALO, b]
        return inner[a - HALO, b]

    for a in range(0, CX, 2):
        two = [plane_sum(second, a + 1, count), plane_sum(second, a + 2, count)]
        for b in range(count):
            p = jnp.concatenate(
                [
                    PRE_SRC * src(a + i + HALO, b) + PRE_SEC * second(a + i + 1, b) + PRE_T * two[i][b]
                    for i in range(2)
                ],
                axis=0,
            )
            hi, lo = split(p)
            owner, at = b // CY, (b % CY // 2 * CX + a) * modes
            lanes = (b % 2) * CZ
            press[owner, at : at + 2 * modes, lanes : lanes + CZ] = hi
            press[owner, at : at + 2 * modes, 2 * CZ + lanes : 3 * CZ + lanes] = lo

    def joined(owner, chunk, devices):
        loads = [Lists(both.at[k], modes, capacity).load(owner, chunk) for k in devices]
        return [jnp.concatenate(x, axis=1) for x in zip(*loads)]

    def pick(owner, chunk, devices):
        a, b, c, node, weight = joined(owner, chunk, devices)
        hot = onehot((b & 1) * CZ + c, 2 * CZ)
        got = dot(press[owner], jnp.concatenate([hot, hot], axis=0))
        pair = jnp.broadcast_to(lax.shift_right_logical(b, 1) * CX + a, (modes, a.shape[1]))
        picked = jnp.zeros(pair.shape, F32)
        for r in range(CX * CY // 2):
            picked = jnp.where(pair == r, got[r * modes : (r + 1) * modes], picked)
        return picked * weight, node

    def to_nodes(picked, node):
        hi, lo = split(picked)
        sums = dot_t(jnp.concatenate([hi, lo], axis=0), onehot(node, local))
        return sums[:modes] + sums[modes:]

    def collect(k, owner, chunk):
        return to_nodes(*pick(owner, chunk, [k]))

    if groups <= 4:
        every = [pick(o, 0, range(groups)) for o in range(groups)]
        for k in range(groups):
            lanes = slice(k * width, (k + 1) * width)
            parts = [[x[:, lanes] for x in one] for one in every]
            force[k] = to_nodes(*[jnp.concatenate(x, axis=1) for x in zip(*parts)])
    else:

        def per_device(k):
            force[k] = jnp.zeros((modes, local), F32)

            def per_owner(o):
                force[k] = force[k] + collect(k, o, 0)

            each(groups, per_owner)

        each(groups, per_device)
    chunks = Lists(both.at[0], modes, capacity).chunks
    if chunks > 1:
        later = [(k, o, c) for k in range(groups) for o in range(groups) for c in range(1, chunks)]
        tops = [
            jnp.max(Lists(both.at[k], modes, capacity).row(2, o, c)) for k, o, c in later
        ]
        for (k, o, c), top in zip(later, tops):

            @pl.when(top > 0.0)
            def _():
                force[k] = force[k] + collect(k, o, c)

    for k in range(groups):
        for w in range(3):
            outs[k][w * modes : (w + 1) * modes, :] = force[(1 - k - w) % groups]
        if k in (1, groups - 1):
            at = 3 * modes
            outs[k][at : at + 8, :] = jnp.broadcast_to(mdiag[...], (8, local))
            outs[k][at + 8 :, :] = stiff[...]


def apply_blocks(window, cols_ref, kb_ref, sub, groups, diag, field):
    rb, nb, bs, _ = kb_ref.shape
    pieces = []
    for q in range(rb):
        parts = []
        for n in range(nb):
            j = cols_ref[q, n]
            where = sub + j // rb - 1
            inside = jnp.where((where >= 0) & (where < groups), 1.0, 0.0)
            parts.append(window[j] * inside)
        pieces.append(
            lax.dot_general(
                jnp.concatenate(parts, axis=1),
                kb_ref[q].reshape(nb * bs, bs),
                (((1,), (0,)), ((), ())),
                precision=lax.Precision.HIGHEST,
                preferred_element_type=F32,
            )
        )
    return diag * field + jnp.concatenate(pieces, axis=1)


def fill_window(win, blocks, bs):
    at = 0
    for blk in blocks:
        for i in range(blk.shape[1] // bs):
            win[at] = blk[:, i * bs : (i + 1) * bs]
            at += 1


def stiff_kernel(modes, groups, sub_ref, cols_ref, prev, own, nxt, diag, kb, out, win):
    bs = kb.shape[2]
    fill_window(win, [prev[0:modes, :], own[0:modes, :], nxt[0:modes, :]], bs)
    out[...] = apply_blocks(win, cols_ref, kb, sub_ref[0], groups, diag[...], own[0:modes, :])


def first_mode(modes, groups, count, sub):
    return pl.multiple_of(lax.shift_right_logical(sub * (modes // groups), log2(count)) * count, count)


def gram_kernel(modes, groups, count, sub_ref, cols_ref, prev, pack, nxt, mdiag, *refs):
    parts = refs[:groups]
    stiff, diag, kb, keep, send, mass, win, gram, force = refs[groups:]
    bs = kb.shape[2]
    for k in range(groups):
        source = lax.rem(sub_ref[0] + groups - k, groups)
        at = first_mode(modes, groups, count, source)
        for w in range(3):
            force[w, pl.ds(at, count), :] = parts[k][w * count : (w + 1) * count, :]
    at = 3 * count
    before, after = parts[1], parts[groups - 1]
    fields = [
        force[0] + before[at : at + 1, :] * prev[0:modes, :],
        force[1] + mdiag[...] * pack[0:modes, :],
        force[2] + after[at : at + 1, :] * nxt[0:modes, :],
    ]
    own = fields[1]
    mass[...] = own
    s = stiff[...]
    ends = [before[at + 8 :, :], s, after[at + 8 :, :]]
    both = [jnp.concatenate([x, y], axis=0) for x, y in zip(ends, fields)]
    fill_window(win, both, bs)
    image = apply_blocks(win, cols_ref, kb, sub_ref[0], groups, diag[...], both[1])
    v = pack[0:modes, :]
    left = jnp.concatenate([v, s, own], axis=0)
    right = jnp.concatenate([s, image, own], axis=0)

    def inner(x, y):
        return lax.dot_general(
            x,
            y,
            (((1,), (1,)), ((), ())),
            precision=lax.Precision.HIGHEST,
            preferred_element_type=F32,
        )

    whole = inner(left, right)
    half = 3 * modes // 2
    gram[0] = whole[:half]
    gram[1] = whole[half:]
    gram[1, 2 * modes - half : 3 * modes - half, 0:modes] = inner(v, v)
    core = sub_ref[1]
    keep[...] = gram[core]
    send[...] = gram[1 - core]


def final_kernel(modes, total, sub_ref, mine, other, stiff, mass, residual, g_stiff, g_plain, gram):
    m = modes
    core = sub_ref[1]
    half = 3 * m // 2
    gram[pl.ds(pl.multiple_of(core * half, half), half), :] = mine[...]
    gram[pl.ds(pl.multiple_of((1 - core) * half, half), half), :] = other[...]
    blocks = [
        [gram[i * m : (i + 1) * m, j * m : (j + 1) * m] for j in range(4)] for i in range(3)
    ]
    (vs, vks, vkm, vm), (ss, sks, skm, sm), (vv, mks, mkm, mm) = blocks
    rows = lax.broadcasted_iota(jnp.int32, (m, m), 0)
    lanes = lax.broadcasted_iota(jnp.int32, (m, m), 1)
    eye = rows == lanes

    def column(x):
        return jnp.sum(jnp.where(eye, x, 0.0), axis=1, keepdims=True)

    def line(x):
        return jnp.sum(jnp.where(eye, x, 0.0), axis=0, keepdims=True)

    tc = column(vs) / column(vm)
    tl = line(vs) / line(vm)
    residual[...] = stiff[...] - tc * mass[...]
    ms = sm.T
    scale = 1.0 / total
    vr = vs - vm * tl
    g_plain[0:m, 0:m] = vv * scale
    g_plain[0:m, m : 2 * m] = vr * scale
    g_plain[m : 2 * m, 0:m] = vr.T * scale
    g_plain[m : 2 * m, m : 2 * m] = (ss - sm * tl - tc * (ms - mm * tl)) * scale
    g_stiff[0:m, 0:m] = vs * scale
    g_stiff[0:m, m : 2 * m] = (vks - vkm * tl) * scale
    g_stiff[m : 2 * m, 0:m] = (ss - tc * ms) * scale
    g_stiff[m : 2 * m, m : 2 * m] = (sks - skm * tl - tc * (mks - mkm * tl)) * scale


def shifted(x, axis, k):
    n = lax.axis_size(axis)
    return lax.ppermute(x, axis, [(i, (i + k) % n) for i in range(n)])


def swapped(x, axis, k):
    n = lax.axis_size(axis)
    return lax.ppermute(x, axis, [(i, i ^ k) for i in range(n)])


def summed(x, axis, bit):
    n = lax.axis_size(axis)
    while (1 << bit) < n:
        if (4 << bit) <= n:
            one, two, three = [swapped(x, axis, k << bit) for k in (1, 2, 3)]
            x = (x + one) + (two + three)
            bit += 2
        else:
            x = x + swapped(x, axis, 1 << bit)
            bit += 1
    return x


def smem():
    return pl.BlockSpec(memory_space=pltpu.SMEM)


def vmem():
    return pl.BlockSpec(memory_space=pltpu.VMEM)


def call(kernel, name, out_shape, scalars, arrays, scratch, flops, mib=4):
    return pl.pallas_call(
        kernel,
        name=name,
        out_shape=out_shape,
        in_specs=[smem()] * len(scalars) + [vmem()] * len(arrays),
        out_specs=jax.tree.map(lambda _: vmem(), out_shape),
        scratch_shapes=scratch,
        compiler_params=pltpu.CompilerParams(vmem_limit_bytes=mib << 20),
        cost_estimate=pl.CostEstimate(flops=flops, transcendentals=0, bytes_accessed=1 << 20),
    )(*scalars, *arrays)


def body(
    block_vectors,
    stiffness,
    mass_diag,
    kblocks,
    block_cols,
    slot_node,
    slot_owner,
    slot_cell,
    slot_weight,
    live_slots,
):
    modes, local = block_vectors.shape
    groups = lax.axis_size("sub")
    slots = slot_node.shape[0]
    bs = kblocks.shape[2]
    total = local * lax.axis_size("passage") * groups
    sub = jnp.stack([lax.axis_index("sub"), lax.axis_index("passage") & 1]).astype(jnp.int32)
    deep, wide = slots // 128, 128
    capacity = 2 * slots // groups
    slotted = [x.reshape(deep, wide) for x in (slot_owner, slot_cell, slot_node, slot_weight)]
    pack, mdiag, diag, cols = pl.pallas_call(
        functools.partial(pack_kernel, modes, groups),
        name="pack",
        out_shape=(
            jax.ShapeDtypeStruct((modes + 3 * deep, local), F32),
            jax.ShapeDtypeStruct((1, local), F32),
            jax.ShapeDtypeStruct((1, local), F32),
            jax.ShapeDtypeStruct(block_cols.shape, jnp.int32),
        ),
        in_specs=[smem()] + [pl.BlockSpec(memory_space=pltpu.MemorySpace.HBM)] * 8,
        out_specs=(vmem(), vmem(), vmem(), vmem()),
        scratch_shapes=[pltpu.VMEM((deep, wide), x.dtype) for x in slotted]
        + [pltpu.SemaphoreType.DMA((8,))],
        compiler_params=pltpu.CompilerParams(vmem_limit_bytes=4 << 20),
        cost_estimate=pl.CostEstimate(flops=1 << 28, transcendentals=0, bytes_accessed=1 << 20),
    )(
        live_slots,
        *[
            pltpu.with_memory_space_constraint(x, pltpu.MemorySpace.HBM)
            for x in (
                *slotted,
                block_vectors,
                mass_diag[None, :],
                stiffness[None, :],
                block_cols,
            )
        ]
    )
    packs = [pack] + [shifted(pack, "sub", k) for k in range(1, groups)]
    mine = max(8, modes // groups)
    start = first_mode(modes, groups, mine, lax.axis_index("sub").astype(jnp.int32))
    both = jnp.stack(
        [
            jnp.concatenate([lax.dynamic_slice_in_dim(x, start, mine), x[modes:]], axis=0)
            for x in packs
        ]
    )
    low = shifted(both, "passage", 1)
    high = shifted(both, "passage", -1)
    window = [packs[1], packs[0], packs[groups - 1]]
    nwin = 3 * local // bs
    stiff = call(
        functools.partial(stiff_kernel, modes, groups),
        "stiff",
        jax.ShapeDtypeStruct((modes, local), F32),
        [sub, cols],
        [*window, diag, kblocks],
        [pltpu.VMEM((nwin, modes, bs), F32)],
        1 << 29,
    )
    width = min(local, capacity)
    sets = groups if groups <= 4 else 1

    def field(*shape):
        return jax.ShapeDtypeStruct(shape, F32)

    def operands(rows, chunk):
        deep = min(chunk, width) * groups
        return sets * [pltpu.VMEM((2 * rows, deep), BF), pltpu.VMEM((2 * CZ, deep), BF)]

    rows = CX * CY // 2 * mine
    edge_rows = HALO * CY // 2 * mine
    mib = 20 if groups <= 4 else 36
    source, inner = call(
        functools.partial(own_source_kernel, mine, groups, capacity),
        "own_source",
        (field(groups, rows, 2 * CZ), field(CX - 2, groups * CY, mine, CZ)),
        [],
        [both, stiff],
        operands(rows, width),
        1 << 32,
        mib,
    )
    force = call(
        functools.partial(fluid_kernel, mine, groups, capacity),
        "fluid",
        tuple(
            field(3 * mine + (8 + modes if k in (1, groups - 1) else 0), local)
            for k in range(groups)
        ),
        [],
        [both, low, high, source, inner, mdiag, stiff],
        [
            *[pltpu.VMEM((groups, edge_rows, 2 * CZ), F32)] * 2,
            pltpu.VMEM((4, groups * CY, mine, CZ), F32),
            pltpu.VMEM((groups, rows, 4 * CZ), BF),
            pltpu.VMEM((groups, mine, local), F32),
            *operands(edge_rows, 128),
            *operands(edge_rows, 256),
        ],
        1 << 32,
        mib,
    )
    parts = [force[0]] + [shifted(force[k], "sub", k) for k in range(1, groups)]
    keep, send, mass = call(
        functools.partial(gram_kernel, modes, groups, mine),
        "gram",
        (field(3 * modes // 2, 4 * modes), field(3 * modes // 2, 4 * modes), field(modes, local)),
        [sub, cols],
        [*window, mdiag, *parts, stiff, diag, kblocks],
        [
            pltpu.VMEM((nwin, 2 * modes, bs), F32),
            pltpu.VMEM((2, 3 * modes // 2, 4 * modes), F32),
            pltpu.VMEM((3, modes, local), F32),
        ],
        1 << 29,
    )
    mine = keep + swapped(send, "passage", 1)
    mine = summed(mine, "passage", 1)
    mine = summed(mine, "sub", 0)
    other = swapped(mine, "passage", 1)
    return call(
        functools.partial(final_kernel, modes, float(total)),
        "final",
        (field(modes, local), field(2 * modes, 2 * modes), field(2 * modes, 2 * modes)),
        [sub],
        [mine, other, stiff, mass],
        [pltpu.VMEM((3 * modes, 4 * modes), F32)],
        1 << 20,
    )


def solution(mesh):
    return jax.shard_map(
        body,
        mesh=mesh,
        in_specs=(
            P(None, ("passage", "sub")),
            P(("passage", "sub")),
            P(("passage", "sub")),
            P(("passage", "sub"), None, None, None),
            P(("passage", "sub"), None),
            P(("passage", "sub")),
            P(("passage", "sub"), None),
            P(("passage", "sub")),
            P(("passage", "sub")),
            P(("passage", "sub")),
        ),
        out_specs=(P(None, ("passage", "sub")), P(), P()),
        check_vma=False,
    )
```

```python
import functools
import jax
import jax.numpy as jnp
from jax import lax
from jax.experimental import pallas as pl
from jax.experimental.pallas import tpu as pltpu
from jax.sharding import PartitionSpec as P

CX = 8
CY = 8
CZ = 128
HALO = 2

center_weight = 15.0
lower_bound = 1.0 / 15.0
upper_bound = 17.0 / 15.0
middle = (upper_bound + lower_bound) / 2.0
radius = (upper_bound - lower_bound) / 2.0
sigma_ratio = middle / radius
first_rho = 1.0 / sigma_ratio
second_rho = 1.0 / (2.0 * sigma_ratio - first_rho)
third_rho = 1.0 / (2.0 * sigma_ratio - second_rho)

FIRST = 1.0 / (center_weight * middle)
GAIN2 = 2.0 * second_rho / (radius * center_weight)
SEC_U = FIRST * (1.0 + second_rho * first_rho) + GAIN2 * (1.0 - 17.0 * FIRST)
SEC_T = GAIN2 * 2.0 * FIRST
STEP3 = third_rho * second_rho
GAIN3 = 2.0 * third_rho / (radius * center_weight)
PRE_SRC = GAIN3 - STEP3 * FIRST
PRE_SEC = 1.0 + STEP3 - 17.0 * GAIN3
PRE_T = 2.0 * GAIN3

BF = jnp.bfloat16
F32 = jnp.float32
CELLS = CX * CY * CZ


def log2(n):
    return n.bit_length() - 1


def split(x):
    hi = x.astype(BF)
    return hi, (x - hi.astype(F32)).astype(BF)


def lanes_from(x, index):
    return jnp.take_along_axis(
        x, jnp.broadcast_to(index, x.shape), axis=1, mode="promise_in_bounds"
    )


def onehot(values, height):
    shape = (height, values.shape[1])
    rows = lax.broadcasted_iota(jnp.int32, shape, 0)
    return jnp.where(rows == values, 1.0, 0.0).astype(BF)


def dot_t(x, y):
    return lax.dot_general(x, y, (((1,), (1,)), ((), ())), preferred_element_type=F32)


def dot(x, y):
    return lax.dot_general(x, y, (((1,), (0,)), ((), ())), preferred_element_type=F32)


def pack_kernel(modes, groups, live_ref, *refs):
    sources, (out, mdiag, diag, cols) = refs[:8], refs[8:12]
    owner_ref, cell_ref, node_ref, weight_ref, sems = refs[12:]
    targets = [owner_ref, cell_ref, node_ref, weight_ref]
    targets += [out.at[0:modes, :], mdiag, diag, cols]
    copies = [
        pltpu.make_async_copy(x, y, sems.at[i]) for i, (x, y) in enumerate(zip(sources, targets))
    ]
    for copy in copies:
        copy.start()
    for copy in copies[:4]:
        copy.wait()
    deep, wide = owner_ref.shape
    capacity = 2 * deep * wide // groups
    keys = groups * CX
    owner, cell, weight = owner_ref[...], cell_ref[...], weight_ref[...]
    shape = (deep, wide)
    place = lax.broadcasted_iota(jnp.int32, shape, 0) * wide + lax.broadcasted_iota(
        jnp.int32, shape, 1
    )
    live = place < live_ref[0]
    a = lax.shift_right_logical(cell, log2(CY * CZ))
    key = jnp.where(live, owner * CX + ((a + HALO) & (CX - 1)), -1)
    hots = jnp.concatenate([jnp.where(key == k, 1.0, 0.0) for k in range(keys)], axis=0).astype(BF)
    rows = lax.broadcasted_iota(jnp.int32, (wide, wide), 0)
    lanes = lax.broadcasted_iota(jnp.int32, (wide, wide), 1)
    within = dot(hots, jnp.where(rows <= lanes, 1.0, 0.0).astype(BF))
    size = keys * deep
    rows = lax.broadcasted_iota(jnp.int32, (size, size), 0)
    lanes = lax.broadcasted_iota(jnp.int32, (size, size), 1)
    shift = log2(CX * deep)
    same = lax.shift_right_logical(rows, shift) == lax.shift_right_logical(lanes, shift)
    earlier = jnp.where(same & (lanes < rows), 1.0, 0.0).astype(BF)
    ahead = dot(dot(earlier, hots).astype(BF), jnp.ones((wide, wide), BF))
    order = within + ahead - 1.0
    pos = jnp.zeros(shape, F32)
    for k in range(keys):
        pos = jnp.where(key == k, order[k * deep : (k + 1) * deep], pos)
    target = owner * capacity + pos.astype(jnp.int32)
    line = lax.shift_right_logical(target, log2(wide))
    half = deep
    line = jnp.where(live, lax.shift_right_logical(line, 1) + (line & 1) * half, -1)
    lane = target & (wide - 1)
    w1 = weight.astype(BF).astype(F32)
    w2 = (weight - w1).astype(BF).astype(F32)
    values = [
        lax.shift_right_logical(cell, 8).astype(F32),
        (cell & 255).astype(F32),
        node_ref[...].astype(F32),
        w1,
        w2,
        weight - w1 - w2,
    ]
    lefts, rights = [], []
    for r in range(deep):
        into = lax.broadcasted_iota(jnp.int32, (2 * half, wide), 0) == line[r : r + 1]
        lefts.append(
            jnp.concatenate([jnp.where(into, v[r : r + 1], 0.0) for v in values], axis=0).astype(BF)
        )
        rights.append(onehot(lane[r : r + 1], wide))
    listed = dot_t(jnp.concatenate(lefts, axis=1), jnp.concatenate(rights, axis=1))
    part = [listed[i * 2 * half : (i + 1) * 2 * half] for i in range(6)]
    lists = [256.0 * part[0] + part[1], part[2], part[3] + part[4] + part[5]]
    for i, x in enumerate(lists):
        at = modes + i * half
        out[at : at + half, 0:wide] = x[:half]
        out[at : at + half, wide : 2 * wide] = x[half:]
    for copy in copies[4:]:
        copy.wait()


class Lists:
    def __init__(self, blk, modes, capacity, width=None):
        self.blk, self.modes = blk, modes
        self.local = blk.shape[1]
        self.lines = (blk.shape[0] - modes) // 3
        self.width = min(width or self.local, capacity)
        self.capacity = capacity
        self.chunks = capacity // self.width

    def row(self, kind, owner, chunk):
        at = owner * self.capacity + chunk * self.width
        line = at // self.local if isinstance(at, int) else lax.shift_right_logical(at, log2(self.local))
        x = self.blk[pl.ds(self.modes + kind * self.lines + line, 1), :]
        if self.width < self.local:
            if isinstance(at, int):
                first = at % self.local
                return x[:, first : first + self.width]
            group = lax.shift_right_logical(at, log2(self.width)) & (self.local // self.width - 1)
            got = x[:, : self.width]
            for g in range(1, self.local // self.width):
                got = jnp.where(group == g, x[:, g * self.width : (g + 1) * self.width], got)
            x = got
        return x

    def load(self, owner, chunk):
        cell = self.row(0, owner, chunk).astype(jnp.int32)
        node = self.row(1, owner, chunk).astype(jnp.int32)
        weight = self.row(2, owner, chunk)
        a = lax.shift_right_logical(cell, log2(CY * CZ))
        b = lax.shift_right_logical(cell, log2(CZ)) & (CY - 1)
        return a, b, cell & (CZ - 1), node, weight


def each(n, step):
    if n <= 4:
        for i in range(n):
            step(i)
        return

    def one(i, carry):
        step(i)
        return carry

    lax.fori_loop(0, n, one, 0)


def fill(lists, owner, chunk, a_first, a_count, lhs, rhs, at):
    modes, width = lists.modes, lists.width
    a, b, c, node, weight = lists.load(owner, chunk)
    aloc = a - a_first
    valid = (aloc >= 0) & (aloc < a_count)
    pair = jnp.where(valid, lax.shift_right_logical(b, 1) * a_count + aloc, -16)
    pieces = []
    for h in range(width // 128):
        idx = node[:, h * 128 : (h + 1) * 128]
        got = None
        for g in range(lists.local // 128):
            part = lanes_from(lists.blk[0:modes, g * 128 : (g + 1) * 128], idx & 127)
            got = part if g == 0 else jnp.where(lax.shift_right_logical(idx, 7) == g, part, got)
        pieces.append(got)
    vals = jnp.concatenate(pieces, axis=1) * weight
    times = max(1, 16 // modes)
    tall = times * modes
    hi, lo = split(jnp.concatenate([vals] * times, axis=0))
    step = lax.shift_right_logical(
        lax.broadcasted_iota(jnp.int32, (tall, width), 0), log2(modes)
    )
    wide = (pair - step).astype(F32).astype(BF)
    zero = jnp.zeros((tall, width), BF)
    lanes = pl.ds(at, width)
    half = a_count * CY // 2 * modes
    for r in range(0, a_count * CY // 2, times):
        mask = wide == jnp.asarray(r, BF)
        row = r * modes
        lhs[row : row + tall, lanes] = jnp.where(mask, hi, zero)
        lhs[half + row : half + row + tall, lanes] = jnp.where(mask, lo, zero)
    rhs[:, lanes] = onehot((b & 1) * CZ + c, 2 * CZ)


def scatter(both, modes, capacity, owner, a_first, a_count, out, lhs, rhs, width=None):
    groups = both.shape[0]

    def lists_of(k):
        return Lists(both.at[k], modes, capacity, width)

    some = lists_of(0)
    wide = some.width

    def first(k):
        at = k * wide
        at = at if isinstance(k, int) else pl.multiple_of(at, 128)
        fill(lists_of(k), owner, 0, a_first, a_count, lhs, rhs, at)

    def product(lanes):
        got = dot_t(lhs[:, 0:lanes], rhs[:, 0:lanes])
        half = got.shape[0] // 2
        return got[:half] + got[half:]

    each(groups, first)
    out[...] = product(wide * groups)
    jobs = []
    if some.chunks == 1:
        return jobs
    for k in range(groups):
        lists = lists_of(k)
        last = jnp.zeros((1, wide), jnp.int32)
        for chunk in range(1, lists.chunks):
            a, b, c, node, weight = lists.load(owner, chunk)
            needed = (weight > 0.0) & (a >= a_first) & (a < a_first + a_count)
            last = jnp.where(needed, chunk + 1, last)

        def one(chunk, carry, lists=lists):
            fill(lists, owner, chunk, a_first, a_count, lhs, rhs, 0)
            out[...] += product(wide)
            return carry

        jobs.append((last, one))
    return jobs


def later_chunks(jobs):
    if not jobs:
        return
    top = None
    for count, _ in jobs:
        most = jnp.max(count, axis=1, keepdims=True)
        top = most if top is None else jnp.maximum(top, most)

    @pl.when(jnp.max(top) > 0)
    def _():
        for last, (count, one) in zip([jnp.max(count) for count, _ in jobs], jobs):
            lax.fori_loop(1, last, one, 0)


def shift_sum(x):
    lane = lax.broadcasted_iota(jnp.int32, x.shape, 1)
    left = jnp.where(lane == 0, 0.0, pltpu.roll(x, 1, 1))
    right = jnp.where(lane == CZ - 1, 0.0, pltpu.roll(x, CZ - 1, 1))
    return x + 0.5 * (left + right)


def plane_sum(src, a, count):
    cols = [src(a, b) + 0.5 * (src(a - 1, b) + src(a + 1, b)) for b in range(count)]
    out = []
    for b in range(count):
        beside = [cols[i] for i in (b - 1, b + 1) if 0 <= i < count]
        total = beside[0] if len(beside) == 1 else beside[0] + beside[1]
        out.append(shift_sum(cols[b] + 0.5 * total))
    return out


def second_plane(src, a, count):
    return [SEC_U * src(a, b) + SEC_T * t for b, t in enumerate(plane_sum(src, a, count))]


def source_reader(modes, mid, edge=None):
    def src(a, b):
        lanes = slice((b % 2) * CZ, (b % 2 + 1) * CZ)
        owner, pair = b // CY, b % CY // 2
        if a < HALO:
            ref, at = edge.at[0], pair * HALO + a
        elif a >= CX + HALO:
            ref, at = edge.at[1], pair * HALO + a - CX - HALO
        else:
            ref, at = mid, pair * CX + a - HALO
        return ref[owner, at * modes : (at + 1) * modes, lanes]

    return src


def edge_source(there, modes, groups, capacity, low, out, sets, jobs):
    a_first = jnp.where(low > 0, CX - HALO, 0)

    def one(o):
        at = 2 * o if isinstance(o, int) else 0
        mem = sets[at : at + 2]
        jobs.extend(scatter(there, modes, capacity, o, a_first, HALO, out.at[o], *mem))

    each(groups, one)


def own_source_kernel(modes, groups, capacity, odd_ref, both, near, _, own, inner, edge, *scratch):
    jobs = []
    half = len(scratch) // 2
    edges, scratch = scratch[half:], scratch[:half]

    def one(o):
        at = 2 * o if isinstance(o, int) else 0
        mem = scratch[at : at + 2]
        jobs.extend(scatter(both, modes, capacity, o, 0, CX, own.at[o], *mem))

    each(groups, one)
    edge_source(near, modes, groups, capacity, odd_ref[0], edge, edges, jobs)
    later_chunks(jobs)
    src = source_reader(modes, own)
    for a in range(HALO + 1, CX + HALO - 1):
        for b, sec in enumerate(second_plane(src, a, groups * CY)):
            inner[a - HALO - 1, b] = sec


def fluid_kernel(
    modes, groups, capacity, odd_ref, both, far, near_edge, mid, inner, mdiag, stiff, *refs
):
    outs = refs[:groups]
    edge, outer, press, force, scratch = (
        refs[groups],
        *refs[groups + 1 : groups + 4],
        refs[groups + 4 :],
    )
    local = both.shape[2]
    count = groups * CY
    width = min(local, capacity)
    jobs = []
    odd = odd_ref[0]
    edge[1 - odd] = near_edge[...]
    edge_source(far, modes, groups, capacity, 1 - odd, edge.at[odd], scratch, jobs)
    later_chunks(jobs)
    src = source_reader(modes, mid, edge)
    for i, a in enumerate((1, 2, CX + HALO - 1, CX + HALO)):
        for b, sec in enumerate(second_plane(src, a, count)):
            outer[i, b] = sec

    def second(a, b):
        if a < HALO:
            return outer[a, b]
        if a >= CX:
            return outer[a - CX + HALO, b]
        return inner[a - HALO, b]

    for a in range(0, CX, 2):
        two = [plane_sum(second, a + 1, count), plane_sum(second, a + 2, count)]
        for b in range(count):
            p = jnp.concatenate(
                [
                    PRE_SRC * src(a + i + HALO, b) + PRE_SEC * second(a + i + 1, b) + PRE_T * two[i][b]
                    for i in range(2)
                ],
                axis=0,
            )
            hi, lo = split(p)
            owner, at = b // CY, (b % CY // 2 * CX + a) * modes
            lanes = (b % 2) * CZ
            press[owner, at : at + 2 * modes, lanes : lanes + CZ] = hi
            press[owner, at : at + 2 * modes, 2 * CZ + lanes : 3 * CZ + lanes] = lo

    def joined(owner, chunk, devices):
        loads = [Lists(both.at[k], modes, capacity).load(owner, chunk) for k in devices]
        return [jnp.concatenate(x, axis=1) for x in zip(*loads)]

    def pick(owner, chunk, devices):
        a, b, c, node, weight = joined(owner, chunk, devices)
        hot = onehot((b & 1) * CZ + c, 2 * CZ)
        got = dot(press[owner], jnp.concatenate([hot, hot], axis=0))
        pair = jnp.broadcast_to(lax.shift_right_logical(b, 1) * CX + a, (modes, a.shape[1]))
        picked = jnp.zeros(pair.shape, F32)
        for r in range(CX * CY // 2):
            picked = jnp.where(pair == r, got[r * modes : (r + 1) * modes], picked)
        return picked * weight, node

    def to_nodes(picked, node):
        hi, lo = split(picked)
        sums = dot_t(jnp.concatenate([hi, lo], axis=0), onehot(node, local))
        return sums[:modes] + sums[modes:]

    def collect(k, owner, chunk):
        return to_nodes(*pick(owner, chunk, [k]))

    if groups <= 4:
        every = [pick(o, 0, range(groups)) for o in range(groups)]
        for k in range(groups):
            lanes = slice(k * width, (k + 1) * width)
            parts = [[x[:, lanes] for x in one] for one in every]
            force[k] = to_nodes(*[jnp.concatenate(x, axis=1) for x in zip(*parts)])
    else:

        def per_device(k):
            force[k] = jnp.zeros((modes, local), F32)

            def per_owner(o):
                force[k] = force[k] + collect(k, o, 0)

            each(groups, per_owner)

        each(groups, per_device)
    chunks = Lists(both.at[0], modes, capacity).chunks
    if chunks > 1:
        later = [(k, o, c) for k in range(groups) for o in range(groups) for c in range(1, chunks)]
        tops = [
            jnp.max(Lists(both.at[k], modes, capacity).row(2, o, c)) for k, o, c in later
        ]
        for (k, o, c), top in zip(later, tops):

            @pl.when(top > 0.0)
            def _():
                force[k] = force[k] + collect(k, o, c)

    for k in range(groups):
        for w in range(3):
            outs[k][w * modes : (w + 1) * modes, :] = force[(1 - k - w) % groups]
        if k in (1, groups - 1):
            at = 3 * modes
            outs[k][at : at + 8, :] = jnp.broadcast_to(mdiag[...], (8, local))
            outs[k][at + 8 :, :] = stiff[...]


def apply_blocks(window, cols_ref, kb_ref, sub, groups, diag, field):
    rb, nb, bs, _ = kb_ref.shape
    pieces = []
    for q in range(rb):
        parts = []
        for n in range(nb):
            j = cols_ref[q, n]
            where = sub + j // rb - 1
            inside = jnp.where((where >= 0) & (where < groups), 1.0, 0.0)
            parts.append(window[j] * inside)
        pieces.append(
            lax.dot_general(
                jnp.concatenate(parts, axis=1),
                kb_ref[q].reshape(nb * bs, bs),
                (((1,), (0,)), ((), ())),
                precision=lax.Precision.HIGHEST,
                preferred_element_type=F32,
            )
        )
    return diag * field + jnp.concatenate(pieces, axis=1)


def fill_window(win, blocks, bs):
    at = 0
    for blk in blocks:
        for i in range(blk.shape[1] // bs):
            win[at] = blk[:, i * bs : (i + 1) * bs]
            at += 1


def stiff_kernel(modes, groups, sub_ref, cols_ref, prev, own, nxt, diag, kb, out, win):
    bs = kb.shape[2]
    fill_window(win, [prev[0:modes, :], own[0:modes, :], nxt[0:modes, :]], bs)
    out[...] = apply_blocks(win, cols_ref, kb, sub_ref[0], groups, diag[...], own[0:modes, :])


def first_mode(modes, groups, count, sub):
    return pl.multiple_of(lax.shift_right_logical(sub * (modes // groups), log2(count)) * count, count)


def gram_kernel(modes, groups, count, sub_ref, cols_ref, prev, pack, nxt, mdiag, *refs):
    parts = refs[:groups]
    stiff, diag, kb, keep, send, mass, win, gram, force = refs[groups:]
    bs = kb.shape[2]
    for k in range(groups):
        source = lax.rem(sub_ref[0] + groups - k, groups)
        at = first_mode(modes, groups, count, source)
        for w in range(3):
            force[w, pl.ds(at, count), :] = parts[k][w * count : (w + 1) * count, :]
    at = 3 * count
    before, after = parts[1], parts[groups - 1]
    fields = [
        force[0] + before[at : at + 1, :] * prev[0:modes, :],
        force[1] + mdiag[...] * pack[0:modes, :],
        force[2] + after[at : at + 1, :] * nxt[0:modes, :],
    ]
    own = fields[1]
    mass[...] = own
    s = stiff[...]
    ends = [before[at + 8 :, :], s, after[at + 8 :, :]]
    both = [jnp.concatenate([x, y], axis=0) for x, y in zip(ends, fields)]
    fill_window(win, both, bs)
    image = apply_blocks(win, cols_ref, kb, sub_ref[0], groups, diag[...], both[1])
    v = pack[0:modes, :]
    left = jnp.concatenate([v, s, own], axis=0)
    right = jnp.concatenate([s, image, own], axis=0)

    def inner(x, y):
        return lax.dot_general(
            x,
            y,
            (((1,), (1,)), ((), ())),
            precision=lax.Precision.HIGHEST,
            preferred_element_type=F32,
        )

    whole = inner(left, right)
    half = 3 * modes // 2
    gram[0] = whole[:half]
    gram[1] = whole[half:]
    gram[1, 2 * modes - half : 3 * modes - half, 0:modes] = inner(v, v)
    core = sub_ref[1]
    keep[...] = gram[core]
    send[...] = gram[1 - core]


def final_kernel(modes, total, sub_ref, mine, other, stiff, mass, residual, g_stiff, g_plain, gram):
    m = modes
    core = sub_ref[1]
    half = 3 * m // 2
    gram[pl.ds(pl.multiple_of(core * half, half), half), :] = mine[...]
    gram[pl.ds(pl.multiple_of((1 - core) * half, half), half), :] = other[...]
    blocks = [
        [gram[i * m : (i + 1) * m, j * m : (j + 1) * m] for j in range(4)] for i in range(3)
    ]
    (vs, vks, vkm, vm), (ss, sks, skm, sm), (vv, mks, mkm, mm) = blocks
    rows = lax.broadcasted_iota(jnp.int32, (m, m), 0)
    lanes = lax.broadcasted_iota(jnp.int32, (m, m), 1)
    eye = rows == lanes

    def column(x):
        return jnp.sum(jnp.where(eye, x, 0.0), axis=1, keepdims=True)

    def line(x):
        return jnp.sum(jnp.where(eye, x, 0.0), axis=0, keepdims=True)

    tc = column(vs) / column(vm)
    tl = line(vs) / line(vm)
    residual[...] = stiff[...] - tc * mass[...]
    ms = sm.T
    scale = 1.0 / total
    vr = vs - vm * tl
    g_plain[0:m, 0:m] = vv * scale
    g_plain[0:m, m : 2 * m] = vr * scale
    g_plain[m : 2 * m, 0:m] = vr.T * scale
    g_plain[m : 2 * m, m : 2 * m] = (ss - sm * tl - tc * (ms - mm * tl)) * scale
    g_stiff[0:m, 0:m] = vs * scale
    g_stiff[0:m, m : 2 * m] = (vks - vkm * tl) * scale
    g_stiff[m : 2 * m, 0:m] = (ss - tc * ms) * scale
    g_stiff[m : 2 * m, m : 2 * m] = (sks - skm * tl - tc * (mks - mkm * tl)) * scale


def shifted(x, axis, k):
    n = lax.axis_size(axis)
    return lax.ppermute(x, axis, [(i, (i + k) % n) for i in range(n)])


def swapped(x, axis, k):
    n = lax.axis_size(axis)
    return lax.ppermute(x, axis, [(i, i ^ k) for i in range(n)])


def summed(x, axis, bit):
    n = lax.axis_size(axis)
    while (1 << bit) < n:
        if (4 << bit) <= n:
            one, two, three = [swapped(x, axis, k << bit) for k in (1, 2, 3)]
            x = (x + one) + (two + three)
            bit += 2
        else:
            x = x + swapped(x, axis, 1 << bit)
            bit += 1
    return x


def smem():
    return pl.BlockSpec(memory_space=pltpu.SMEM)


def vmem():
    return pl.BlockSpec(memory_space=pltpu.VMEM)


def call(kernel, name, out_shape, scalars, arrays, scratch, flops, mib=4):
    return pl.pallas_call(
        kernel,
        name=name,
        out_shape=out_shape,
        in_specs=[smem()] * len(scalars) + [vmem()] * len(arrays),
        out_specs=jax.tree.map(lambda _: vmem(), out_shape),
        scratch_shapes=scratch,
        compiler_params=pltpu.CompilerParams(vmem_limit_bytes=mib << 20),
        cost_estimate=pl.CostEstimate(flops=flops, transcendentals=0, bytes_accessed=1 << 20),
    )(*scalars, *arrays)


def body(
    block_vectors,
    stiffness,
    mass_diag,
    kblocks,
    block_cols,
    slot_node,
    slot_owner,
    slot_cell,
    slot_weight,
    live_slots,
):
    modes, local = block_vectors.shape
    groups = lax.axis_size("sub")
    slots = slot_node.shape[0]
    bs = kblocks.shape[2]
    total = local * lax.axis_size("passage") * groups
    sub = jnp.stack([lax.axis_index("sub"), lax.axis_index("passage") & 1]).astype(jnp.int32)
    deep, wide = slots // 128, 128
    capacity = 2 * slots // groups
    slotted = [x.reshape(deep, wide) for x in (slot_owner, slot_cell, slot_node, slot_weight)]
    pack, mdiag, diag, cols = pl.pallas_call(
        functools.partial(pack_kernel, modes, groups),
        name="pack",
        out_shape=(
            jax.ShapeDtypeStruct((modes + 3 * deep, local), F32),
            jax.ShapeDtypeStruct((1, local), F32),
            jax.ShapeDtypeStruct((1, local), F32),
            jax.ShapeDtypeStruct(block_cols.shape, jnp.int32),
        ),
        in_specs=[smem()] + [pl.BlockSpec(memory_space=pltpu.MemorySpace.HBM)] * 8,
        out_specs=(vmem(), vmem(), vmem(), vmem()),
        scratch_shapes=[pltpu.VMEM((deep, wide), x.dtype) for x in slotted]
        + [pltpu.SemaphoreType.DMA((8,))],
        compiler_params=pltpu.CompilerParams(vmem_limit_bytes=4 << 20),
        cost_estimate=pl.CostEstimate(flops=1 << 28, transcendentals=0, bytes_accessed=1 << 20),
    )(
        live_slots,
        *[
            pltpu.with_memory_space_constraint(x, pltpu.MemorySpace.HBM)
            for x in (
                *slotted,
                block_vectors,
                mass_diag[None, :],
                stiffness[None, :],
                block_cols,
            )
        ]
    )
    packs = [pack] + [shifted(pack, "sub", k) for k in range(1, groups)]
    mine = max(8, modes // groups)
    start = first_mode(modes, groups, mine, lax.axis_index("sub").astype(jnp.int32))
    both = jnp.stack(
        [
            jnp.concatenate([lax.dynamic_slice_in_dim(x, start, mine), x[modes:]], axis=0)
            for x in packs
        ]
    )
    ring = lax.axis_size("passage")
    pairs = [(i, (i + 1 if i % 2 else i - 1) % ring) for i in range(ring)]
    far = lax.ppermute(both, "passage", pairs)
    near = swapped(both, "passage", 1)
    odd = (lax.axis_index("passage") & 1).astype(jnp.int32).reshape(1)
    window = [packs[1], packs[0], packs[groups - 1]]
    nwin = 3 * local // bs
    stiff = call(
        functools.partial(stiff_kernel, modes, groups),
        "stiff",
        jax.ShapeDtypeStruct((modes, local), F32),
        [sub, cols],
        [*window, diag, kblocks],
        [pltpu.VMEM((nwin, modes, bs), F32)],
        1 << 29,
    )
    width = min(local, capacity)
    sets = groups if groups <= 4 else 1

    def field(*shape):
        return jax.ShapeDtypeStruct(shape, F32)

    def operands(rows, chunk):
        deep = min(chunk, width) * groups
        return sets * [pltpu.VMEM((2 * rows, deep), BF), pltpu.VMEM((2 * CZ, deep), BF)]

    rows = CX * CY // 2 * mine
    edge_rows = HALO * CY // 2 * mine
    mib = 20 if groups <= 4 else 36
    source, inner, near_edge = call(
        functools.partial(own_source_kernel, mine, groups, capacity),
        "own_source",
        (
            field(groups, rows, 2 * CZ),
            field(CX - 2, groups * CY, mine, CZ),
            field(groups, edge_rows, 2 * CZ),
        ),
        [odd],
        [both, near, stiff],
        operands(rows, width) + operands(edge_rows, width),
        1 << 32,
        mib,
    )
    force = call(
        functools.partial(fluid_kernel, mine, groups, capacity),
        "fluid",
        tuple(
            field(3 * mine + (8 + modes if k in (1, groups - 1) else 0), local)
            for k in range(groups)
        ),
        [odd],
        [both, far, near_edge, source, inner, mdiag, stiff],
        [
            pltpu.VMEM((2, groups, edge_rows, 2 * CZ), F32),
            pltpu.VMEM((4, groups * CY, mine, CZ), F32),
            pltpu.VMEM((groups, rows, 4 * CZ), BF),
            pltpu.VMEM((groups, mine, local), F32),
            *operands(edge_rows, width),
        ],
        1 << 32,
        mib,
    )
    parts = [force[0]] + [shifted(force[k], "sub", k) for k in range(1, groups)]
    keep, send, mass = call(
        functools.partial(gram_kernel, modes, groups, mine),
        "gram",
        (field(3 * modes // 2, 4 * modes), field(3 * modes // 2, 4 * modes), field(modes, local)),
        [sub, cols],
        [*window, mdiag, *parts, stiff, diag, kblocks],
        [
            pltpu.VMEM((nwin, 2 * modes, bs), F32),
            pltpu.VMEM((2, 3 * modes // 2, 4 * modes), F32),
            pltpu.VMEM((3, modes, local), F32),
        ],
        1 << 29,
    )
    mine = keep + swapped(send, "passage", 1)
    mine = summed(mine, "passage", 1)
    mine = summed(mine, "sub", 0)
    other = swapped(mine, "passage", 1)
    return call(
        functools.partial(final_kernel, modes, float(total)),
        "final",
        (field(modes, local), field(2 * modes, 2 * modes), field(2 * modes, 2 * modes)),
        [sub],
        [mine, other, stiff, mass],
        [pltpu.VMEM((3 * modes, 4 * modes), F32)],
        1 << 20,
    )


def solution(mesh):
    return jax.shard_map(
        body,
        mesh=mesh,
        in_specs=(
            P(None, ("passage", "sub")),
            P(("passage", "sub")),
            P(("passage", "sub")),
            P(("passage", "sub"), None, None, None),
            P(("passage", "sub"), None),
            P(("passage", "sub")),
            P(("passage", "sub"), None),
            P(("passage", "sub")),
            P(("passage", "sub")),
            P(("passage", "sub")),
        ),
        out_specs=(P(None, ("passage", "sub")), P(), P()),
        check_vma=False,
    )
```

```python
import functools
import jax
import jax.numpy as jnp
from jax import lax
from jax.experimental import pallas as pl
from jax.experimental.pallas import tpu as pltpu
from jax.sharding import PartitionSpec as P

CX = 8
CY = 8
CZ = 128
HALO = 2

center_weight = 15.0
lower_bound = 1.0 / 15.0
upper_bound = 17.0 / 15.0
middle = (upper_bound + lower_bound) / 2.0
radius = (upper_bound - lower_bound) / 2.0
sigma_ratio = middle / radius
first_rho = 1.0 / sigma_ratio
second_rho = 1.0 / (2.0 * sigma_ratio - first_rho)
third_rho = 1.0 / (2.0 * sigma_ratio - second_rho)

FIRST = 1.0 / (center_weight * middle)
GAIN2 = 2.0 * second_rho / (radius * center_weight)
SEC_U = FIRST * (1.0 + second_rho * first_rho) + GAIN2 * (1.0 - 17.0 * FIRST)
SEC_T = GAIN2 * 2.0 * FIRST
STEP3 = third_rho * second_rho
GAIN3 = 2.0 * third_rho / (radius * center_weight)
PRE_SRC = GAIN3 - STEP3 * FIRST
PRE_SEC = 1.0 + STEP3 - 17.0 * GAIN3
PRE_T = 2.0 * GAIN3

BF = jnp.bfloat16
F32 = jnp.float32
CELLS = CX * CY * CZ


def log2(n):
    return n.bit_length() - 1


def split(x):
    hi = x.astype(BF)
    return hi, (x - hi.astype(F32)).astype(BF)


def lanes_from(x, index):
    return jnp.take_along_axis(
        x, jnp.broadcast_to(index, x.shape), axis=1, mode="promise_in_bounds"
    )


def onehot(values, height):
    shape = (height, values.shape[1])
    rows = lax.broadcasted_iota(jnp.int32, shape, 0)
    return jnp.where(rows == values, 1.0, 0.0).astype(BF)


def dot_t(x, y):
    return lax.dot_general(x, y, (((1,), (1,)), ((), ())), preferred_element_type=F32)


def dot(x, y):
    return lax.dot_general(x, y, (((1,), (0,)), ((), ())), preferred_element_type=F32)


def pack_kernel(modes, groups, count, live_ref, *refs):
    sources, (out, mdiag, diag, cols) = refs[:8], refs[8:12]
    distant = refs[12:-5]
    owner_ref, cell_ref, node_ref, weight_ref, sems = refs[-5:]
    targets = [owner_ref, cell_ref, node_ref, weight_ref]
    targets += [out.at[0:modes, :], mdiag, diag, cols]
    copies = [
        pltpu.make_async_copy(x, y, sems.at[i]) for i, (x, y) in enumerate(zip(sources, targets))
    ]
    for copy in copies:
        copy.start()
    for copy in copies[:4]:
        copy.wait()
    deep, wide = owner_ref.shape
    capacity = 2 * deep * wide // groups
    keys = groups * CX
    owner, cell, weight = owner_ref[...], cell_ref[...], weight_ref[...]
    shape = (deep, wide)
    place = lax.broadcasted_iota(jnp.int32, shape, 0) * wide + lax.broadcasted_iota(
        jnp.int32, shape, 1
    )
    live = place < live_ref[0]
    a = lax.shift_right_logical(cell, log2(CY * CZ))
    key = jnp.where(live, owner * CX + ((a + HALO) & (CX - 1)), -1)
    hots = jnp.concatenate([jnp.where(key == k, 1.0, 0.0) for k in range(keys)], axis=0).astype(BF)
    rows = lax.broadcasted_iota(jnp.int32, (wide, wide), 0)
    lanes = lax.broadcasted_iota(jnp.int32, (wide, wide), 1)
    within = dot(hots, jnp.where(rows <= lanes, 1.0, 0.0).astype(BF))
    size = keys * deep
    rows = lax.broadcasted_iota(jnp.int32, (size, size), 0)
    lanes = lax.broadcasted_iota(jnp.int32, (size, size), 1)
    shift = log2(CX * deep)
    same = lax.shift_right_logical(rows, shift) == lax.shift_right_logical(lanes, shift)
    earlier = jnp.where(same & (lanes < rows), 1.0, 0.0).astype(BF)
    ahead = dot(dot(earlier, hots).astype(BF), jnp.ones((wide, wide), BF))
    order = within + ahead - 1.0
    pos = jnp.zeros(shape, F32)
    for k in range(keys):
        pos = jnp.where(key == k, order[k * deep : (k + 1) * deep], pos)
    target = owner * capacity + pos.astype(jnp.int32)
    line = lax.shift_right_logical(target, log2(wide))
    half = deep
    line = jnp.where(live, lax.shift_right_logical(line, 1) + (line & 1) * half, -1)
    lane = target & (wide - 1)
    w1 = weight.astype(BF).astype(F32)
    w2 = (weight - w1).astype(BF).astype(F32)
    values = [
        lax.shift_right_logical(cell, 8).astype(F32),
        (cell & 255).astype(F32),
        node_ref[...].astype(F32),
        w1,
        w2,
        weight - w1 - w2,
    ]
    lefts, rights = [], []
    for r in range(deep):
        into = lax.broadcasted_iota(jnp.int32, (2 * half, wide), 0) == line[r : r + 1]
        lefts.append(
            jnp.concatenate([jnp.where(into, v[r : r + 1], 0.0) for v in values], axis=0).astype(BF)
        )
        rights.append(onehot(lane[r : r + 1], wide))
    listed = dot_t(jnp.concatenate(lefts, axis=1), jnp.concatenate(rights, axis=1))
    part = [listed[i * 2 * half : (i + 1) * 2 * half] for i in range(6)]
    lists = [256.0 * part[0] + part[1], part[2], part[3] + part[4] + part[5]]
    for i, x in enumerate(lists):
        at = modes + i * half
        out[at : at + half, 0:wide] = x[:half]
        out[at : at + half, wide : 2 * wide] = x[half:]
    for copy in copies[4:]:
        copy.wait()
    for k, far in enumerate(distant, 2):
        at = first_mode(modes, groups, count, lax.rem(lax.axis_index("sub").astype(jnp.int32) + k, groups))
        far[0:count, :] = out[pl.ds(at, count), :]
        far[count:, :] = out[modes:, :]


class Lists:
    def __init__(self, blk, modes, capacity, width=None):
        self.blk, self.modes = blk, modes
        self.local = blk.shape[1]
        self.lines = (blk.shape[0] - modes) // 3
        self.width = min(width or self.local, capacity)
        self.capacity = capacity
        self.chunks = capacity // self.width

    def row(self, kind, owner, chunk):
        at = owner * self.capacity + chunk * self.width
        line = at // self.local if isinstance(at, int) else lax.shift_right_logical(at, log2(self.local))
        x = self.blk[pl.ds(self.modes + kind * self.lines + line, 1), :]
        if self.width < self.local:
            if isinstance(at, int):
                first = at % self.local
                return x[:, first : first + self.width]
            group = lax.shift_right_logical(at, log2(self.width)) & (self.local // self.width - 1)
            got = x[:, : self.width]
            for g in range(1, self.local // self.width):
                got = jnp.where(group == g, x[:, g * self.width : (g + 1) * self.width], got)
            x = got
        return x

    def load(self, owner, chunk):
        cell = self.row(0, owner, chunk).astype(jnp.int32)
        node = self.row(1, owner, chunk).astype(jnp.int32)
        weight = self.row(2, owner, chunk)
        a = lax.shift_right_logical(cell, log2(CY * CZ))
        b = lax.shift_right_logical(cell, log2(CZ)) & (CY - 1)
        return a, b, cell & (CZ - 1), node, weight


def each(n, step):
    if n <= 4:
        for i in range(n):
            step(i)
        return

    def one(i, carry):
        step(i)
        return carry

    lax.fori_loop(0, n, one, 0)


def fill(lists, owner, chunk, a_first, a_count, lhs, rhs, at):
    modes, width = lists.modes, lists.width
    a, b, c, node, weight = lists.load(owner, chunk)
    aloc = a - a_first
    valid = (aloc >= 0) & (aloc < a_count)
    pair = jnp.where(valid, lax.shift_right_logical(b, 1) * a_count + aloc, -16)
    pieces = []
    for h in range(width // 128):
        idx = node[:, h * 128 : (h + 1) * 128]
        got = None
        for g in range(lists.local // 128):
            part = lanes_from(lists.blk[0:modes, g * 128 : (g + 1) * 128], idx & 127)
            got = part if g == 0 else jnp.where(lax.shift_right_logical(idx, 7) == g, part, got)
        pieces.append(got)
    vals = jnp.concatenate(pieces, axis=1) * weight
    times = max(1, 16 // modes)
    tall = times * modes
    hi, lo = split(jnp.concatenate([vals] * times, axis=0))
    step = lax.shift_right_logical(
        lax.broadcasted_iota(jnp.int32, (tall, width), 0), log2(modes)
    )
    wide = (pair - step).astype(F32).astype(BF)
    zero = jnp.zeros((tall, width), BF)
    lanes = pl.ds(at, width)
    half = a_count * CY // 2 * modes
    for r in range(0, a_count * CY // 2, times):
        mask = wide == jnp.asarray(r, BF)
        row = r * modes
        lhs[row : row + tall, lanes] = jnp.where(mask, hi, zero)
        lhs[half + row : half + row + tall, lanes] = jnp.where(mask, lo, zero)
    rhs[:, lanes] = onehot((b & 1) * CZ + c, 2 * CZ)


def scatter(both, modes, capacity, owner, a_first, a_count, out, lhs, rhs, width=None):
    groups = both.shape[0]

    def lists_of(k):
        return Lists(both.at[k], modes, capacity, width)

    some = lists_of(0)
    wide = some.width

    def first(k):
        at = k * wide
        at = at if isinstance(k, int) else pl.multiple_of(at, 128)
        fill(lists_of(k), owner, 0, a_first, a_count, lhs, rhs, at)

    def product(lanes):
        got = dot_t(lhs[:, 0:lanes], rhs[:, 0:lanes])
        half = got.shape[0] // 2
        return got[:half] + got[half:]

    each(groups, first)
    out[...] = product(wide * groups)
    jobs = []
    if some.chunks == 1:
        return jobs
    for k in range(groups):
        lists = lists_of(k)
        last = jnp.zeros((1, wide), jnp.int32)
        for chunk in range(1, lists.chunks):
            a, b, c, node, weight = lists.load(owner, chunk)
            needed = (weight > 0.0) & (a >= a_first) & (a < a_first + a_count)
            last = jnp.where(needed, chunk + 1, last)

        def one(chunk, carry, lists=lists):
            fill(lists, owner, chunk, a_first, a_count, lhs, rhs, 0)
            out[...] += product(wide)
            return carry

        jobs.append((last, one))
    return jobs


def later_chunks(jobs):
    if not jobs:
        return
    top = None
    for count, _ in jobs:
        most = jnp.max(count, axis=1, keepdims=True)
        top = most if top is None else jnp.maximum(top, most)

    @pl.when(jnp.max(top) > 0)
    def _():
        for last, (count, one) in zip([jnp.max(count) for count, _ in jobs], jobs):
            lax.fori_loop(1, last, one, 0)


def shift_sum(x):
    lane = lax.broadcasted_iota(jnp.int32, x.shape, 1)
    left = jnp.where(lane == 0, 0.0, pltpu.roll(x, 1, 1))
    right = jnp.where(lane == CZ - 1, 0.0, pltpu.roll(x, CZ - 1, 1))
    return x + 0.5 * (left + right)


def plane_sum(src, a, count):
    cols = [src(a, b) + 0.5 * (src(a - 1, b) + src(a + 1, b)) for b in range(count)]
    out = []
    for b in range(count):
        beside = [cols[i] for i in (b - 1, b + 1) if 0 <= i < count]
        total = beside[0] if len(beside) == 1 else beside[0] + beside[1]
        out.append(shift_sum(cols[b] + 0.5 * total))
    return out


def second_plane(src, a, count):
    return [SEC_U * src(a, b) + SEC_T * t for b, t in enumerate(plane_sum(src, a, count))]


def source_reader(modes, mid, edge=None):
    def src(a, b):
        lanes = slice((b % 2) * CZ, (b % 2 + 1) * CZ)
        owner, pair = b // CY, b % CY // 2
        if a < HALO:
            ref, at = edge[0], pair * HALO + a
        elif a >= CX + HALO:
            ref, at = edge[1], pair * HALO + a - CX - HALO
        else:
            ref, at = mid, pair * CX + a - HALO
        return ref[owner, at * modes : (at + 1) * modes, lanes]

    return src


def own_source_kernel(modes, groups, capacity, both, _, own, inner, *scratch):
    jobs = []

    def one(o):
        at = 2 * o if isinstance(o, int) else 0
        mem = scratch[at : at + 2]
        jobs.extend(scatter(both, modes, capacity, o, 0, CX, own.at[o], *mem))

    each(groups, one)
    later_chunks(jobs)
    src = source_reader(modes, own)
    for a in range(HALO + 1, CX + HALO - 1):
        for b, sec in enumerate(second_plane(src, a, groups * CY)):
            inner[a - HALO - 1, b] = sec


def fluid_kernel(modes, groups, capacity, both, low, high, mid, inner, mdiag, stiff, *refs):
    outs = refs[:groups]
    edge, outer, press, force, scratch = (
        refs[groups : groups + 2],
        *refs[groups + 2 : groups + 5],
        refs[groups + 5 :],
    )
    local = both.shape[2]
    count = groups * CY
    width = min(local, capacity)
    jobs = []
    for side, there in enumerate((low, high)):
        a_first = CX - HALO if side == 0 else 0
        wide = 128 if side == 0 else 256
        half = len(scratch) // 2
        sets = scratch[side * half : (side + 1) * half]

        def one(o, there=there, a_first=a_first, wide=wide, sets=sets, side=side):
            at = 2 * o if isinstance(o, int) else 0
            mem = sets[at : at + 2]
            target = edge[side].at[o]
            jobs.extend(scatter(there, modes, capacity, o, a_first, HALO, target, *mem, wide))

        each(groups, one)
    later_chunks(jobs)
    src = source_reader(modes, mid, edge)
    for i, a in enumerate((1, 2, CX + HALO - 1, CX + HALO)):
        for b, sec in enumerate(second_plane(src, a, count)):
            outer[i, b] = sec

    def second(a, b):
        if a < HALO:
            return outer[a, b]
        if a >= CX:
            return outer[a - CX + HALO, b]
        return inner[a - HALO, b]

    for a in range(0, CX, 2):
        two = [plane_sum(second, a + 1, count), plane_sum(second, a + 2, count)]
        for b in range(count):
            p = jnp.concatenate(
                [
                    PRE_SRC * src(a + i + HALO, b) + PRE_SEC * second(a + i + 1, b) + PRE_T * two[i][b]
                    for i in range(2)
                ],
                axis=0,
            )
            hi, lo = split(p)
            owner, at = b // CY, (b % CY // 2 * CX + a) * modes
            lanes = (b % 2) * CZ
            press[owner, at : at + 2 * modes, lanes : lanes + CZ] = hi
            press[owner, at : at + 2 * modes, 2 * CZ + lanes : 3 * CZ + lanes] = lo

    def joined(owner, chunk, devices):
        loads = [Lists(both.at[k], modes, capacity).load(owner, chunk) for k in devices]
        return [jnp.concatenate(x, axis=1) for x in zip(*loads)]

    def pick(owner, chunk, devices):
        a, b, c, node, weight = joined(owner, chunk, devices)
        hot = onehot((b & 1) * CZ + c, 2 * CZ)
        got = dot(press[owner], jnp.concatenate([hot, hot], axis=0))
        pair = jnp.broadcast_to(lax.shift_right_logical(b, 1) * CX + a, (modes, a.shape[1]))
        picked = jnp.zeros(pair.shape, F32)
        for r in range(CX * CY // 2):
            picked = jnp.where(pair == r, got[r * modes : (r + 1) * modes], picked)
        return picked * weight, node

    def to_nodes(picked, node):
        hi, lo = split(picked)
        sums = dot_t(jnp.concatenate([hi, lo], axis=0), onehot(node, local))
        return sums[:modes] + sums[modes:]

    def collect(k, owner, chunk):
        return to_nodes(*pick(owner, chunk, [k]))

    if groups <= 4:
        every = [pick(o, 0, range(groups)) for o in range(groups)]
        for k in range(groups):
            lanes = slice(k * width, (k + 1) * width)
            parts = [[x[:, lanes] for x in one] for one in every]
            force[k] = to_nodes(*[jnp.concatenate(x, axis=1) for x in zip(*parts)])
    else:

        def per_device(k):
            force[k] = jnp.zeros((modes, local), F32)

            def per_owner(o):
                force[k] = force[k] + collect(k, o, 0)

            each(groups, per_owner)

        each(groups, per_device)
    chunks = Lists(both.at[0], modes, capacity).chunks
    if chunks > 1:
        later = [(k, o, c) for k in range(groups) for o in range(groups) for c in range(1, chunks)]
        tops = [
            jnp.max(Lists(both.at[k], modes, capacity).row(2, o, c)) for k, o, c in later
        ]
        for (k, o, c), top in zip(later, tops):

            @pl.when(top > 0.0)
            def _():
                force[k] = force[k] + collect(k, o, c)

    for k in range(groups):
        for w in range(3):
            outs[k][w * modes : (w + 1) * modes, :] = force[(1 - k - w) % groups]
        if k in (1, groups - 1):
            at = 3 * modes
            outs[k][at : at + 8, :] = jnp.broadcast_to(mdiag[...], (8, local))
            outs[k][at + 8 :, :] = stiff[...]


def apply_blocks(window, cols_ref, kb_ref, sub, groups, diag, field):
    rb, nb, bs, _ = kb_ref.shape
    pieces = []
    for q in range(rb):
        parts = []
        for n in range(nb):
            j = cols_ref[q, n]
            where = sub + j // rb - 1
            inside = jnp.where((where >= 0) & (where < groups), 1.0, 0.0)
            parts.append(window[j] * inside)
        pieces.append(
            lax.dot_general(
                jnp.concatenate(parts, axis=1),
                kb_ref[q].reshape(nb * bs, bs),
                (((1,), (0,)), ((), ())),
                precision=lax.Precision.HIGHEST,
                preferred_element_type=F32,
            )
        )
    return diag * field + jnp.concatenate(pieces, axis=1)


def fill_window(win, blocks, bs):
    at = 0
    for blk in blocks:
        for i in range(blk.shape[1] // bs):
            win[at] = blk[:, i * bs : (i + 1) * bs]
            at += 1


def stiff_kernel(modes, groups, sub_ref, cols_ref, prev, own, nxt, diag, kb, out, win):
    bs = kb.shape[2]
    fill_window(win, [prev[0:modes, :], own[0:modes, :], nxt[0:modes, :]], bs)
    out[...] = apply_blocks(win, cols_ref, kb, sub_ref[0], groups, diag[...], own[0:modes, :])


def first_mode(modes, groups, count, sub):
    return pl.multiple_of(lax.shift_right_logical(sub * (modes // groups), log2(count)) * count, count)


def gram_kernel(modes, groups, count, sub_ref, cols_ref, prev, pack, nxt, mdiag, *refs):
    parts = refs[:groups]
    stiff, diag, kb, keep, send, mass, win, gram, force = refs[groups:]
    bs = kb.shape[2]
    for k in range(groups):
        source = lax.rem(sub_ref[0] + groups - k, groups)
        at = first_mode(modes, groups, count, source)
        for w in range(3):
            force[w, pl.ds(at, count), :] = parts[k][w * count : (w + 1) * count, :]
    at = 3 * count
    before, after = parts[1], parts[groups - 1]
    fields = [
        force[0] + before[at : at + 1, :] * prev[0:modes, :],
        force[1] + mdiag[...] * pack[0:modes, :],
        force[2] + after[at : at + 1, :] * nxt[0:modes, :],
    ]
    own = fields[1]
    mass[...] = own
    s = stiff[...]
    ends = [before[at + 8 :, :], s, after[at + 8 :, :]]
    both = [jnp.concatenate([x, y], axis=0) for x, y in zip(ends, fields)]
    fill_window(win, both, bs)
    image = apply_blocks(win, cols_ref, kb, sub_ref[0], groups, diag[...], both[1])
    v = pack[0:modes, :]
    left = jnp.concatenate([v, s, own], axis=0)
    right = jnp.concatenate([s, image, own], axis=0)

    def inner(x, y):
        return lax.dot_general(
            x,
            y,
            (((1,), (1,)), ((), ())),
            precision=lax.Precision.HIGHEST,
            preferred_element_type=F32,
        )

    whole = inner(left, right)
    half = 3 * modes // 2
    gram[0] = whole[:half]
    gram[1] = whole[half:]
    gram[1, 2 * modes - half : 3 * modes - half, 0:modes] = inner(v, v)
    core = sub_ref[1]
    keep[...] = gram[core]
    send[...] = gram[1 - core]


def final_kernel(modes, total, sub_ref, mine, other, stiff, mass, residual, g_stiff, g_plain, gram):
    m = modes
    core = sub_ref[1]
    half = 3 * m // 2
    gram[pl.ds(pl.multiple_of(core * half, half), half), :] = mine[...]
    gram[pl.ds(pl.multiple_of((1 - core) * half, half), half), :] = other[...]
    blocks = [
        [gram[i * m : (i + 1) * m, j * m : (j + 1) * m] for j in range(4)] for i in range(3)
    ]
    (vs, vks, vkm, vm), (ss, sks, skm, sm), (vv, mks, mkm, mm) = blocks
    rows = lax.broadcasted_iota(jnp.int32, (m, m), 0)
    lanes = lax.broadcasted_iota(jnp.int32, (m, m), 1)
    eye = rows == lanes

    def column(x):
        return jnp.sum(jnp.where(eye, x, 0.0), axis=1, keepdims=True)

    def line(x):
        return jnp.sum(jnp.where(eye, x, 0.0), axis=0, keepdims=True)

    tc = column(vs) / column(vm)
    tl = line(vs) / line(vm)
    residual[...] = stiff[...] - tc * mass[...]
    ms = sm.T
    scale = 1.0 / total
    vr = vs - vm * tl
    g_plain[0:m, 0:m] = vv * scale
    g_plain[0:m, m : 2 * m] = vr * scale
    g_plain[m : 2 * m, 0:m] = vr.T * scale
    g_plain[m : 2 * m, m : 2 * m] = (ss - sm * tl - tc * (ms - mm * tl)) * scale
    g_stiff[0:m, 0:m] = vs * scale
    g_stiff[0:m, m : 2 * m] = (vks - vkm * tl) * scale
    g_stiff[m : 2 * m, 0:m] = (ss - tc * ms) * scale
    g_stiff[m : 2 * m, m : 2 * m] = (sks - skm * tl - tc * (mks - mkm * tl)) * scale


def shifted(x, axis, k):
    n = lax.axis_size(axis)
    return lax.ppermute(x, axis, [(i, (i + k) % n) for i in range(n)])


def swapped(x, axis, k):
    n = lax.axis_size(axis)
    return lax.ppermute(x, axis, [(i, i ^ k) for i in range(n)])


def summed(x, axis, bit):
    n = lax.axis_size(axis)
    while (1 << bit) < n:
        if (4 << bit) <= n:
            one, two, three = [swapped(x, axis, k << bit) for k in (1, 2, 3)]
            x = (x + one) + (two + three)
            bit += 2
        else:
            x = x + swapped(x, axis, 1 << bit)
            bit += 1
    return x


def smem():
    return pl.BlockSpec(memory_space=pltpu.SMEM)


def vmem():
    return pl.BlockSpec(memory_space=pltpu.VMEM)


def call(kernel, name, out_shape, scalars, arrays, scratch, flops, mib=4):
    return pl.pallas_call(
        kernel,
        name=name,
        out_shape=out_shape,
        in_specs=[smem()] * len(scalars) + [vmem()] * len(arrays),
        out_specs=jax.tree.map(lambda _: vmem(), out_shape),
        scratch_shapes=scratch,
        compiler_params=pltpu.CompilerParams(vmem_limit_bytes=mib << 20),
        cost_estimate=pl.CostEstimate(flops=flops, transcendentals=0, bytes_accessed=1 << 20),
    )(*scalars, *arrays)


def body(
    block_vectors,
    stiffness,
    mass_diag,
    kblocks,
    block_cols,
    slot_node,
    slot_owner,
    slot_cell,
    slot_weight,
    live_slots,
):
    modes, local = block_vectors.shape
    groups = lax.axis_size("sub")
    slots = slot_node.shape[0]
    bs = kblocks.shape[2]
    total = local * lax.axis_size("passage") * groups
    sub = jnp.stack([lax.axis_index("sub"), lax.axis_index("passage") & 1]).astype(jnp.int32)
    deep, wide = slots // 128, 128
    capacity = 2 * slots // groups
    slotted = [x.reshape(deep, wide) for x in (slot_owner, slot_cell, slot_node, slot_weight)]
    mine = max(8, modes // groups)
    beyond = range(2, groups - 1)
    pack, mdiag, diag, cols, *distant = pl.pallas_call(
        functools.partial(pack_kernel, modes, groups, mine),
        name="pack",
        out_shape=(
            jax.ShapeDtypeStruct((modes + 3 * deep, local), F32),
            jax.ShapeDtypeStruct((1, local), F32),
            jax.ShapeDtypeStruct((1, local), F32),
            jax.ShapeDtypeStruct(block_cols.shape, jnp.int32),
            *[jax.ShapeDtypeStruct((mine + 3 * deep, local), F32) for _ in beyond],
        ),
        in_specs=[smem()] + [pl.BlockSpec(memory_space=pltpu.MemorySpace.HBM)] * 8,
        out_specs=(vmem(), vmem(), vmem(), vmem(), *[vmem() for _ in beyond]),
        scratch_shapes=[pltpu.VMEM((deep, wide), x.dtype) for x in slotted]
        + [pltpu.SemaphoreType.DMA((8,))],
        compiler_params=pltpu.CompilerParams(vmem_limit_bytes=4 << 20),
        cost_estimate=pl.CostEstimate(flops=1 << 28, transcendentals=0, bytes_accessed=1 << 20),
    )(
        live_slots,
        *[
            pltpu.with_memory_space_constraint(x, pltpu.MemorySpace.HBM)
            for x in (
                *slotted,
                block_vectors,
                mass_diag[None, :],
                stiffness[None, :],
                block_cols,
            )
        ]
    )
    packs = [pack] + [
        shifted(distant[k - 2] if k in beyond else pack, "sub", k) for k in range(1, groups)
    ]
    start = first_mode(modes, groups, mine, lax.axis_index("sub").astype(jnp.int32))
    both = jnp.stack(
        [
            x
            if k in beyond
            else jnp.concatenate([lax.dynamic_slice_in_dim(x, start, mine), x[modes:]], axis=0)
            for k, x in enumerate(packs)
        ]
    )
    low = shifted(both, "passage", 1)
    high = shifted(both, "passage", -1)
    window = [packs[1], packs[0], packs[groups - 1]]
    nwin = 3 * local // bs
    stiff = call(
        functools.partial(stiff_kernel, modes, groups),
        "stiff",
        jax.ShapeDtypeStruct((modes, local), F32),
        [sub, cols],
        [*window, diag, kblocks],
        [pltpu.VMEM((nwin, modes, bs), F32)],
        1 << 29,
    )
    width = min(local, capacity)
    sets = groups if groups <= 4 else 1

    def field(*shape):
        return jax.ShapeDtypeStruct(shape, F32)

    def operands(rows, chunk):
        deep = min(chunk, width) * groups
        return sets * [pltpu.VMEM((2 * rows, deep), BF), pltpu.VMEM((2 * CZ, deep), BF)]

    rows = CX * CY // 2 * mine
    edge_rows = HALO * CY // 2 * mine
    mib = 20 if groups <= 4 else 36
    source, inner = call(
        functools.partial(own_source_kernel, mine, groups, capacity),
        "own_source",
        (field(groups, rows, 2 * CZ), field(CX - 2, groups * CY, mine, CZ)),
        [],
        [both, stiff],
        operands(rows, width),
        1 << 32,
        mib,
    )
    force = call(
        functools.partial(fluid_kernel, mine, groups, capacity),
        "fluid",
        tuple(
            field(3 * mine + (8 + modes if k in (1, groups - 1) else 0), local)
            for k in range(groups)
        ),
        [],
        [both, low, high, source, inner, mdiag, stiff],
        [
            *[pltpu.VMEM((groups, edge_rows, 2 * CZ), F32)] * 2,
            pltpu.VMEM((4, groups * CY, mine, CZ), F32),
            pltpu.VMEM((groups, rows, 4 * CZ), BF),
            pltpu.VMEM((groups, mine, local), F32),
            *operands(edge_rows, 128),
            *operands(edge_rows, 256),
        ],
        1 << 32,
        mib,
    )
    parts = [force[0]] + [shifted(force[k], "sub", k) for k in range(1, groups)]
    keep, send, mass = call(
        functools.partial(gram_kernel, modes, groups, mine),
        "gram",
        (field(3 * modes // 2, 4 * modes), field(3 * modes // 2, 4 * modes), field(modes, local)),
        [sub, cols],
        [*window, mdiag, *parts, stiff, diag, kblocks],
        [
            pltpu.VMEM((nwin, 2 * modes, bs), F32),
            pltpu.VMEM((2, 3 * modes // 2, 4 * modes), F32),
            pltpu.VMEM((3, modes, local), F32),
        ],
        1 << 29,
    )
    mine = keep + swapped(send, "passage", 1)
    mine = summed(mine, "passage", 1)
    mine = summed(mine, "sub", 0)
    other = swapped(mine, "passage", 1)
    return call(
        functools.partial(final_kernel, modes, float(total)),
        "final",
        (field(modes, local), field(2 * modes, 2 * modes), field(2 * modes, 2 * modes)),
        [sub],
        [mine, other, stiff, mass],
        [pltpu.VMEM((3 * modes, 4 * modes), F32)],
        1 << 20,
    )


def solution(mesh):
    return jax.shard_map(
        body,
        mesh=mesh,
        in_specs=(
            P(None, ("passage", "sub")),
            P(("passage", "sub")),
            P(("passage", "sub")),
            P(("passage", "sub"), None, None, None),
            P(("passage", "sub"), None),
            P(("passage", "sub")),
            P(("passage", "sub"), None),
            P(("passage", "sub")),
            P(("passage", "sub")),
            P(("passage", "sub")),
        ),
        out_specs=(P(None, ("passage", "sub")), P(), P()),
        check_vma=False,
    )
```
